32 devices in a mesh: dp: 8 (over z, x), mp: 4 (over y, core).
Axes of the slice: x: 2, y: 2, z: 4, core: 2. Of those that a mesh axis runs over, the one named last changes fastest.
Arguments:
- latent: bfloat16 [65536, 512], P('dp'), may hold values from -6 to 6
- actions: bfloat16 [6, 65536], P(None, 'dp'), may hold values from -1 to 1
- task_ids: int32 [65536], P('dp'), may hold values from 0 to 79
- action_masks: int32 [80, 6], replicated, may hold values 0 or 1
- next_latent: bfloat16 [65536, 512], P('dp', 'mp'), may hold values from 0 to 0.25
- reward_bins: int32 [65536], P('dp'), may hold values from 0 to 99
- reward_frac: float32 [65536], P('dp'), may hold values from 0 to 1
- task_embed: bfloat16 [80, 96], replicated, may hold values from -6 to 6
- dyn_w1: bfloat16 [614, 1024], P(None, 'mp'), may hold values from -0.25 to 0.25
- dyn_b1: float32 [1024], P('mp'), may hold values from -3 to 3
- dyn_gain: float32 [1024], P('mp'), may hold values from 0.5 to 1.5
- dyn_shift: float32 [1024], P('mp'), may hold values from -2 to 2
- rew_w1: bfloat16 [614, 1024], P(None, 'mp'), may hold values from -0.25 to 0.25
- rew_b1: float32 [1024], P('mp'), may hold values from -3 to 3
- rew_gain: float32 [1024], P('mp'), may hold values from 0.5 to 1.5
- rew_shift: float32 [1024], P('mp'), may hold values from -2 to 2
- dyn_w2: bfloat16 [1024, 512], P('mp'), may hold values from -0.375 to 0.375
- dyn_b2: float32 [512], replicated, may hold values from -2 to 2
- rew_w2: bfloat16 [1024, 101], P('mp'), may hold values from -0.375 to 0.375
- rew_b2: float32 [101], replicated, may hold values from -2 to 2
Outputs:
- latents: bfloat16 [65536, 512], P('dp', 'mp')
- latent_grad: bfloat16 [65536, 512], P('dp', 'mp')
- losses: float32 [2], replicated
- grad_task_embed: float32 [80, 96], replicated
- grad_dyn_w1: float32 [614, 1024], P(None, 'mp')
- grad_dyn_b1: float32 [1024], P('mp')
- grad_dyn_gain: float32 [1024], P('mp')
- grad_dyn_shift: float32 [1024], P('mp')
- grad_rew_w1: float32 [614, 1024], P(None, 'mp')
- grad_rew_b1: float32 [1024], P('mp')
- grad_rew_gain: float32 [1024], P('mp')
- grad_rew_shift: float32 [1024], P('mp')
- grad_dyn_w2: float32 [1024, 512], P('mp')
- grad_dyn_b2: float32 [512], replicated
- grad_rew_w2: float32 [1024, 101], P('mp')
- grad_rew_b2: float32 [101], replicated
The draws below stay inside these ranges and needn't reach their ends.
Inputs may be any that keep to these rules, and one draw needn't show every extreme that they name: The upper bin reward_bins + 1 is a valid bin.
All inputs are finite; a program needn't handle non-finite values.
Results may differ from the reference program's by a relative error of at most 0.024.
Values may be sent and summed in bfloat16 or wider, within the bound.
A program may use at most 192 MiB of HBM per device.

```python
import jax
import jax.numpy as jnp
from jax import lax

D_LAT = 512
HID = 1024
ACT = 6
TDIM = 96
TASKS = 80
BINS = 101
GROUP = 8
IN_DIM = 614
ROWS = 65536
N_MP = 4


def touch_ends(result, key, least, largest):
    longest = result.shape.index(max(result.shape))
    spots = []
    for shift in (0, 1):
        where = [jax.random.randint(jax.random.fold_in(key, axis), (), 0, length) for axis, length in enumerate(result.shape)]
        where[longest] = (where[longest] + shift) % result.shape[longest]
        spots.append(tuple(where))
    return result.at[spots[0]].set(least).at[spots[1]].set(largest)


def steps_of(key, dims, pieces, least, top_value):
    level = 1.0
    for position, shards_of in pieces:
        steps = jax.random.uniform(jax.random.fold_in(jax.random.fold_in(key, 6), position), (shards_of,), jnp.float32, least / len(pieces), top_value / len(pieces))
        level = level * jnp.repeat(jnp.exp(steps), dims[position] // shards_of).reshape((-1,) + (1,) * (len(dims) - 1 - position))
    return level


def noise(rng, dims, spread, reach, pieces=(), held_as=jnp.bfloat16):
    array = spread * jax.random.normal(rng, dims, jnp.float32)
    if pieces:
        array = array * steps_of(rng, dims, pieces, -0.22, 0.18)
    return jnp.clip(array, -reach, reach).astype(held_as)


def setup_inputs(seed: int = 0) -> dict:
    key_of = jax.random.split(jax.random.key(seed), 21)
    return {
        "latent": noise(key_of[0], (ROWS, D_LAT), 1.0, 6.0, ((0, 8),)),
        "actions": jnp.clip(jax.random.uniform(key_of[1], (ACT, ROWS), jnp.float32, -1.0, 1.0) * steps_of(key_of[1], (ACT, ROWS), ((1, 8),), -0.4, 0.0), -1.0, 1.0).astype(jnp.bfloat16),
        "task_ids": touch_ends(jax.random.randint(key_of[2], (ROWS,), 0, TASKS), jax.random.fold_in(key_of[2], 1), 0, TASKS - 1).astype(jnp.int32),
        "action_masks": touch_ends((jax.random.randint(key_of[3], (TASKS, ACT), 0, 4) < 3).astype(jnp.int32), jax.random.fold_in(key_of[3], 1), 0, 1),
        "next_latent": jnp.clip(0.25 * jax.random.uniform(key_of[4], (ROWS, D_LAT), jnp.float32) ** steps_of(key_of[4], (ROWS, D_LAT), ((0, 8), (1, 4)), -0.2, 0.2), 0.0, 0.25).astype(jnp.bfloat16),
        "reward_bins": touch_ends(jax.random.randint(key_of[5], (ROWS,), 0, BINS - 1), jax.random.fold_in(key_of[5], 1), 0, (BINS - 1) - 1).astype(jnp.int32),
        "reward_frac": jnp.clip(1.0 * jax.random.uniform(key_of[6], (ROWS,), jnp.float32) ** steps_of(key_of[6], (ROWS,), ((0, 8),), -0.2, 0.2), 0.0, 1.0),
        "task_embed": noise(key_of[7], (TASKS, TDIM), 1.0, 6.0),
        "dyn_w1": noise(key_of[8], (IN_DIM, HID), IN_DIM ** -0.5, 0.25, ((1, 4),)),
        "dyn_b1": noise(key_of[9], (HID,), 0.5, 3.0, ((0, 4),), jnp.float32),
        "dyn_gain": jnp.clip(1.0 + 0.1 * jax.random.normal(key_of[10], (HID,), jnp.float32), 0.5, 1.5),
        "dyn_shift": noise(key_of[11], (HID,), 0.3, 2.0, ((0, 4),), jnp.float32),
        "rew_w1": noise(key_of[12], (IN_DIM, HID), IN_DIM ** -0.5, 0.25, ((1, 4),)),
        "rew_b1": noise(key_of[13], (HID,), 0.5, 3.0, ((0, 4),), jnp.float32),
        "rew_gain": jnp.clip(1.0 + 0.1 * jax.random.normal(key_of[14], (HID,), jnp.float32), 0.5, 1.5),
        "rew_shift": noise(key_of[15], (HID,), 0.3, 2.0, ((0, 4),), jnp.float32),
        "dyn_w2": noise(key_of[16], (HID, D_LAT), (HID // 4) ** -0.5, 0.375, ((0, 4),)),
        "dyn_b2": noise(key_of[17], (D_LAT,), 0.3, 2.0, (), jnp.float32),
        "rew_w2": noise(key_of[18], (HID, BINS), (HID // 4) ** -0.5, 0.375, ((0, 4),)),
        "rew_b2": noise(key_of[19], (BINS,), 0.3, 2.0, (), jnp.float32),
    }


@jax.custom_vjp
def low(v):
    return lax.optimization_barrier(v.astype(jnp.bfloat16)).astype(jnp.float32)

@jax.custom_vjp
def low_back(v):
    return v

def low_keep(v):
    return (low(v), None)

def low_pass(kept, grad):
    return (grad,)

def back_keep(v):
    return (v, None)

def back_low(kept, grad):
    return (low(grad),)
low.defvjp(low_keep, low_pass)
low_back.defvjp(back_keep, back_low)
CONS_COEF = 20.0
REW_COEF = 0.1

def matmul_high(left, right):
    return jnp.dot(left, right, precision=lax.Precision.HIGHEST)

def mish_act(values):
    return values * jnp.tanh(jax.nn.softplus(values))

def layer_norm(pre_act, gain_vec, shift_vec):
    average = lax.optimization_barrier(jnp.mean(pre_act, axis=-1, keepdims=True))
    centred = pre_act - average
    variance = lax.optimization_barrier(jnp.mean(centred * centred, axis=-1, keepdims=True))
    return centred * lax.rsqrt(variance + 1e-05) * gain_vec + shift_vec

def block_terms(params, latent_rows, action_rows, id_rows, target_rows, bin_rows, frac_rows, action_masks):
    embed_tab, w1_dyn, b1_dyn, gain_dyn, shift_dyn, w1_rew, b1_rew, gain_rew, shift_rew, w2_dyn, b2_dyn, w2_rew, b2_rew = params
    onehot = (id_rows[:, None] == jnp.arange(TASKS, dtype=jnp.int32)[None, :]).astype(jnp.float32)
    embedded = matmul_high(onehot, embed_tab)
    masked = action_rows * matmul_high(onehot, action_masks.astype(jnp.float32))
    shard_width = HID // N_MP
    parts_dyn = []
    parts_rew = []
    for shard in range(N_MP):
        inputs = jnp.concatenate([low_back(latent_rows), masked, embedded], axis=1)
        cols = slice(shard * shard_width, (shard + 1) * shard_width)
        parts_dyn.append(matmul_high(inputs, w1_dyn[:, cols]))
        parts_rew.append(matmul_high(inputs, w1_rew[:, cols]))
    pre_dyn = low_back(jnp.concatenate(parts_dyn, axis=1) + b1_dyn)
    pre_rew = low_back(jnp.concatenate(parts_rew, axis=1) + b1_rew)
    hidden_dyn = low(mish_act(layer_norm(pre_dyn, gain_dyn, shift_dyn)))
    hidden_rew = low(mish_act(layer_norm(pre_rew, gain_rew, shift_rew)))
    lat_sum = jnp.zeros((latent_rows.shape[0], D_LAT), jnp.float32)
    for shard in range(N_MP):
        cols = slice(shard * shard_width, (shard + 1) * shard_width)
        lat_sum = lat_sum + low(matmul_high(hidden_dyn[:, cols], w2_dyn[cols]))
    lat_pre = low_back(lat_sum + b2_dyn)
    logits = low_back(matmul_high(hidden_rew, w2_rew) + b2_rew)
    simplex = jax.nn.softmax(lat_pre.reshape(-1, D_LAT // GROUP, GROUP), axis=-1).reshape(-1, D_LAT)
    lat_error = simplex - target_rows
    cons = jnp.sum(lat_error * lat_error)
    log_probs = jax.nn.log_softmax(logits, axis=-1)
    bin_iota = jnp.arange(BINS, dtype=jnp.int32)[None, :]
    target = jnp.where(bin_iota == bin_rows[:, None], 1.0 - frac_rows[:, None], 0.0)
    target = target + jnp.where(bin_iota == bin_rows[:, None] + 1, frac_rows[:, None], 0.0)
    rew = -jnp.sum(target * log_probs)
    return (cons, rew, simplex)

def reference(latent, actions, task_ids, action_masks, next_latent, reward_bins, reward_frac, task_embed, dyn_w1, dyn_b1, dyn_gain, dyn_shift, rew_w1, rew_b1, rew_gain, rew_shift, dyn_w2, dyn_b2, rew_w2, rew_b2):
    params = tuple((item.astype(jnp.float32) for item in (task_embed, dyn_w1, dyn_b1, dyn_gain, dyn_shift, rew_w1, rew_b1, rew_gain, rew_shift, dyn_w2, dyn_b2, rew_w2, rew_b2)))
    row_count = latent.shape[0]
    block_rows = min(4096, row_count)
    num_blocks = row_count // block_rows
    latent_f = latent.astype(jnp.float32)
    blocks_rest = (actions.astype(jnp.float32).T.reshape(num_blocks, block_rows, ACT), task_ids.reshape(num_blocks, block_rows), next_latent.astype(jnp.float32).reshape(num_blocks, block_rows, D_LAT), reward_bins.reshape(num_blocks, block_rows), reward_frac.astype(jnp.float32).reshape(num_blocks, block_rows))

    def forward(params_in, latent_in):

        def one_block(running, block):
            cons, rew, simplex = block_terms(params_in, block[0], block[1], block[2], block[3], block[4], block[5], action_masks)
            return ((running[0] + cons, running[1] + rew), simplex)
        blocks = (latent_in.reshape(num_blocks, block_rows, D_LAT),) + blocks_rest
        sums, simplex = lax.scan(jax.checkpoint(one_block), (jnp.zeros((), jnp.float32), jnp.zeros((), jnp.float32)), blocks)
        objective = (CONS_COEF * sums[0] + REW_COEF * sums[1]) / row_count
        return (objective, (sums[0], sums[1], simplex))
    objective, vjp_fn, aux = jax.vjp(forward, params, latent_f, has_aux=True)
    grad_params, grad_latent = vjp_fn(jnp.ones((), jnp.float32))
    latents_out = aux[2].reshape(row_count, D_LAT).astype(jnp.bfloat16)
    latent_grad = (grad_latent * row_count).astype(jnp.bfloat16)
    losses = jnp.stack([aux[0], aux[1]]) / row_count
    return (latents_out, latent_grad, losses, grad_params[0], grad_params[1], grad_params[2], grad_params[3], grad_params[4], grad_params[5], grad_params[6], grad_params[7], grad_params[8], grad_params[9], grad_params[10], grad_params[11], grad_params[12])
```

```python
import functools

import jax
import jax.numpy as jnp
from jax import lax
from jax.experimental import pallas as pl
from jax.experimental.pallas import tpu as pltpu
from jax.sharding import PartitionSpec as P

GROUP = 8
CONS_COEF = 20.0
REW_COEF = 0.1
EPS = 1e-05
LANES = 128
TILE = 512
SUB = 64
MESH = pl.DeviceIdType.MESH
F32 = jnp.float32
BF16 = jnp.bfloat16


def dot(left, right, left_dim=1, right_dim=0):
    return lax.dot_general(
        left, right, (((left_dim,), (right_dim,)), ((), ())), preferred_element_type=F32
    )


def aligned(start, size):
    return pl.ds(pl.multiple_of(start, size), size)


def split_dot(left, right, left_dim, right_dim):
    high = left.astype(BF16)
    low = (left - high.astype(F32)).astype(BF16)
    return dot(high, right, left_dim, right_dim) + dot(low, right, left_dim, right_dim)


def main_kernel(
    sizes,
    latent_in,
    next_in,
    w1_in,
    w2t_in,
    rw2t_in,
    vecs_in,
    ids_ref,
    act_ref,
    masks_ref,
    bins_ref,
    frac_ref,
    embed_ref,
    b2_ref,
    rb2_ref,
    lat_out,
    grad_out,
    ga_ref,
    gb_ref,
    gs_ref,
    ge_ref,
    x_all,
    x_t,
    w1_raw,
    w1_c,
    w2_t,
    rw2_t,
    vecs,
    next_lat,
    dpl,
    dpl_send,
    lat_stage,
    lg_stage,
    d_rew,
    g1,
    g2t,
    rg2t,
    pre,
    dh,
    dm,
    hid,
    d_pre,
    zt,
    latt,
    dlog,
    inv_ref,
    col_acc,
    sum_acc,
    row_acc,
    b2_acc,
    load_sem,
    w_send,
    w_recv,
    n_send,
    n_recv,
    d_send,
    d_recv,
    l_local,
    l_send,
    l_recv,
    g_local,
    g_send,
    g_recv,
):
    n_mp, total_rows, hid_width = sizes
    mine = lax.axis_index("mp")
    pair = mine // 2
    half = mine % 2
    own_rows = x_all.shape[0] // 2
    lat_width = latent_in.shape[1]
    shard = w1_in.shape[2]
    share = next_in.shape[1]
    n_task = embed_ref.shape[0]
    chip_cols = 2 * share
    n_tiles = own_rows // TILE
    n_lane = hid_width // LANES

    def peer_of(flip):
        near = mine + 1 - 2 * half
        if flip == 1:
            return near
        across = 2 * (1 - pair)
        return across + half if flip == 2 else across + 1 - half

    def rows_of(device):
        return aligned(device * own_rows, own_rows)

    barrier = pltpu.get_barrier_semaphore()
    for flip in (1, 2, 3):
        pl.semaphore_signal(
            barrier, inc=1, device_id={"mp": peer_of(flip)}, device_id_type=MESH
        )
    pl.semaphore_wait(barrier, 3)

    near, across = peer_of(1), peer_of(2)

    w_pairs = []
    for net in range(2):
        cols = aligned(net * hid_width + mine * shard, shard)
        w_pairs.append((w1_in.at[net], w1_raw.at[:, cols], net))
        w_pairs.append((vecs_in.at[net], vecs.at[:, cols], net))
    block = aligned(mine * shard, shard)
    w_pairs.append((w2t_in, w2_t.at[:, block], 0))
    w_pairs.append((rw2t_in, rw2_t.at[:, block], 1))
    order = [0, 1, 4, 2, 3, 5]

    def weight_copy(index, flip):
        source, target, _ = w_pairs[index]
        return pltpu.make_async_remote_copy(
            src_ref=source,
            dst_ref=target,
            send_sem=w_send.at[flip - 1, index],
            recv_sem=w_recv.at[flip - 1, index],
            device_id={"mp": peer_of(flip)},
            device_id_type=MESH,
        )

    def next_copy(slot):
        rows = near if slot == 1 else peer_of(3)
        return pltpu.make_async_remote_copy(
            src_ref=next_in.at[rows_of(rows), :],
            dst_ref=next_lat.at[slot, half],
            send_sem=n_send.at[slot],
            recv_sem=n_recv.at[slot],
            device_id={"mp": near},
            device_id_type=MESH,
        )

    loads = []
    for slot, device in ((0, across), (1, mine)):
        loads.append(
            (
                latent_in.at[rows_of(device), :],
                x_all.at[pl.ds(slot * own_rows, own_rows), pl.ds(0, lat_width)],
            )
        )
    for slot, device in ((0, across), (1, mine)):
        loads.append((next_in.at[rows_of(device), :], next_lat.at[slot, half]))
    for source, target, _ in w_pairs:
        loads.append((source, target))
    loads = [
        pltpu.make_async_copy(source, target, load_sem.at[i])
        for i, (source, target) in enumerate(loads)
    ]
    for copy in loads:
        copy.start()
    for index in order:
        for flip in (2, 3, 1):
            weight_copy(index, flip).start()
    next_copy(0).start()
    next_copy(1).start()

    for ref in (g1, g2t, rg2t, col_acc, sum_acc, row_acc, b2_acc):
        ref[...] = jnp.zeros_like(ref)

    for slot, device in ((0, across), (1, mine)):
        base = device * own_rows

        @pl.loop(0, n_tiles)
        def _(tile):
            lanes = aligned(base + tile * TILE, TILE)
            ids = ids_ref[:, lanes]
            tasks = lax.broadcasted_iota(jnp.int32, (n_task, TILE), 0)
            onehot = jnp.where(tasks == ids, 1.0, 0.0).astype(BF16)
            masks = dot(masks_ref[...], onehot)
            masked = (act_ref[:, lanes].astype(F32) * masks).astype(BF16)
            rest = LANES - n_task - masked.shape[0]
            extra = jnp.concatenate([onehot, masked, jnp.zeros((rest, TILE), BF16)], axis=0)
            rows = aligned(slot * own_rows + tile * TILE, TILE)
            x_all[rows, pl.ds(lat_width, LANES)] = extra.T
            if slot == 1:
                x_t[pl.ds(lat_width, LANES), aligned(tile * TILE, TILE)] = extra

    for copy in loads[:2]:
        copy.wait()

    @pl.loop(0, n_tiles)
    def _(tile):
        rows = aligned(own_rows + tile * TILE, TILE)
        x_t[pl.ds(0, lat_width), aligned(tile * TILE, TILE)] = x_all[
            rows, pl.ds(0, lat_width)
        ].T

    def centre(values):
        return values - jnp.sum(values, axis=1, keepdims=True) * (1.0 / hid_width)

    def prepare(net):
        for index in range(len(w_pairs)):
            if w_pairs[index][2] == net:
                loads[4 + index].wait()
                for flip in (1, 2, 3):
                    weight_copy(index, flip).wait_recv()
        cols = pl.ds(net * hid_width, hid_width)

        @pl.loop(0, lat_width // SUB)
        def _(step):
            rows = aligned(step * SUB, SUB)
            w1_c[rows, cols] = centre(w1_raw[rows, cols].astype(F32)).astype(BF16)

        n_embed = embed_ref.shape[1]
        table = dot(embed_ref[...], w1_raw[pl.ds(lat_width, n_embed), cols])
        w1_c[pl.ds(lat_width, n_task), cols] = centre(table).astype(BF16)
        act = centre(w1_raw[pl.ds(lat_width + n_embed, 16), cols].astype(F32))
        bias = centre(vecs[pl.ds(0, 1), cols])
        high = bias.astype(BF16).astype(F32)
        row = lax.broadcasted_iota(jnp.int32, act.shape, 0)
        act = jnp.where(row == 6, high, jnp.where(row == 7, bias - high, act))
        w1_c[pl.ds(lat_width + n_task, 16), cols] = act.astype(BF16)
        rest = LANES - n_task - 16
        w1_c[pl.ds(lat_width + n_task + 16, rest), cols] = jnp.zeros((rest, hid_width), BF16)

    def forward(net, rows, keep):
        cols = pl.ds(net * hid_width, hid_width)
        pre[...] = dot(x_all[rows, :], w1_c[:, cols])

        @pl.loop(0, TILE // SUB)
        def _(step):
            part = aligned(step * SUB, SUB)
            values = pre[part, :]
            square = jnp.sum(values * values, axis=1, keepdims=True)
            inv_ref[part, :] = jnp.broadcast_to(
                lax.rsqrt(square * (1.0 / hid_width) + EPS), (SUB, LANES)
            )

        @pl.loop(0, TILE // SUB)
        def _(step):
            part = aligned(step * SUB, SUB)
            inv = inv_ref[part, :]
            for lane in range(n_lane):
                lanes = pl.ds(lane * LANES, LANES)
                wide = pl.ds(net * hid_width + lane * LANES, LANES)
                xhat = pre[part, lanes] * inv
                y = xhat * vecs[pl.ds(1, 1), wide] + vecs[pl.ds(2, 1), wide]
                e = jnp.exp(jnp.minimum(y, 20.0))
                e2 = e + 2.0
                r = 1.0 / (e * e2 + 2.0)
                u = e * r
                t = u * e2
                hid[part, lanes] = (y * t).astype(BF16)
                if keep:
                    pre[part, lanes] = xhat
                    dm[part, lanes] = t + (4.0 * y) * (u * (r + u))

    def backward(net, target, first_row):
        @pl.loop(0, TILE // SUB)
        def _(step):
            part = aligned(step * SUB, SUB)
            first = jnp.zeros((SUB, LANES), F32)
            second = jnp.zeros((SUB, LANES), F32)
            for lane in range(n_lane):
                lanes = pl.ds(lane * LANES, LANES)
                wide = pl.ds(net * hid_width + lane * LANES, LANES)
                d_y = dh[part, lanes] * dm[part, lanes]
                xhat = pre[part, lanes]
                scaled = d_y * xhat
                col_acc[pl.ds(0, 8), wide] += jnp.sum(
                    scaled.reshape(SUB // 8, 8, LANES), axis=0
                )
                col_acc[pl.ds(8, 8), wide] += jnp.sum(d_y.reshape(SUB // 8, 8, LANES), axis=0)
                gain = vecs[pl.ds(1, 1), wide]
                g = d_y * gain
                first += g
                second += scaled * gain
                dh[part, lanes] = g
            inv = inv_ref[part, :]
            first = jnp.broadcast_to(
                jnp.sum(first, axis=1, keepdims=True) * (1.0 / hid_width), (SUB, LANES)
            )
            second = jnp.broadcast_to(
                jnp.sum(second, axis=1, keepdims=True) * (1.0 / hid_width), (SUB, LANES)
            )
            first = first * inv
            second = second * inv
            for lane in range(n_lane):
                lanes = pl.ds(lane * LANES, LANES)
                value = dh[part, lanes] * inv - first - pre[part, lanes] * second
                target[aligned(first_row + step * SUB, SUB), lanes] = value.astype(BF16)

    d_scale = 2.0 * CONS_COEF / total_rows

    def simnorm(slot, tile, target, row, col):
        rows = aligned(tile * TILE, TILE)
        zt[...] = dot(w2_t[aligned(pair * chip_cols, chip_cols), :], hid[...], 1, 1)
        for side in range(2):
            latt[pl.ds(side * share, share), :] = next_lat[slot, side, rows, :].T.astype(F32)

        @pl.loop(0, chip_cols // SUB)
        def _(step):
            part = aligned(step * SUB, SUB)
            bias = b2_ref[aligned(pair * chip_cols + step * SUB, SUB), :]
            for lane in range(TILE // LANES):
                lanes = pl.ds(lane * LANES, LANES)
                z = (zt[part, lanes] + bias).reshape(SUB // GROUP, GROUP, LANES)
                e = jnp.exp(z - jnp.max(z, axis=1, keepdims=True))
                s = e * (1.0 / jnp.sum(e, axis=1, keepdims=True))
                error = s - latt[part, lanes].reshape(z.shape)
                sum_acc[pl.ds(0, 8), :] += jnp.sum(error * error, axis=0)
                d_lat = d_scale * error
                d_z = s * (d_lat - jnp.sum(s * d_lat, axis=1, keepdims=True))
                zt[part, lanes] = s.reshape(SUB, LANES)
                target[
                    aligned(row + step * SUB, SUB), aligned(col + lane * LANES, LANES)
                ] = d_z.reshape(SUB, LANES).astype(BF16)

        for side in range(2):
            lat_stage[slot, side, rows, :] = zt[pl.ds(side * share, share), :].astype(BF16).T

    def lat_copies(slot, tile):
        device = across if slot == 0 else mine
        rows = aligned(tile * TILE, TILE)
        out_rows = lat_out.at[aligned(device * own_rows + tile * TILE, TILE), :]
        index = slot * n_tiles + tile
        local = pltpu.make_async_copy(
            lat_stage.at[slot, half, rows, :], out_rows, l_local.at[index]
        )
        remote = pltpu.make_async_remote_copy(
            src_ref=lat_stage.at[slot, 1 - half, rows, :],
            dst_ref=out_rows,
            send_sem=l_send.at[index],
            recv_sem=l_recv.at[index],
            device_id={"mp": near},
            device_id_type=MESH,
        )
        return local, remote

    def dpl_copy(tile):
        cols = aligned(tile * TILE, TILE)
        return pltpu.make_async_remote_copy(
            src_ref=dpl_send.at[:, cols],
            dst_ref=dpl.at[aligned(pair * chip_cols, chip_cols), cols],
            send_sem=d_send.at[tile],
            recv_sem=d_recv.at[tile],
            device_id={"mp": across},
            device_id_type=MESH,
        )

    def grad_copies(tile):
        rows = aligned(tile * TILE, TILE)
        out_rows = grad_out.at[aligned(mine * own_rows + tile * TILE, TILE), :]
        remotes = []
        for flip in (2, 3, 1):
            peer = peer_of(flip)
            remotes.append(
                pltpu.make_async_remote_copy(
                    src_ref=lg_stage.at[peer, rows, :],
                    dst_ref=out_rows,
                    send_sem=g_send.at[flip - 1, tile],
                    recv_sem=g_recv.at[flip - 1, tile],
                    device_id={"mp": peer},
                    device_id_type=MESH,
                )
            )
        local = pltpu.make_async_copy(lg_stage.at[mine, rows, :], out_rows, g_local.at[tile])
        return local, remotes

    prepare(0)
    loads[2].wait()
    next_copy(0).wait_recv()

    @pl.loop(0, n_tiles)
    def _(tile):
        forward(0, aligned(tile * TILE, TILE), False)
        simnorm(0, tile, dpl_send, 0, tile * TILE)
        dpl_copy(tile).start()
        local, remote = lat_copies(0, tile)
        local.start()
        remote.start()

    prepare(1)

    @pl.loop(0, n_tiles)
    def _(tile):
        cols = aligned(tile * TILE, TILE)
        forward(1, aligned(own_rows + tile * TILE, TILE), True)
        bins = bins_ref[:, aligned(mine * own_rows + tile * TILE, TILE)]
        frac = frac_ref[:, aligned(mine * own_rows + tile * TILE, TILE)]
        z = dot(rw2_t[...], hid[...], 1, 1)
        bias = rb2_ref[...]
        z = z + jnp.concatenate([bias] * (TILE // LANES), axis=1)
        z = z - jnp.max(z, axis=0, keepdims=True)
        e = jnp.exp(z)
        total = jnp.sum(e, axis=0, keepdims=True)
        row = lax.broadcasted_iota(jnp.int32, z.shape, 0)
        target = jnp.where(row == bins, 1.0 - frac, 0.0) + jnp.where(row == bins + 1, frac, 0.0)
        loss = jnp.sum(target * (jnp.log(total) - z), axis=0, keepdims=True)
        row_acc[...] += loss
        d_logits = (REW_COEF / total_rows) * (e * (1.0 / total) - target)
        dlog[...] = d_logits.astype(BF16)
        sum_acc[pl.ds(8, 8), :] += dot(jnp.ones((8, TILE), BF16), dlog[...], 1, 1)
        rg2t[...] += dot(dlog[...], hid[...])
        dh[...] = dot(dlog[...], rw2_t[...], 0, 0)
        backward(1, d_rew, tile * TILE)
        g1[:, pl.ds(hid_width, hid_width)] += dot(x_t[:, cols], d_rew[cols, :])

    loads[3].wait()
    next_copy(1).wait_recv()

    @pl.loop(0, n_tiles)
    def _(tile):
        cols = aligned(tile * TILE, TILE)
        forward(0, aligned(own_rows + tile * TILE, TILE), True)
        simnorm(1, tile, dpl, pair * chip_cols, tile * TILE)
        local, remote = lat_copies(1, tile)
        local.start()
        remote.start()
        dpl_copy(tile).wait_recv()
        d_lat = dpl[:, cols]
        b2_acc[...] += dot(jnp.ones((8, TILE), BF16), d_lat, 1, 1)
        g2t[...] += dot(d_lat, hid[...])
        dh[...] = dot(d_lat, w2_t[...], 0, 0)
        backward(0, d_pre, 0)
        g1[:, pl.ds(0, hid_width)] += dot(x_t[:, cols], d_pre[...])
        lat_rows = pl.ds(0, lat_width)
        lg = dot(d_pre[...], w1_raw[lat_rows, pl.ds(0, hid_width)], 1, 1)
        lg = lg + dot(d_rew[cols, :], w1_raw[lat_rows, pl.ds(hid_width, hid_width)], 1, 1)
        lg = (lg * total_rows).astype(BF16)
        for device in range(n_mp):
            lg_stage[device, cols, :] = lg[:, device * share : (device + 1) * share]
        local, remotes = grad_copies(tile)
        local.start()
        for remote in remotes:
            remote.start()

    for device in range(n_mp):
        for net in range(2):
            wide = pl.ds(net * hid_width + device * shard, shard)
            cols = pl.ds(net * shard, shard)
            ga_ref[device, :, cols] = g1[pl.ds(0, ga_ref.shape[1]), wide].astype(BF16)
        block_cols = pl.ds(device * shard, shard)
        gb_ref[device, pl.ds(0, lat_width), :] = g2t[:, block_cols].astype(BF16)
        gb_ref[device, pl.ds(lat_width, LANES), :] = rg2t[:, block_cols].astype(BF16)
    tasks = g1[pl.ds(lat_width, n_task), :]
    n_embed = embed_ref.shape[1]
    ge_ref[...] = split_dot(tasks, w1_raw[pl.ds(lat_width, n_embed), :], 1, 1)
    cons = jnp.sum(sum_acc[pl.ds(0, 8), :])
    rew = jnp.sum(row_acc[...])
    gs_ref[...] = jnp.zeros_like(gs_ref)
    for device in range(n_mp):
        for net in range(2):
            wide = pl.ds(net * hid_width + device * shard, shard)
            cols = pl.ds(net * shard, shard)
            for line in range(2):
                gs_ref[device, pl.ds(line, 1), cols] = jnp.sum(
                    col_acc[pl.ds(8 * line, 8), wide], axis=0, keepdims=True
                )
        gs_ref[device, pl.ds(2, 1), :] = b2_acc[pl.ds(0, 1), :]
        gs_ref[device, pl.ds(3, 1), pl.ds(0, LANES)] = sum_acc[pl.ds(8, 1), :]
        gs_ref[device, pl.ds(4, 1), :] = jnp.full((1, lat_width), cons)
        gs_ref[device, pl.ds(5, 1), :] = jnp.full((1, lat_width), rew)

    for index in range(len(w_pairs)):
        for flip in (1, 2, 3):
            weight_copy(index, flip).wait_send()
    for slot in range(2):
        next_copy(slot).wait_send()

        @pl.loop(0, n_tiles)
        def _(tile):
            local, remote = lat_copies(slot, tile)
            local.wait()
            remote.wait()

    @pl.loop(0, n_tiles)
    def _(tile):
        dpl_copy(tile).wait_send()
        local, remotes = grad_copies(tile)
        local.wait()
        for remote in remotes:
            remote.wait()


def run_main(n_mp, total_rows, args):
    latent, next_latent, w1, w2t = args[0], args[1], args[2], args[3]
    tok_rows, lat_width = latent.shape
    share = next_latent.shape[1]
    shard = w1.shape[2]
    hid_width = n_mp * shard
    own = tok_rows // n_mp
    in_rows = lat_width + LANES
    n_tiles = own // TILE
    embed = args[11]
    n_task, n_embed = embed.shape
    ga_rows = lat_width + n_task + 16
    any_spec = pl.BlockSpec(memory_space=pl.ANY)
    vmem_spec = pl.BlockSpec(memory_space=pltpu.VMEM)
    shape = jax.ShapeDtypeStruct
    dma = pltpu.SemaphoreType.DMA
    return pl.pallas_call(
        functools.partial(main_kernel, (n_mp, total_rows, hid_width)),
        out_shape=(
            shape((tok_rows, share), BF16),
            shape((tok_rows, share), BF16),
            shape((n_mp, ga_rows, 2 * shard), BF16),
            shape((n_mp, in_rows, shard), BF16),
            shape((n_mp, 8, lat_width), F32),
            shape((n_task, n_embed), F32),
        ),
        in_specs=[any_spec] * 6 + [vmem_spec] * 8,
        out_specs=[any_spec] * 2 + [vmem_spec] * 4,
        scratch_shapes=[
            pltpu.VMEM((2 * own, in_rows), BF16),
            pltpu.VMEM((in_rows, own), BF16),
            pltpu.VMEM((in_rows, 2 * hid_width), BF16),
            pltpu.VMEM((in_rows, 2 * hid_width), BF16),
            pltpu.VMEM((lat_width, hid_width), BF16),
            pltpu.VMEM((LANES, hid_width), BF16),
            pltpu.VMEM((8, 2 * hid_width), F32),
            pltpu.VMEM((2, 2, own, share), BF16),
            pltpu.VMEM((lat_width, own), BF16),
            pltpu.VMEM((2 * share, own), BF16),
            pltpu.VMEM((2, 2, own, share), BF16),
            pltpu.VMEM((n_mp, own, share), BF16),
            pltpu.VMEM((own, hid_width), BF16),
            pltpu.VMEM((in_rows, 2 * hid_width), F32),
            pltpu.VMEM((lat_width, hid_width), F32),
            pltpu.VMEM((LANES, hid_width), F32),
            pltpu.VMEM((TILE, hid_width), F32),
            pltpu.VMEM((TILE, hid_width), F32),
            pltpu.VMEM((TILE, hid_width), F32),
            pltpu.VMEM((TILE, hid_width), BF16),
            pltpu.VMEM((TILE, hid_width), BF16),
            pltpu.VMEM((2 * share, TILE), F32),
            pltpu.VMEM((2 * share, TILE), F32),
            pltpu.VMEM((LANES, TILE), BF16),
            pltpu.VMEM((TILE, LANES), F32),
            pltpu.VMEM((16, 2 * hid_width), F32),
            pltpu.VMEM((16, LANES), F32),
            pltpu.VMEM((1, TILE), F32),
            pltpu.VMEM((8, lat_width), F32),
            dma((10,)),
            dma((3, 6)),
            dma((3, 6)),
            dma((2,)),
            dma((2,)),
            dma((n_tiles,)),
            dma((n_tiles,)),
            dma((2 * n_tiles,)),
            dma((2 * n_tiles,)),
            dma((2 * n_tiles,)),
            dma((n_tiles,)),
            dma((3, n_tiles)),
            dma((3, n_tiles)),
        ],
        compiler_params=pltpu.CompilerParams(
            collective_id=0, has_side_effects=True, vmem_limit_bytes=60 << 20
        ),
    )(*args)


def on_device(
    latent,
    actions,
    task_ids,
    action_masks,
    next_latent,
    reward_bins,
    reward_frac,
    task_embed,
    dyn_w1,
    dyn_b1,
    dyn_gain,
    dyn_shift,
    rew_w1,
    rew_b1,
    rew_gain,
    rew_shift,
    dyn_w2,
    dyn_b2,
    rew_w2,
    rew_b2,
):
    n_mp = lax.axis_size("mp")
    tok_rows, lat_width = latent.shape
    total_rows = tok_rows * lax.axis_size("dp")
    n_act = actions.shape[0]
    n_task, n_embed = task_embed.shape
    n_bins = rew_w2.shape[1]
    shard = dyn_w1.shape[1]
    in_rows = lat_width + LANES

    def first_layer(w1):
        pad = jnp.zeros((in_rows - w1.shape[0], shard), BF16)
        return jnp.concatenate(
            [w1[:lat_width], w1[lat_width + n_act :], w1[lat_width : lat_width + n_act], pad]
        )

    w1 = jnp.stack([first_layer(dyn_w1), first_layer(rew_w1)])
    none = jnp.zeros_like(dyn_b1)
    vecs = jnp.stack(
        [
            jnp.stack([dyn_b1, dyn_gain, dyn_shift] + [none] * 5),
            jnp.stack([rew_b1, rew_gain, rew_shift] + [none] * 5),
        ]
    )
    rw2t = jnp.pad(rew_w2.T, ((0, LANES - n_bins), (0, 0)))
    act = jnp.concatenate(
        [actions, jnp.ones((2, tok_rows), BF16), jnp.zeros((14 - n_act, tok_rows), BF16)]
    )
    masks = jnp.concatenate(
        [
            action_masks.astype(BF16).T,
            jnp.ones((2, n_task), BF16),
            jnp.zeros((14 - n_act, n_task), BF16),
        ]
    )
    b2 = jnp.broadcast_to(dyn_b2[:, None], (lat_width, LANES))
    rb2 = jnp.pad(rew_b2, (0, LANES - n_bins), constant_values=-1e30)
    rb2 = jnp.broadcast_to(rb2[:, None], (LANES, LANES))
    args = (
        latent,
        next_latent,
        w1,
        dyn_w2.T,
        rw2t,
        vecs,
        task_ids[None, :],
        act,
        masks,
        reward_bins[None, :],
        reward_frac[None, :],
        task_embed,
        b2,
        rb2,
    )
    latents, latent_grad, ga, gb, gs, ge = run_main(n_mp, total_rows, args)
    ga = lax.psum_scatter(ga, "mp", scatter_dimension=0, tiled=True)
    gb = lax.psum_scatter(gb, "mp", scatter_dimension=0, tiled=True)
    gs = lax.psum_scatter(gs, "mp", scatter_dimension=0, tiled=True)
    ga, gb = lax.psum((ga, gb), "dp")
    gs = lax.psum(gs, "dp")
    ge = lax.psum(ge, ("dp", "mp"))
    ga, gb, gs = ga[0].astype(F32), gb[0].astype(F32), gs[0]
    grad_task = jnp.dot(
        task_embed.astype(F32).T,
        ga[lat_width : lat_width + n_task],
        precision=lax.Precision.HIGHEST,
    )
    first = lat_width + n_task
    grad_w1 = jnp.concatenate([ga[:lat_width], ga[first : first + n_act], grad_task])
    grad_b1 = ga[first + n_act]
    losses = jnp.stack([gs[4, 0], gs[5, 0]]) / total_rows
    return (
        latents,
        latent_grad,
        losses,
        ge,
        grad_w1[:, :shard],
        grad_b1[:shard],
        gs[0, :shard],
        gs[1, :shard],
        grad_w1[:, shard:],
        grad_b1[shard:],
        gs[0, shard:],
        gs[1, shard:],
        gb[:lat_width].T,
        gs[2],
        gb[lat_width : lat_width + n_bins].T,
        gs[3, :n_bins],
    )


def solution(mesh):
    return jax.shard_map(
        on_device,
        mesh=mesh,
        in_specs=(
            P("dp", None),
            P(None, "dp"),
            P("dp"),
            P(),
            P("dp", "mp"),
            P("dp"),
            P("dp"),
            P(),
            P(None, "mp"),
            P("mp"),
            P("mp"),
            P("mp"),
            P(None, "mp"),
            P("mp"),
            P("mp"),
            P("mp"),
            P("mp", None),
            P(),
            P("mp", None),
            P(),
        ),
        out_specs=(
            P("dp", "mp"),
            P("dp", "mp"),
            P(),
            P(),
            P(None, "mp"),
            P("mp"),
            P("mp"),
            P("mp"),
            P(None, "mp"),
            P("mp"),
            P("mp"),
            P("mp"),
            P("mp", None),
            P(),
            P("mp", None),
            P(),
        ),
        check_vma=False,
    )
```

```python
import functools

import jax
import jax.numpy as jnp
from jax import lax
from jax.experimental import pallas as pl
from jax.experimental.pallas import tpu as pltpu
from jax.sharding import PartitionSpec as P

GROUP = 8
CONS_COEF = 20.0
REW_COEF = 0.1
EPS = 1e-05
LANES = 128
TILE = 512
SUB = 64
MESH = pl.DeviceIdType.MESH
F32 = jnp.float32
BF16 = jnp.bfloat16


def dot(left, right, left_dim=1, right_dim=0):
    return lax.dot_general(
        left, right, (((left_dim,), (right_dim,)), ((), ())), preferred_element_type=F32
    )


def aligned(start, size):
    return pl.ds(pl.multiple_of(start, size), size)


def aligned_to(start, size):
    return pl.ds(pl.multiple_of(start, 16), size)


def split_dot(left, right, left_dim, right_dim):
    high = left.astype(BF16)
    low = (left - high.astype(F32)).astype(BF16)
    return dot(high, right, left_dim, right_dim) + dot(low, right, left_dim, right_dim)


def main_kernel(
    sizes,
    latent_in,
    next_in,
    w1_in,
    w2t_in,
    rw2t_in,
    vecs_in,
    ids_ref,
    act_ref,
    masks_ref,
    bins_ref,
    frac_ref,
    embed_ref,
    b2_ref,
    rb2_ref,
    lat_out,
    grad_out,
    fin_dyn,
    fin_rew,
    fin_sums,
    x_all,
    x_t,
    w1_raw,
    w1_c,
    w2_t,
    rw2_t,
    vecs,
    next_lat,
    dpl,
    dpl_send,
    lat_stage,
    lg_stage,
    d_dyn,
    part_dyn,
    part_rew,
    got_dyn,
    got_rew,
    sums,
    got_sums,
    g1,
    g2t,
    rg2t,
    pre,
    dh,
    dm,
    hid,
    d_pre,
    zt,
    latt,
    dlog,
    inv_ref,
    col_acc,
    sum_acc,
    row_acc,
    b2_acc,
    load_sem,
    w_send,
    w_recv,
    n_send,
    n_recv,
    d_send,
    d_recv,
    l_local,
    l_send,
    l_recv,
    g_local,
    g_send,
    g_recv,
    r_send,
    r_recv,
    s_send,
    s_recv,
):
    n_mp, n_dp, total_rows, hid_width = sizes
    n_bits = n_dp.bit_length() - 1
    mine = lax.axis_index("mp")
    column = lax.axis_index("dp")
    pair = mine // 2
    half = mine % 2
    own_rows = x_all.shape[0] // 2
    lat_width = latent_in.shape[1]
    shard = w1_in.shape[2]
    share = next_in.shape[1]
    n_task = embed_ref.shape[0]
    chip_cols = 2 * share
    n_tiles = own_rows // TILE
    n_lane = hid_width // LANES

    def peer_of(flip):
        near = mine + 1 - 2 * half
        if flip == 1:
            return near
        across = 2 * (1 - pair)
        return across + half if flip == 2 else across + 1 - half

    def bit_of(bit):
        return (column // (1 << bit)) % 2

    def column_peer(bit):
        return column + (1 - 2 * bit_of(bit)) * (1 << bit)

    def rows_of(device):
        return aligned(device * own_rows, own_rows)

    barrier = pltpu.get_barrier_semaphore()
    for flip in (1, 2, 3):
        pl.semaphore_signal(
            barrier, inc=1, device_id={"mp": peer_of(flip)}, device_id_type=MESH
        )
    for bit in range(n_bits):
        pl.semaphore_signal(
            barrier, inc=1, device_id={"dp": column_peer(bit)}, device_id_type=MESH
        )
    pl.semaphore_wait(barrier, 3 + n_bits)

    near, across = peer_of(1), peer_of(2)

    def w_pairs(block):
        pairs = []
        for net in range(2):
            cols = aligned(net * hid_width + block * shard, shard)
            pairs.append((w1_in.at[net], w1_raw.at[:, cols]))
            pairs.append((vecs_in.at[net], vecs.at[:, cols]))
        cols = aligned(block * shard, shard)
        pairs.append((w2t_in, w2_t.at[:, cols]))
        pairs.append((rw2t_in, rw2_t.at[:, cols]))
        return pairs

    w_needs = ((0, 1, 4), (2, 3, 5))
    own_weights = w_pairs(mine)

    def weight_copy(index, kind):
        source, target = own_weights[index]
        if kind == 2:
            source = target = w_pairs(across)[index][1]
        return pltpu.make_async_remote_copy(
            src_ref=source,
            dst_ref=target,
            send_sem=w_send.at[kind, index],
            recv_sem=w_recv.at[kind, index],
            device_id={"mp": across if kind == 1 else near},
            device_id_type=MESH,
        )

    def next_copy(slot):
        rows = near if slot == 1 else peer_of(3)
        return pltpu.make_async_remote_copy(
            src_ref=next_in.at[rows_of(rows), :],
            dst_ref=next_lat.at[slot, half],
            send_sem=n_send.at[slot],
            recv_sem=n_recv.at[slot],
            device_id={"mp": near},
            device_id_type=MESH,
        )

    loads = []
    for slot, device in ((0, across), (1, mine)):
        loads.append(
            (
                latent_in.at[rows_of(device), :],
                x_all.at[pl.ds(slot * own_rows, own_rows), pl.ds(0, lat_width)],
            )
        )
    for slot, device in ((0, across), (1, mine)):
        loads.append((next_in.at[rows_of(device), :], next_lat.at[slot, half]))
    loads += own_weights
    loads = [
        pltpu.make_async_copy(source, target, load_sem.at[i])
        for i, (source, target) in enumerate(loads)
    ]
    for copy in loads:
        copy.start()
    for index in w_needs[0] + w_needs[1]:
        weight_copy(index, 1).start()
        weight_copy(index, 0).start()
    next_copy(0).start()
    next_copy(1).start()

    for ref in (g1, g2t, rg2t, col_acc, sum_acc, row_acc, b2_acc):
        ref[...] = jnp.zeros_like(ref)

    for slot, device in ((0, across), (1, mine)):
        base = device * own_rows

        @pl.loop(0, n_tiles)
        def _(tile):
            lanes = aligned(base + tile * TILE, TILE)
            ids = ids_ref[:, lanes]
            tasks = lax.broadcasted_iota(jnp.int32, (n_task, TILE), 0)
            onehot = jnp.where(tasks == ids, 1.0, 0.0).astype(BF16)
            masks = dot(masks_ref[...], onehot)
            masked = (act_ref[:, lanes].astype(F32) * masks).astype(BF16)
            rest = LANES - n_task - masked.shape[0]
            extra = jnp.concatenate([onehot, masked, jnp.zeros((rest, TILE), BF16)], axis=0)
            rows = aligned(slot * own_rows + tile * TILE, TILE)
            x_all[rows, pl.ds(lat_width, LANES)] = extra.T
            if slot == 1:
                x_t[pl.ds(lat_width, LANES), aligned(tile * TILE, TILE)] = extra

    for copy in loads[:2]:
        copy.wait()

    @pl.loop(0, n_tiles)
    def _(tile):
        rows = aligned(own_rows + tile * TILE, TILE)
        x_t[pl.ds(0, lat_width), aligned(tile * TILE, TILE)] = x_all[
            rows, pl.ds(0, lat_width)
        ].T

    def centre(values):
        return values - jnp.sum(values, axis=1, keepdims=True) * (1.0 / hid_width)

    def prepare(net):
        for index in w_needs[net]:
            weight_copy(index, 1).wait_recv()
            weight_copy(index, 2).start()
        for index in w_needs[net]:
            loads[4 + index].wait()
            weight_copy(index, 0).wait_recv()
            weight_copy(index, 2).wait_recv()
        cols = pl.ds(net * hid_width, hid_width)

        @pl.loop(0, lat_width // SUB)
        def _(step):
            rows = aligned(step * SUB, SUB)
            w1_c[rows, cols] = centre(w1_raw[rows, cols].astype(F32)).astype(BF16)

        n_embed = embed_ref.shape[1]
        table = dot(embed_ref[...], w1_raw[pl.ds(lat_width, n_embed), cols])
        w1_c[pl.ds(lat_width, n_task), cols] = centre(table).astype(BF16)
        act = centre(w1_raw[pl.ds(lat_width + n_embed, 16), cols].astype(F32))
        bias = centre(vecs[pl.ds(0, 1), cols])
        high = bias.astype(BF16).astype(F32)
        row = lax.broadcasted_iota(jnp.int32, act.shape, 0)
        act = jnp.where(row == 6, high, jnp.where(row == 7, bias - high, act))
        w1_c[pl.ds(lat_width + n_task, 16), cols] = act.astype(BF16)
        rest = LANES - n_task - 16
        w1_c[pl.ds(lat_width + n_task + 16, rest), cols] = jnp.zeros((rest, hid_width), BF16)

    def forward(net, rows, keep):
        cols = pl.ds(net * hid_width, hid_width)
        pre[...] = dot(x_all[rows, :], w1_c[:, cols])

        @pl.loop(0, TILE // SUB)
        def _(step):
            part = aligned(step * SUB, SUB)
            values = pre[part, :]
            square = jnp.sum(values * values, axis=1, keepdims=True)
            inv_ref[part, :] = jnp.broadcast_to(
                lax.rsqrt(square * (1.0 / hid_width) + EPS), (SUB, LANES)
            )

        @pl.loop(0, TILE // SUB)
        def _(step):
            part = aligned(step * SUB, SUB)
            inv = inv_ref[part, :]
            for lane in range(n_lane):
                lanes = pl.ds(lane * LANES, LANES)
                wide = pl.ds(net * hid_width + lane * LANES, LANES)
                xhat = pre[part, lanes] * inv
                y = xhat * vecs[pl.ds(1, 1), wide] + vecs[pl.ds(2, 1), wide]
                e = jnp.exp(jnp.minimum(y, 20.0))
                e2 = e + 2.0
                r = 1.0 / (e * e2 + 2.0)
                u = e * r
                t = u * e2
                hid[part, lanes] = (y * t).astype(BF16)
                if keep:
                    pre[part, lanes] = xhat
                    dm[part, lanes] = t + (4.0 * y) * (u * (r + u))

    def backward(net, target, first_row):
        @pl.loop(0, TILE // SUB)
        def _(step):
            part = aligned(step * SUB, SUB)
            first = jnp.zeros((SUB, LANES), F32)
            second = jnp.zeros((SUB, LANES), F32)
            for lane in range(n_lane):
                lanes = pl.ds(lane * LANES, LANES)
                wide = pl.ds(net * hid_width + lane * LANES, LANES)
                d_y = dh[part, lanes] * dm[part, lanes]
                xhat = pre[part, lanes]
                scaled = d_y * xhat
                col_acc[pl.ds(0, 8), wide] += jnp.sum(
                    scaled.reshape(SUB // 8, 8, LANES), axis=0
                )
                col_acc[pl.ds(8, 8), wide] += jnp.sum(d_y.reshape(SUB // 8, 8, LANES), axis=0)
                gain = vecs[pl.ds(1, 1), wide]
                g = d_y * gain
                first += g
                second += scaled * gain
                dh[part, lanes] = g
            inv = inv_ref[part, :]
            first = jnp.broadcast_to(
                jnp.sum(first, axis=1, keepdims=True) * (1.0 / hid_width), (SUB, LANES)
            )
            second = jnp.broadcast_to(
                jnp.sum(second, axis=1, keepdims=True) * (1.0 / hid_width), (SUB, LANES)
            )
            first = first * inv
            second = second * inv
            for lane in range(n_lane):
                lanes = pl.ds(lane * LANES, LANES)
                value = dh[part, lanes] * inv - first - pre[part, lanes] * second
                target[aligned(first_row + step * SUB, SUB), lanes] = value.astype(BF16)

    d_scale = 2.0 * CONS_COEF / total_rows

    def simnorm(slot, tile, target, row, col):
        rows = aligned(tile * TILE, TILE)
        zt[...] = dot(w2_t[aligned(pair * chip_cols, chip_cols), :], hid[...], 1, 1)
        for side in range(2):
            latt[pl.ds(side * share, share), :] = next_lat[slot, side, rows, :].T.astype(F32)

        @pl.loop(0, chip_cols // SUB)
        def _(step):
            part = aligned(step * SUB, SUB)
            bias = b2_ref[aligned(pair * chip_cols + step * SUB, SUB), :]
            for lane in range(TILE // LANES):
                lanes = pl.ds(lane * LANES, LANES)
                z = (zt[part, lanes] + bias).reshape(SUB // GROUP, GROUP, LANES)
                e = jnp.exp(z - jnp.max(z, axis=1, keepdims=True))
                s = e * (1.0 / jnp.sum(e, axis=1, keepdims=True))
                error = s - latt[part, lanes].reshape(z.shape)
                sum_acc[pl.ds(0, 8), :] += jnp.sum(error * error, axis=0)
                d_lat = d_scale * error
                d_z = s * (d_lat - jnp.sum(s * d_lat, axis=1, keepdims=True))
                zt[part, lanes] = s.reshape(SUB, LANES)
                target[
                    aligned(row + step * SUB, SUB), aligned(col + lane * LANES, LANES)
                ] = d_z.reshape(SUB, LANES).astype(BF16)

        for side in range(2):
            lat_stage[slot, side, rows, :] = zt[pl.ds(side * share, share), :].astype(BF16).T

    def lat_copies(slot, tile):
        device = across if slot == 0 else mine
        rows = aligned(tile * TILE, TILE)
        out_rows = lat_out.at[aligned(device * own_rows + tile * TILE, TILE), :]
        index = slot * n_tiles + tile
        local = pltpu.make_async_copy(
            lat_stage.at[slot, half, rows, :], out_rows, l_local.at[index]
        )
        remote = pltpu.make_async_remote_copy(
            src_ref=lat_stage.at[slot, 1 - half, rows, :],
            dst_ref=out_rows,
            send_sem=l_send.at[index],
            recv_sem=l_recv.at[index],
            device_id={"mp": near},
            device_id_type=MESH,
        )
        return local, remote

    def dpl_copy(tile):
        cols = aligned(tile * TILE, TILE)
        return pltpu.make_async_remote_copy(
            src_ref=dpl_send.at[:, cols],
            dst_ref=dpl.at[aligned(pair * chip_cols, chip_cols), cols],
            send_sem=d_send.at[tile],
            recv_sem=d_recv.at[tile],
            device_id={"mp": across},
            device_id_type=MESH,
        )

    def grad_copies(tile):
        rows = aligned(tile * TILE, TILE)
        out_rows = grad_out.at[aligned(mine * own_rows + tile * TILE, TILE), :]
        remotes = []
        for flip in (2, 3, 1):
            peer = peer_of(flip)
            remotes.append(
                pltpu.make_async_remote_copy(
                    src_ref=lg_stage.at[peer, rows, :],
                    dst_ref=out_rows,
                    send_sem=g_send.at[flip - 1, tile],
                    recv_sem=g_recv.at[flip - 1, tile],
                    device_id={"mp": peer},
                    device_id_type=MESH,
                )
            )
        local = pltpu.make_async_copy(lg_stage.at[mine, rows, :], out_rows, g_local.at[tile])
        return local, remotes

    prepare(0)
    loads[2].wait()
    next_copy(0).wait_recv()

    @pl.loop(0, n_tiles)
    def _(tile):
        forward(0, aligned(tile * TILE, TILE), False)
        simnorm(0, tile, dpl_send, 0, tile * TILE)
        dpl_copy(tile).start()
        local, remote = lat_copies(0, tile)
        local.start()
        remote.start()

    loads[3].wait()
    next_copy(1).wait_recv()

    @pl.loop(0, n_tiles)
    def _(tile):
        cols = aligned(tile * TILE, TILE)
        forward(0, aligned(own_rows + tile * TILE, TILE), True)
        simnorm(1, tile, dpl, pair * chip_cols, tile * TILE)
        local, remote = lat_copies(1, tile)
        local.start()
        remote.start()
        dpl_copy(tile).wait_recv()
        d_lat = dpl[:, cols]
        b2_acc[...] += dot(jnp.ones((8, TILE), BF16), d_lat, 1, 1)
        g2t[...] += dot(d_lat, hid[...])
        dh[...] = dot(d_lat, w2_t[...], 0, 0)
        backward(0, d_dyn, tile * TILE)
        g1[:, pl.ds(0, hid_width)] += dot(x_t[:, cols], d_dyn[cols, :])

    def add_into(target, other, n_rows):
        step_rows = 48 if n_rows % 48 == 0 else 16

        @pl.loop(0, n_rows // step_rows)
        def _(step):
            rows = aligned(step * step_rows, step_rows)
            total = target[rows, :].astype(F32) + other[rows, :].astype(F32)
            target[rows, :] = total.astype(BF16)

    def reduction(key, part, got, fin, with_sums):
        n_rows = part.shape[2]
        stages = [("near", 0, n_rows), ("across", 0, n_rows)]
        offset, length = 0, n_rows
        place = 3 * n_rows
        gathers = []
        for bit in range(n_bits):
            if length % 32 == 0:
                length //= 2
                keep = offset + bit_of(bit) * length
                stages.append(("half", bit, offset + (1 - bit_of(bit)) * length, keep, length, place))
                gathers.append(("gather", bit, keep, length))
                offset = keep
            else:
                stages.append(("whole", bit, offset, offset, length, place))
            place += length
        last = len(stages)
        stages += gathers[::-1]
        whole = part.at[half, pair]

        def ends(index):
            stage = stages[index]
            kind = stage[0]
            if kind == "near":
                return part.at[1 - half], got.at[:, pl.ds(0, n_rows), :], {"mp": near}
            if kind == "across":
                return part.at[half, 1 - pair], got.at[0, pl.ds(n_rows, n_rows), :], {"mp": across}
            device = {"dp": column_peer(stage[1])}
            if kind == "gather":
                rows = aligned_to(stage[2], stage[3])
                return fin.at[rows, :], fin.at[rows, :], device
            rows = aligned_to(stage[2], stage[4])
            base = 2 * n_rows + stage[5] - 3 * n_rows
            return whole.at[rows, :], got.at[0, pl.ds(base, stage[4]), :], device

        def copy(index):
            source, target, device = ends(index)
            return pltpu.make_async_remote_copy(
                src_ref=source,
                dst_ref=target,
                send_sem=r_send.at[key, index],
                recv_sem=r_recv.at[key, index],
                device_id=device,
                device_id_type=MESH,
            )

        def sums_copy(index):
            return pltpu.make_async_remote_copy(
                src_ref=sums.at[index],
                dst_ref=got_sums.at[index],
                send_sem=s_send.at[index],
                recv_sem=s_recv.at[index],
                device_id=ends(index)[2],
                device_id_type=MESH,
            )

        def start(index):
            copy(index).start()
            if with_sums and index < last:
                sums_copy(index).start()

        def finish(index):
            stage = stages[index]
            kind = stage[0]
            if kind == "whole":
                copy(index).wait_send()
            copy(index).wait_recv()
            if with_sums and index < last:
                sums_copy(index).wait_recv()
                sums[index + 1] = sums[index] + got_sums[index]
            if kind == "near":
                for other in range(2):
                    add_into(
                        part.at[half, other], got.at[other, pl.ds(0, n_rows), :], n_rows
                    )
            elif kind == "across":
                add_into(whole, got.at[0, pl.ds(n_rows, n_rows), :], n_rows)
            elif kind != "gather":
                base = 2 * n_rows + stage[5] - 3 * n_rows
                add_into(
                    whole.at[aligned_to(stage[3], stage[4]), :],
                    got.at[0, pl.ds(base, stage[4]), :],
                    stage[4],
                )
            if index + 1 == last:
                rows = aligned_to(offset, length)
                fin[rows, :] = whole[rows, :]
            if index + 1 < len(stages):
                start(index + 1)

        def drain():
            for index, stage in enumerate(stages):
                if stage[0] != "whole":
                    copy(index).wait_send()
                if with_sums and index < last:
                    sums_copy(index).wait_send()

        return start, finish, drain, len(stages)

    def fill(part, net, first, count, source, base):
        for device in range(n_mp):
            cols = pl.ds(net * hid_width + device * shard, shard)
            part[device % 2, device // 2, pl.ds(first, count), :] = source[
                pl.ds(base, count), cols
            ].astype(BF16)

    def add_columns(net):
        cols = pl.ds(net * hid_width, hid_width)
        for line in range(2):
            g1[pl.ds(lat_width + n_task + 8 + line, 1), cols] = jnp.sum(
                col_acc[pl.ds(8 * line, 8), cols], axis=0, keepdims=True
            )

    in_rows = g1.shape[0]
    add_columns(0)
    fill(part_dyn, 0, 0, in_rows, g1, 0)
    fill(part_dyn, 0, in_rows, lat_width, g2t, 0)
    start, finish, drain_dyn, n_stages = reduction(0, part_dyn, got_dyn, fin_dyn, False)
    start(0)
    points = [0, 1, 2]
    waiting = list(range(n_stages))

    prepare(1)

    def point(tile, number):
        for index in range(n_stages):
            if index % len(points) == number and index // len(points) < n_tiles:

                @pl.when(tile == index // len(points))
                def _():
                    finish(index)

    @pl.loop(0, n_tiles)
    def _(tile):
        cols = aligned(tile * TILE, TILE)
        forward(1, aligned(own_rows + tile * TILE, TILE), True)
        point(tile, 0)
        bins = bins_ref[:, aligned(mine * own_rows + tile * TILE, TILE)]
        frac = frac_ref[:, aligned(mine * own_rows + tile * TILE, TILE)]
        z = dot(rw2_t[...], hid[...], 1, 1)
        bias = rb2_ref[...]
        z = z + jnp.concatenate([bias] * (TILE // LANES), axis=1)
        z = z - jnp.max(z, axis=0, keepdims=True)
        e = jnp.exp(z)
        total = jnp.sum(e, axis=0, keepdims=True)
        row = lax.broadcasted_iota(jnp.int32, z.shape, 0)
        target = jnp.where(row == bins, 1.0 - frac, 0.0) + jnp.where(row == bins + 1, frac, 0.0)
        loss = jnp.sum(target * (jnp.log(total) - z), axis=0, keepdims=True)
        row_acc[...] += loss
        d_logits = (REW_COEF / total_rows) * (e * (1.0 / total) - target)
        dlog[...] = d_logits.astype(BF16)
        sum_acc[pl.ds(8, 8), :] += dot(jnp.ones((8, TILE), BF16), dlog[...], 1, 1)
        rg2t[...] += dot(dlog[...], hid[...])
        dh[...] = dot(dlog[...], rw2_t[...], 0, 0)
        backward(1, d_pre, 0)
        point(tile, 1)
        lat_rows = pl.ds(0, lat_width)
        lg = dot(d_dyn[cols, :], w1_raw[lat_rows, pl.ds(0, hid_width)], 1, 1)
        lg = lg + dot(d_pre[...], w1_raw[lat_rows, pl.ds(hid_width, hid_width)], 1, 1)
        lg = (lg * total_rows).astype(BF16)
        for device in range(n_mp):
            lg_stage[device, cols, :] = lg[:, device * share : (device + 1) * share]
        local, remotes = grad_copies(tile)
        local.start()
        for remote in remotes:
            remote.start()
        g1[:, pl.ds(hid_width, hid_width)] += dot(x_t[:, cols], d_pre[...])
        point(tile, 2)

    for index in range(n_tiles * len(points), n_stages):
        finish(index)

    add_columns(1)
    fill_rows = part_rew.shape[3]
    for device in range(n_mp):
        cols = pl.ds(hid_width + device * shard, shard)
        block = pl.ds(device * shard, shard)
        where = (device % 2, device // 2)
        part_rew[(0,) + where] = g1[pl.ds(0, fill_rows), cols].astype(BF16)
        part_rew[(1,) + where + (pl.ds(0, in_rows - fill_rows),)] = g1[
            pl.ds(fill_rows, in_rows - fill_rows), cols
        ].astype(BF16)
        part_rew[(1,) + where + (pl.ds(in_rows - fill_rows, LANES),)] = rg2t[:, block].astype(BF16)
    n_embed = embed_ref.shape[1]
    tasks = g1[pl.ds(lat_width, n_task), :]
    table = split_dot(tasks, w1_raw[pl.ds(lat_width, n_embed), :], 1, 1).astype(BF16)
    spare = in_rows - fill_rows - 32
    for device in range(n_mp):
        where = (1, device % 2, device // 2)
        part_rew[where + (pl.ds(spare, 32), pl.ds(0, n_embed))] = table[0:32]
        part_rew[where + (pl.ds(spare, 32), pl.ds(LANES, n_embed))] = table[32:64]
        part_rew[where + (pl.ds(fill_rows - 16, 16), pl.ds(0, n_embed))] = table[64:80]
    sums[0] = jnp.zeros(sums.shape[1:], F32)
    sums[0, pl.ds(0, 1), :] = b2_acc[pl.ds(0, 1), :]
    sums[0, pl.ds(1, 1), pl.ds(0, LANES)] = sum_acc[pl.ds(8, 1), :]
    cons = jnp.sum(sum_acc[pl.ds(0, 8), :])
    rew = jnp.sum(row_acc[...])
    sums[0, pl.ds(2, 1), :] = jnp.full((1, lat_width), cons)
    sums[0, pl.ds(3, 1), :] = jnp.full((1, lat_width), rew)
    parts = [
        reduction(
            1 + k, part_rew.at[k], got_rew.at[k], fin_rew.at[pl.ds(k * fill_rows, fill_rows), :], k == 0
        )
        for k in range(2)
    ]
    for part in parts:
        part[0](0)
    for index in range(parts[0][3]):
        for part in parts:
            part[1](index)
    fin_sums[...] = sums[2 + n_bits]
    drain_dyn()
    for part in parts:
        part[2]()

    for index in range(6):
        for kind in range(3):
            weight_copy(index, kind).wait_send()
    for slot in range(2):
        next_copy(slot).wait_send()

        @pl.loop(0, n_tiles)
        def _(tile):
            local, remote = lat_copies(slot, tile)
            local.wait()
            remote.wait()

    @pl.loop(0, n_tiles)
    def _(tile):
        dpl_copy(tile).wait_send()
        local, remotes = grad_copies(tile)
        local.wait()
        for remote in remotes:
            remote.wait()


def run_main(n_mp, n_dp, total_rows, args):
    latent, next_latent, w1, w2t = args[0], args[1], args[2], args[3]
    tok_rows, lat_width = latent.shape
    share = next_latent.shape[1]
    shard = w1.shape[2]
    hid_width = n_mp * shard
    own = tok_rows // n_mp
    in_rows = lat_width + LANES
    n_tiles = own // TILE
    embed = args[11]
    n_task, n_embed = embed.shape
    n_bits = n_dp.bit_length() - 1
    dyn_rows = in_rows + lat_width
    rew_rows = (in_rows + LANES) // 2

    def room(rows):
        extra, length = 0, rows
        for _ in range(n_bits):
            length = length // 2 if length % 32 == 0 else length
            extra += length
        return 2 * rows + extra

    any_spec = pl.BlockSpec(memory_space=pl.ANY)
    vmem_spec = pl.BlockSpec(memory_space=pltpu.VMEM)
    shape = jax.ShapeDtypeStruct
    dma = pltpu.SemaphoreType.DMA
    return pl.pallas_call(
        functools.partial(main_kernel, (n_mp, n_dp, total_rows, hid_width)),
        out_shape=(
            shape((tok_rows, share), BF16),
            shape((tok_rows, share), BF16),
            shape((dyn_rows, shard), BF16),
            shape((2 * rew_rows, shard), BF16),
            shape((8, lat_width), F32),
        ),
        in_specs=[any_spec] * 6 + [vmem_spec] * 8,
        out_specs=[any_spec] * 2 + [vmem_spec] * 3,
        scratch_shapes=[
            pltpu.VMEM((2 * own, in_rows), BF16),
            pltpu.VMEM((in_rows, own), BF16),
            pltpu.VMEM((in_rows, 2 * hid_width), BF16),
            pltpu.VMEM((in_rows, 2 * hid_width), BF16),
            pltpu.VMEM((lat_width, hid_width), BF16),
            pltpu.VMEM((LANES, hid_width), BF16),
            pltpu.VMEM((8, 2 * hid_width), F32),
            pltpu.VMEM((2, 2, own, share), BF16),
            pltpu.VMEM((lat_width, own), BF16),
            pltpu.VMEM((2 * share, own), BF16),
            pltpu.VMEM((2, 2, own, share), BF16),
            pltpu.VMEM((n_mp, own, share), BF16),
            pltpu.VMEM((own, hid_width), BF16),
            pltpu.VMEM((2, 2, dyn_rows, shard), BF16),
            pltpu.VMEM((2, 2, 2, rew_rows, shard), BF16),
            pltpu.VMEM((2, room(dyn_rows), shard), BF16),
            pltpu.VMEM((2, 2, room(rew_rows), shard), BF16),
            pltpu.VMEM((3 + n_bits, 8, lat_width), F32),
            pltpu.VMEM((2 + n_bits, 8, lat_width), F32),
            pltpu.VMEM((in_rows, 2 * hid_width), F32),
            pltpu.VMEM((lat_width, hid_width), F32),
            pltpu.VMEM((LANES, hid_width), F32),
            pltpu.VMEM((TILE, hid_width), F32),
            pltpu.VMEM((TILE, hid_width), F32),
            pltpu.VMEM((TILE, hid_width), F32),
            pltpu.VMEM((TILE, hid_width), BF16),
            pltpu.VMEM((TILE, hid_width), BF16),
            pltpu.VMEM((2 * share, TILE), F32),
            pltpu.VMEM((2 * share, TILE), F32),
            pltpu.VMEM((LANES, TILE), BF16),
            pltpu.VMEM((TILE, LANES), F32),
            pltpu.VMEM((16, 2 * hid_width), F32),
            pltpu.VMEM((16, LANES), F32),
            pltpu.VMEM((1, TILE), F32),
            pltpu.VMEM((8, lat_width), F32),
            dma((10,)),
            dma((3, 6)),
            dma((3, 6)),
            dma((2,)),
            dma((2,)),
            dma((n_tiles,)),
            dma((n_tiles,)),
            dma((2 * n_tiles,)),
            dma((2 * n_tiles,)),
            dma((2 * n_tiles,)),
            dma((n_tiles,)),
            dma((3, n_tiles)),
            dma((3, n_tiles)),
            dma((3, 2 + 2 * n_bits)),
            dma((3, 2 + 2 * n_bits)),
            dma((2 + n_bits,)),
            dma((2 + n_bits,)),
        ],
        compiler_params=pltpu.CompilerParams(
            collective_id=0, has_side_effects=True, vmem_limit_bytes=60 << 20
        ),
    )(*args)


def on_device(
    latent,
    actions,
    task_ids,
    action_masks,
    next_latent,
    reward_bins,
    reward_frac,
    task_embed,
    dyn_w1,
    dyn_b1,
    dyn_gain,
    dyn_shift,
    rew_w1,
    rew_b1,
    rew_gain,
    rew_shift,
    dyn_w2,
    dyn_b2,
    rew_w2,
    rew_b2,
):
    n_mp = lax.axis_size("mp")
    tok_rows, lat_width = latent.shape
    total_rows = tok_rows * lax.axis_size("dp")
    n_act = actions.shape[0]
    n_task, n_embed = task_embed.shape
    n_bins = rew_w2.shape[1]
    shard = dyn_w1.shape[1]
    in_rows = lat_width + LANES

    def first_layer(w1):
        pad = jnp.zeros((in_rows - w1.shape[0], shard), BF16)
        return jnp.concatenate(
            [w1[:lat_width], w1[lat_width + n_act :], w1[lat_width : lat_width + n_act], pad]
        )

    w1 = jnp.stack([first_layer(dyn_w1), first_layer(rew_w1)])
    none = jnp.zeros_like(dyn_b1)
    vecs = jnp.stack(
        [
            jnp.stack([dyn_b1, dyn_gain, dyn_shift] + [none] * 5),
            jnp.stack([rew_b1, rew_gain, rew_shift] + [none] * 5),
        ]
    )
    rw2t = jnp.pad(rew_w2.T, ((0, LANES - n_bins), (0, 0)))
    act = jnp.concatenate(
        [actions, jnp.ones((2, tok_rows), BF16), jnp.zeros((14 - n_act, tok_rows), BF16)]
    )
    masks = jnp.concatenate(
        [
            action_masks.astype(BF16).T,
            jnp.ones((2, n_task), BF16),
            jnp.zeros((14 - n_act, n_task), BF16),
        ]
    )
    b2 = jnp.broadcast_to(dyn_b2[:, None], (lat_width, LANES))
    rb2 = jnp.pad(rew_b2, (0, LANES - n_bins), constant_values=-1e30)
    rb2 = jnp.broadcast_to(rb2[:, None], (LANES, LANES))
    args = (
        latent,
        next_latent,
        w1,
        dyn_w2.T,
        rw2t,
        vecs,
        task_ids[None, :],
        act,
        masks,
        reward_bins[None, :],
        reward_frac[None, :],
        task_embed,
        b2,
        rb2,
    )
    n_dp = lax.axis_size("dp")
    latents, latent_grad, dyn, rew, sums = run_main(n_mp, n_dp, total_rows, args)
    dyn = dyn.astype(F32)
    rew = rew.astype(F32)
    first = lat_width + n_task
    tasks = jnp.concatenate([dyn[lat_width:first], rew[lat_width:first]], axis=1)
    grad_task = jnp.dot(task_embed.astype(F32).T, tasks, precision=lax.Precision.HIGHEST)

    def first_grads(net, task):
        return (
            jnp.concatenate([net[:lat_width], net[first : first + n_act], task]),
            net[first + n_act],
            net[first + 8],
            net[first + 9],
        )

    spare = in_rows - 32
    grad_embed = jnp.concatenate(
        [
            rew[spare : spare + 32, :n_embed],
            rew[spare : spare + 32, LANES : LANES + n_embed],
            rew[in_rows + LANES - 16 :, :n_embed],
        ]
    )
    losses = jnp.stack([sums[2, 0], sums[3, 0]]) / total_rows
    return (
        latents,
        latent_grad,
        losses,
        grad_embed,
        *first_grads(dyn, grad_task[:, :shard]),
        *first_grads(rew, grad_task[:, shard:]),
        dyn[in_rows:].T,
        sums[0],
        rew[in_rows : in_rows + n_bins].T,
        sums[1, :n_bins],
    )


def solution(mesh):
    return jax.shard_map(
        on_device,
        mesh=mesh,
        in_specs=(
            P("dp", None),
            P(None, "dp"),
            P("dp"),
            P(),
            P("dp", "mp"),
            P("dp"),
            P("dp"),
            P(),
            P(None, "mp"),
            P("mp"),
            P("mp"),
            P("mp"),
            P(None, "mp"),
            P("mp"),
            P("mp"),
            P("mp"),
            P("mp", None),
            P(),
            P("mp", None),
            P(),
        ),
        out_specs=(
            P("dp", "mp"),
            P("dp", "mp"),
            P(),
            P(),
            P(None, "mp"),
            P("mp"),
            P("mp"),
            P("mp"),
            P(None, "mp"),
            P("mp"),
            P("mp"),
            P("mp"),
            P("mp", None),
            P(),
            P("mp", None),
            P(),
        ),
        check_vma=False,
    )
```

```python
import functools

import jax
import jax.numpy as jnp
from jax import lax
from jax.experimental import pallas as pl
from jax.experimental.pallas import tpu as pltpu
from jax.sharding import PartitionSpec as P

GROUP = 8
CONS_COEF = 20.0
REW_COEF = 0.1
EPS = 1e-05
LANES = 128
TILE = 512
SUB = 128
PART = 64
FIRST = (0, 3, 5, 6, 7, 8, 9, 11)
SECOND = (1, 6, 8, 10, 11)
MESH = pl.DeviceIdType.MESH
F32 = jnp.float32
BF16 = jnp.bfloat16


def dot(left, right, left_dim=1, right_dim=0):
    return lax.dot_general(
        left, right, (((left_dim,), (right_dim,)), ((), ())), preferred_element_type=F32
    )


def aligned(start, size):
    return pl.ds(pl.multiple_of(start, size), size)


def aligned_to(start, size):
    return pl.ds(pl.multiple_of(start, 16), size)


def split_dot(left, right, left_dim, right_dim):
    high = left.astype(BF16)
    low = (left - high.astype(F32)).astype(BF16)
    return dot(high, right, left_dim, right_dim) + dot(low, right, left_dim, right_dim)


def main_kernel(
    sizes,
    latent_in,
    next_in,
    dyn_w1,
    rew_w1,
    dyn_w2,
    rew_w2,
    dyn_b1,
    dyn_gain,
    dyn_shift,
    rew_b1,
    rew_gain,
    rew_shift,
    ids_ref,
    act_ref,
    masks_ref,
    bins_ref,
    frac_ref,
    embed_ref,
    dyn_b2,
    rew_b2,
    lat_out,
    grad_out,
    fin_dyn,
    fin_rew,
    fin_sums,
    x_all,
    x_t,
    w1_raw,
    w1_c,
    w2_t,
    rw2_t,
    vecs,
    w2_own,
    rw2_own,
    vecs_own,
    embed_wide,
    extra_rows,
    b2_ref,
    rb2_ref,
    next_lat,
    dpl,
    dpl_send,
    lat_stage,
    lg_stage,
    d_dyn,
    part_a,
    part_b,
    part_rew,
    got_a,
    got_b,
    got_rew,
    sums,
    got_sums,
    g1,
    g2t,
    rg2t,
    pre,
    dh,
    dm,
    hid,
    d_pre,
    zt,
    latt,
    dlog,
    inv_ref,
    col_acc,
    sum_acc,
    row_acc,
    b2_acc,
    load_sem,
    w_send,
    w_recv,
    n_send,
    n_recv,
    d_send,
    d_recv,
    l_local,
    l_send,
    l_recv,
    g_local,
    g_send,
    g_recv,
    r_send,
    r_recv,
    s_send,
    s_recv,
):
    n_mp, n_dp, total_rows, hid_width = sizes
    n_bits = n_dp.bit_length() - 1
    mine = lax.axis_index("mp")
    column = lax.axis_index("dp")
    pair = mine // 2
    half = mine % 2
    own_rows = x_all.shape[0] // 2
    lat_width = latent_in.shape[1]
    shard = dyn_w1.shape[1]
    n_act = act_ref.shape[0]
    in_rows = g1.shape[0]
    share = next_in.shape[1]
    n_task = embed_ref.shape[0]
    chip_cols = 2 * share
    n_tiles = own_rows // TILE
    n_lane = hid_width // LANES

    def peer_of(flip):
        near = mine + 1 - 2 * half
        if flip == 1:
            return near
        across = 2 * (1 - pair)
        return across + half if flip == 2 else across + 1 - half

    def bit_of(bit):
        return (column // (1 << bit)) % 2

    def column_peer(bit):
        return column + (1 - 2 * bit_of(bit)) * (1 << bit)

    def rows_of(device):
        return aligned(device * own_rows, own_rows)

    vecs_own[...] = jnp.zeros_like(vecs_own)
    for net, rows in enumerate(((dyn_b1, dyn_gain, dyn_shift), (rew_b1, rew_gain, rew_shift))):
        for line, ref in enumerate(rows):
            vecs_own[net, pl.ds(line, 1), :] = ref[...]
    w2_own[...] = dyn_w2[...].T
    n_bins = rew_w2.shape[0]
    rw2_own[...] = jnp.zeros_like(rw2_own)
    rw2_own[pl.ds(0, n_bins), :] = rew_w2[...]

    barrier = pltpu.get_barrier_semaphore()
    for flip in (1, 2, 3):
        pl.semaphore_signal(
            barrier, inc=1, device_id={"mp": peer_of(flip)}, device_id_type=MESH
        )
    for bit in range(n_bits):
        pl.semaphore_signal(
            barrier, inc=1, device_id={"dp": column_peer(bit)}, device_id_type=MESH
        )
    pl.semaphore_wait(barrier, 3 + n_bits)

    near, across = peer_of(1), peer_of(2)

    def w_pairs(block):
        pairs = []
        for net in range(2):
            cols = aligned(net * hid_width + block * shard, shard)
            pairs.append(((dyn_w1, rew_w1)[net], w1_raw.at[:, cols]))
            pairs.append((vecs_own.at[net], vecs.at[:, cols]))
        cols = aligned(block * shard, shard)
        pairs.append((w2_own, w2_t.at[:, cols]))
        pairs.append((rw2_own, rw2_t.at[:, cols]))
        return pairs

    w_needs = ((1, 0, 4), (3, 2, 5))
    own_weights = w_pairs(mine)

    def weight_copy(index, kind):
        source, target = own_weights[index]
        if kind == 2:
            source = target = w_pairs(across)[index][1]
        return pltpu.make_async_remote_copy(
            src_ref=source,
            dst_ref=target,
            send_sem=w_send.at[kind, index],
            recv_sem=w_recv.at[kind, index],
            device_id={"mp": across if kind == 1 else near},
            device_id_type=MESH,
        )

    def next_copy(slot):
        rows = near if slot == 1 else peer_of(3)
        return pltpu.make_async_remote_copy(
            src_ref=next_in.at[rows_of(rows), :],
            dst_ref=next_lat.at[slot, half],
            send_sem=n_send.at[slot],
            recv_sem=n_recv.at[slot],
            device_id={"mp": near},
            device_id_type=MESH,
        )

    loads = []
    for slot, device in ((0, across), (1, mine)):
        loads.append(
            (
                latent_in.at[rows_of(device), :],
                x_all.at[pl.ds(slot * own_rows, own_rows), pl.ds(0, lat_width)],
            )
        )
    for slot, device in ((0, across), (1, mine)):
        loads.append((next_in.at[rows_of(device), :], next_lat.at[slot, half]))
    loads += own_weights
    loads = [
        pltpu.make_async_copy(source, target, load_sem.at[i])
        for i, (source, target) in enumerate(loads)
    ]
    for copy in loads:
        copy.start()
    for index in w_needs[0] + w_needs[1]:
        weight_copy(index, 1).start()
        weight_copy(index, 0).start()
    next_copy(0).start()
    next_copy(1).start()

    for ref in (g1, g2t, rg2t, col_acc, sum_acc, row_acc, b2_acc):
        ref[...] = jnp.zeros_like(ref)

    line = lax.broadcasted_iota(jnp.int32, extra_rows.shape, 0)
    extra_rows[...] = jnp.where((line == n_act) | (line == n_act + 1), 1.0, 0.0)
    n_embed = embed_ref.shape[1]
    n_rest = n_act + n_embed
    moved = lax.broadcasted_iota(jnp.int32, (n_embed, n_rest), 1) == (
        lax.broadcasted_iota(jnp.int32, (n_embed, n_rest), 0) + n_act
    )
    embed_wide[...] = dot(embed_ref[...], jnp.where(moved, 1.0, 0.0).astype(BF16)).astype(BF16)
    b2_ref[...] = jnp.broadcast_to(dyn_b2[...], (LANES, lat_width)).T
    rb2_ref[...] = jnp.full(rb2_ref.shape, -1e30, F32)
    rb2_ref[:, pl.ds(0, n_bins)] = jnp.broadcast_to(rew_b2[...], (LANES, n_bins))
    rb2_ref[...] = rb2_ref[...].T

    for slot, device in ((0, across), (1, mine)):
        base = device * own_rows

        @pl.loop(0, n_tiles)
        def _(tile):
            lanes = aligned(base + tile * TILE, TILE)
            ids = ids_ref[:, lanes]
            tasks = lax.broadcasted_iota(jnp.int32, (n_task, TILE), 0)
            onehot = jnp.where(tasks == ids, 1.0, 0.0).astype(BF16)
            masks = dot(masks_ref[...].astype(F32).astype(BF16), onehot)
            extra_rows[pl.ds(0, n_act), :] = act_ref[:, lanes].astype(F32) * masks
            masked = extra_rows[...].astype(BF16)
            rest = LANES - n_task - masked.shape[0]
            extra = jnp.concatenate([onehot, masked, jnp.zeros((rest, TILE), BF16)], axis=0)
            rows = aligned(slot * own_rows + tile * TILE, TILE)
            x_all[rows, pl.ds(lat_width, LANES)] = extra.T
            if slot == 1:
                x_t[pl.ds(lat_width, LANES), aligned(tile * TILE, TILE)] = extra

    for copy in loads[:2]:
        copy.wait()

    @pl.loop(0, n_tiles)
    def _(tile):
        rows = aligned(own_rows + tile * TILE, TILE)
        x_t[pl.ds(0, lat_width), aligned(tile * TILE, TILE)] = x_all[
            rows, pl.ds(0, lat_width)
        ].T

    def centre(values):
        return values - jnp.sum(values, axis=1, keepdims=True) * (1.0 / hid_width)

    def prepare(net):
        for index in w_needs[net]:
            weight_copy(index, 1).wait_recv()
            weight_copy(index, 2).start()
        for index in w_needs[net]:
            loads[4 + index].wait()
            weight_copy(index, 0).wait_recv()
            weight_copy(index, 2).wait_recv()
        cols = pl.ds(net * hid_width, hid_width)

        @pl.loop(0, lat_width // PART)
        def _(step):
            rows = aligned(step * PART, PART)
            w1_c[rows, cols] = centre(w1_raw[rows, cols].astype(F32)).astype(BF16)

        table = dot(embed_wide[...], w1_raw[pl.ds(lat_width, n_rest), cols])
        w1_c[pl.ds(lat_width, n_task), cols] = centre(table).astype(BF16)
        act = centre(w1_raw[pl.ds(lat_width, 16), cols].astype(F32))
        bias = centre(vecs[pl.ds(0, 1), cols])
        high = bias.astype(BF16).astype(F32)
        row = lax.broadcasted_iota(jnp.int32, act.shape, 0)
        act = jnp.where(row < n_act, act, 0.0)
        act = jnp.where(row == n_act, high, jnp.where(row == n_act + 1, bias - high, act))
        w1_c[pl.ds(lat_width + n_task, 16), cols] = act.astype(BF16)
        rest = LANES - n_task - 16
        w1_c[pl.ds(lat_width + n_task + 16, rest), cols] = jnp.zeros((rest, hid_width), BF16)

    def forward(net, rows, keep):
        cols = pl.ds(net * hid_width, hid_width)
        values = dot(x_all[rows, :], w1_c[:, cols])
        pre[...] = values
        square = jnp.sum(values * values, axis=1, keepdims=True)
        inv_ref[...] = jnp.broadcast_to(
            lax.rsqrt(square * (1.0 / hid_width) + EPS), (TILE, LANES)
        )

        @pl.loop(0, TILE // SUB)
        def _(step):
            part = aligned(step * SUB, SUB)
            inv = inv_ref[part, :]
            for lane in range(n_lane):
                lanes = pl.ds(lane * LANES, LANES)
                wide = pl.ds(net * hid_width + lane * LANES, LANES)
                xhat = pre[part, lanes] * inv
                y = xhat * vecs[pl.ds(1, 1), wide] + vecs[pl.ds(2, 1), wide]
                e = jnp.exp(jnp.minimum(y, 20.0))
                e2 = e + 2.0
                r = 1.0 / (e * e2 + 2.0)
                u = e * r
                t = u * e2
                hid[part, lanes] = (y * t).astype(BF16)
                if keep:
                    pre[part, lanes] = xhat
                    dm[part, lanes] = t + (4.0 * y) * (u * (r + u))

    def backward(net, target, first_row):
        @pl.loop(0, TILE // SUB)
        def _(step):
            part = aligned(step * SUB, SUB)
            first = jnp.zeros((SUB, LANES), F32)
            second = jnp.zeros((SUB, LANES), F32)
            for lane in range(n_lane):
                lanes = pl.ds(lane * LANES, LANES)
                wide = pl.ds(net * hid_width + lane * LANES, LANES)
                d_y = dh[part, lanes] * dm[part, lanes]
                xhat = pre[part, lanes]
                scaled = d_y * xhat
                col_acc[pl.ds(0, 8), wide] += jnp.sum(
                    scaled.reshape(SUB // 8, 8, LANES), axis=0
                )
                col_acc[pl.ds(8, 8), wide] += jnp.sum(d_y.reshape(SUB // 8, 8, LANES), axis=0)
                gain = vecs[pl.ds(1, 1), wide]
                g = d_y * gain
                first += g
                second += scaled * gain
                dh[part, lanes] = g
            inv = inv_ref[part, :]
            first = jnp.broadcast_to(
                jnp.sum(first, axis=1, keepdims=True) * (1.0 / hid_width), (SUB, LANES)
            )
            second = jnp.broadcast_to(
                jnp.sum(second, axis=1, keepdims=True) * (1.0 / hid_width), (SUB, LANES)
            )
            first = first * inv
            second = second * inv
            for lane in range(n_lane):
                lanes = pl.ds(lane * LANES, LANES)
                value = dh[part, lanes] * inv - first - pre[part, lanes] * second
                target[aligned(first_row + step * SUB, SUB), lanes] = value.astype(BF16)

    d_scale = 2.0 * CONS_COEF / total_rows

    def simnorm(slot, tile, target, row, col):
        rows = aligned(tile * TILE, TILE)
        zt[...] = dot(w2_t[aligned(pair * chip_cols, chip_cols), :], hid[...], 1, 1)
        for side in range(2):
            latt[pl.ds(side * share, share), :] = next_lat[slot, side, rows, :].T.astype(F32)

        @pl.loop(0, chip_cols // PART)
        def _(step):
            part = aligned(step * PART, PART)
            bias = b2_ref[aligned(pair * chip_cols + step * PART, PART), :]
            for lane in range(TILE // LANES):
                lanes = pl.ds(lane * LANES, LANES)
                z = (zt[part, lanes] + bias).reshape(PART // GROUP, GROUP, LANES)
                e = jnp.exp(z - jnp.max(z, axis=1, keepdims=True))
                s = e * (1.0 / jnp.sum(e, axis=1, keepdims=True))
                error = s - latt[part, lanes].reshape(z.shape)
                sum_acc[pl.ds(0, 8), :] += jnp.sum(error * error, axis=0)
                d_lat = d_scale * error
                d_z = s * (d_lat - jnp.sum(s * d_lat, axis=1, keepdims=True))
                zt[part, lanes] = s.reshape(PART, LANES)
                target[
                    aligned(row + step * PART, PART), aligned(col + lane * LANES, LANES)
                ] = d_z.reshape(PART, LANES).astype(BF16)

        for side in range(2):
            lat_stage[slot, side, rows, :] = zt[pl.ds(side * share, share), :].astype(BF16).T

    def lat_copies(slot, tile):
        device = across if slot == 0 else mine
        rows = aligned(tile * TILE, TILE)
        out_rows = lat_out.at[aligned(device * own_rows + tile * TILE, TILE), :]
        index = slot * n_tiles + tile
        local = pltpu.make_async_copy(
            lat_stage.at[slot, half, rows, :], out_rows, l_local.at[index]
        )
        remote = pltpu.make_async_remote_copy(
            src_ref=lat_stage.at[slot, 1 - half, rows, :],
            dst_ref=out_rows,
            send_sem=l_send.at[index],
            recv_sem=l_recv.at[index],
            device_id={"mp": near},
            device_id_type=MESH,
        )
        return local, remote

    def dpl_copy(tile):
        cols = aligned(tile * TILE, TILE)
        return pltpu.make_async_remote_copy(
            src_ref=dpl_send.at[:, cols],
            dst_ref=dpl.at[aligned(pair * chip_cols, chip_cols), cols],
            send_sem=d_send.at[tile],
            recv_sem=d_recv.at[tile],
            device_id={"mp": across},
            device_id_type=MESH,
        )

    def grad_copies(tile):
        rows = aligned(tile * TILE, TILE)
        out_rows = grad_out.at[aligned(mine * own_rows + tile * TILE, TILE), :]
        remotes = []
        for flip in (2, 3, 1):
            peer = peer_of(flip)
            remotes.append(
                pltpu.make_async_remote_copy(
                    src_ref=lg_stage.at[peer, rows, :],
                    dst_ref=out_rows,
                    send_sem=g_send.at[flip - 1, tile],
                    recv_sem=g_recv.at[flip - 1, tile],
                    device_id={"mp": peer},
                    device_id_type=MESH,
                )
            )
        local = pltpu.make_async_copy(lg_stage.at[mine, rows, :], out_rows, g_local.at[tile])
        return local, remotes

    prepare(0)
    loads[2].wait()
    next_copy(0).wait_recv()

    @pl.loop(0, n_tiles)
    def _(tile):
        forward(0, aligned(tile * TILE, TILE), False)
        simnorm(0, tile, dpl_send, 0, tile * TILE)
        dpl_copy(tile).start()
        local, remote = lat_copies(0, tile)
        local.start()
        remote.start()

    loads[3].wait()
    next_copy(1).wait_recv()

    @pl.loop(0, n_tiles)
    def _(tile):
        cols = aligned(tile * TILE, TILE)
        forward(0, aligned(own_rows + tile * TILE, TILE), True)
        simnorm(1, tile, dpl, pair * chip_cols, tile * TILE)
        local, remote = lat_copies(1, tile)
        local.start()
        remote.start()
        dpl_copy(tile).wait_recv()
        d_lat = dpl[:, cols]
        b2_acc[...] += dot(jnp.ones((8, TILE), BF16), d_lat, 1, 1)
        g2t[...] += dot(d_lat, hid[...])
        dh[...] = dot(d_lat, w2_t[...], 0, 0)
        backward(0, d_dyn, tile * TILE)
        g1[:, pl.ds(0, hid_width)] += dot(x_t[:, cols], d_dyn[cols, :])

    def add_into(target, other, n_rows):
        step_rows = 48 if n_rows % 48 == 0 else 16

        @pl.loop(0, n_rows // step_rows)
        def _(step):
            rows = aligned(step * step_rows, step_rows)
            total = target[rows, :].astype(F32) + other[rows, :].astype(F32)
            target[rows, :] = total.astype(BF16)

    def reduction(key, part, got, fin, order, with_sums):
        n_rows = part.shape[2]
        stages, gathers = [], []
        offset, length, place, both = 0, n_rows, n_rows, True
        for what in order:
            if what == "near":
                stages.append((what, 0, 0, 0, n_rows, 0, True))
                continue
            if what == "across":
                both = False
                stages.append((what, 0, offset, offset, length, place, False))
            elif length % 32 == 0:
                length //= 2
                keep = offset + bit_of(what) * length
                send = offset + (1 - bit_of(what)) * length
                stages.append(("half", what, send, keep, length, place, both))
                gathers.append(("gather", what, keep, keep, length, 0, False))
                offset = keep
            else:
                stages.append(("whole", what, offset, offset, length, place, both))
            place += length
        last = len(stages)
        stages += gathers[::-1]

        def ends(index):
            kind, bit, send, keep, count, spot, two = stages[index]
            if kind == "near":
                return part.at[1 - half], got.at[:, pl.ds(0, n_rows), :], {"mp": near}
            rows, spots = aligned_to(send, count), pl.ds(spot, count)
            if kind == "across":
                return part.at[half, 1 - pair, rows, :], got.at[0, spots, :], {"mp": across}
            device = {"dp": column_peer(bit)}
            if kind == "gather":
                return fin.at[rows, :], fin.at[rows, :], device
            if two:
                return part.at[half, :, rows, :], got.at[:, spots, :], device
            return part.at[half, pair, rows, :], got.at[0, spots, :], device

        def copy(index):
            source, target, device = ends(index)
            return pltpu.make_async_remote_copy(
                src_ref=source,
                dst_ref=target,
                send_sem=r_send.at[key, index],
                recv_sem=r_recv.at[key, index],
                device_id=device,
                device_id_type=MESH,
            )

        def sums_copy(index):
            return pltpu.make_async_remote_copy(
                src_ref=sums.at[index],
                dst_ref=got_sums.at[index],
                send_sem=s_send.at[index],
                recv_sem=s_recv.at[index],
                device_id=ends(index)[2],
                device_id_type=MESH,
            )

        def start(index):
            copy(index).start()
            if with_sums and index < last:
                sums_copy(index).start()

        def finish(index):
            kind, bit, send, keep, count, spot, two = stages[index]
            if kind == "whole":
                copy(index).wait_send()
            copy(index).wait_recv()
            if with_sums and index < last:
                sums_copy(index).wait_recv()
                sums[index + 1] = sums[index] + got_sums[index]
            if kind != "gather":
                rows, spots = aligned_to(keep, count), pl.ds(spot, count)
                for side in range(2):
                    if two:
                        add_into(part.at[half, side, rows, :], got.at[side, spots, :], count)
                    elif side == 0:
                        add_into(part.at[half, pair, rows, :], got.at[0, spots, :], count)
            if index + 1 == last:
                rows = aligned_to(offset, length)
                fin[rows, :] = part[half, pair, rows, :]
            if index + 1 < len(stages):
                start(index + 1)

        def drain():
            for index, stage in enumerate(stages):
                if stage[0] != "whole":
                    copy(index).wait_send()
                if with_sums and index < last:
                    sums_copy(index).wait_send()

        return start, finish, drain, len(stages)

    def fill(part, net, first, count, source, base):
        for device in range(n_mp):
            cols = pl.ds(net * hid_width + device * shard, shard)
            part[device % 2, device // 2, pl.ds(first, count), :] = source[
                pl.ds(base, count), cols
            ].astype(BF16)

    def add_columns(net):
        cols = pl.ds(net * hid_width, hid_width)
        for line in range(2):
            g1[pl.ds(lat_width + n_task + 8 + line, 1), cols] = jnp.sum(
                col_acc[pl.ds(8 * line, 8), cols], axis=0, keepdims=True
            )

    bits = list(range(n_bits))
    add_columns(0)
    fill(part_a, 0, 0, lat_width, g2t, 0)
    fill(part_b, 0, 0, in_rows, g1, 0)
    chunks = [
        reduction(0, part_a, got_a, fin_dyn.at[pl.ds(in_rows, lat_width), :], ["near"] + bits + ["across"], False),
        reduction(1, part_b, got_b, fin_dyn.at[pl.ds(0, in_rows), :], ["near"] + bits + ["across"], False),
    ]
    for chunk in chunks:
        chunk[0](0)
    n_stages = 2 + 2 * n_bits
    per_tile = 3
    events = [
        (chunk, index, (FIRST, SECOND)[chunk][index])
        for index in range(n_stages)
        for chunk in range(2)
        if index < min(chunks[chunk][3], len((FIRST, SECOND)[chunk]))
    ]
    inside = [event for event in events if event[2] < per_tile * n_tiles]
    inside.sort(key=lambda event: event[2])
    done = [(event[0], event[1]) for event in inside]

    prepare(1)

    def point(tile, number):
        for chunk, index, place in inside:
            if place % per_tile == number:

                @pl.when(tile == place // per_tile)
                def _():
                    chunks[chunk][1](index)

    @pl.loop(0, n_tiles)
    def _(tile):
        cols = aligned(tile * TILE, TILE)
        forward(1, aligned(own_rows + tile * TILE, TILE), True)
        point(tile, 0)
        bins = bins_ref[:, aligned(mine * own_rows + tile * TILE, TILE)]
        frac = frac_ref[:, aligned(mine * own_rows + tile * TILE, TILE)]
        z = dot(rw2_t[...], hid[...], 1, 1)
        bias = rb2_ref[...]
        z = z + jnp.concatenate([bias] * (TILE // LANES), axis=1)
        z = z - jnp.max(z, axis=0, keepdims=True)
        e = jnp.exp(z)
        total = jnp.sum(e, axis=0, keepdims=True)
        row = lax.broadcasted_iota(jnp.int32, z.shape, 0)
        target = jnp.where(row == bins, 1.0 - frac, 0.0) + jnp.where(row == bins + 1, frac, 0.0)
        loss = jnp.sum(target * (jnp.log(total) - z), axis=0, keepdims=True)
        row_acc[...] += loss
        d_logits = (REW_COEF / total_rows) * (e * (1.0 / total) - target)
        dlog[...] = d_logits.astype(BF16)
        sum_acc[pl.ds(8, 8), :] += dot(jnp.ones((8, TILE), BF16), dlog[...], 1, 1)
        rg2t[...] += dot(dlog[...], hid[...])
        dh[...] = dot(dlog[...], rw2_t[...], 0, 0)
        backward(1, d_pre, 0)
        point(tile, 1)
        lat_rows = pl.ds(0, lat_width)
        lg = dot(d_dyn[cols, :], w1_raw[lat_rows, pl.ds(0, hid_width)], 1, 1)
        lg = lg + dot(d_pre[...], w1_raw[lat_rows, pl.ds(hid_width, hid_width)], 1, 1)
        lg = (lg * total_rows).astype(BF16)
        for device in range(n_mp):
            lg_stage[device, cols, :] = lg[:, device * share : (device + 1) * share]
        local, remotes = grad_copies(tile)
        local.start()
        for remote in remotes:
            remote.start()
        g1[:, pl.ds(hid_width, hid_width)] += dot(x_t[:, cols], d_pre[...])
        point(tile, 2)

    add_columns(1)
    fill_rows = part_rew.shape[3]
    for device in range(n_mp):
        cols = pl.ds(hid_width + device * shard, shard)
        block = pl.ds(device * shard, shard)
        where = (device % 2, device // 2)
        part_rew[(0,) + where] = g1[pl.ds(0, fill_rows), cols].astype(BF16)
        part_rew[(1,) + where + (pl.ds(0, in_rows - fill_rows),)] = g1[
            pl.ds(fill_rows, in_rows - fill_rows), cols
        ].astype(BF16)
        part_rew[(1,) + where + (pl.ds(in_rows - fill_rows, LANES),)] = rg2t[:, block].astype(BF16)
    tasks = g1[pl.ds(lat_width, n_task), :]
    table = split_dot(tasks, w1_raw[pl.ds(lat_width, n_rest), :], 1, 1).astype(BF16)
    spare = in_rows - fill_rows - 32
    for device in range(n_mp):
        where = (1, device % 2, device // 2)
        part_rew[where + (pl.ds(spare, 32), pl.ds(0, n_rest))] = table[0:32]
        part_rew[where + (pl.ds(spare, 32), pl.ds(LANES, n_rest))] = table[32:64]
        part_rew[where + (pl.ds(fill_rows - 16, 16), pl.ds(0, n_rest))] = table[64:80]
    sums[0] = jnp.zeros(sums.shape[1:], F32)
    sums[0, pl.ds(0, 1), :] = b2_acc[pl.ds(0, 1), :]
    sums[0, pl.ds(1, 1), pl.ds(0, LANES)] = sum_acc[pl.ds(8, 1), :]
    cons = jnp.sum(sum_acc[pl.ds(0, 8), :])
    rew = jnp.sum(row_acc[...])
    sums[0, pl.ds(2, 1), :] = jnp.full((1, lat_width), cons)
    sums[0, pl.ds(3, 1), :] = jnp.full((1, lat_width), rew)
    orders = (["near", "across"] + bits, ["near"] + bits[:1] + ["across"] + bits[1:])
    for k in range(2):
        chunks.append(
            reduction(
                2 + k,
                part_rew.at[k],
                got_rew.at[k],
                fin_rew.at[pl.ds(k * fill_rows, fill_rows), :],
                orders[k],
                k == 0,
            )
        )
    chunks[2][0](0)
    chunks[3][0](0)
    left = [(c, index) for index in range(n_stages) for c in range(2) if (c, index) not in done]
    left += [(c, index) for index in range(n_stages) for c in (2, 3)]
    left.sort(key=lambda event: event[1] if event[0] > 1 else event[1] - len(done) // 2)
    for chunk, index in left:
        if index < chunks[chunk][3]:
            chunks[chunk][1](index)
    fin_sums[...] = sums[2 + n_bits]
    for chunk in chunks:
        chunk[2]()

    for index in range(6):
        for kind in range(3):
            weight_copy(index, kind).wait_send()
    for slot in range(2):
        next_copy(slot).wait_send()

        @pl.loop(0, n_tiles)
        def _(tile):
            local, remote = lat_copies(slot, tile)
            local.wait()
            remote.wait()

    @pl.loop(0, n_tiles)
    def _(tile):
        dpl_copy(tile).wait_send()
        local, remotes = grad_copies(tile)
        local.wait()
        for remote in remotes:
            remote.wait()


def finish_kernel(
    dyn,
    rew,
    sums,
    embed,
    losses,
    grad_embed,
    dyn_w1,
    dyn_b1,
    dyn_gain,
    dyn_shift,
    rew_w1,
    rew_b1,
    rew_gain,
    rew_shift,
    dyn_w2,
    dyn_b2,
    rew_w2,
    rew_b2,
    *,
    total_rows,
    lat_width,
):
    n_task, n_embed = embed.shape
    n_rest = dyn_w1.shape[0] - lat_width
    n_act = n_rest - n_embed
    in_rows = lat_width + LANES
    first = lat_width + n_task
    moved = lax.broadcasted_iota(jnp.int32, (n_embed, n_rest), 1) == (
        lax.broadcasted_iota(jnp.int32, (n_embed, n_rest), 0) + n_act
    )
    moved = jnp.where(moved, 1.0, 0.0).astype(BF16)
    line = lax.broadcasted_iota(jnp.int32, (LANES - n_task, n_rest), 0)
    lane = lax.broadcasted_iota(jnp.int32, (LANES - n_task, n_rest), 1)
    acts = jnp.where((line == lane) & (line < n_act), 1.0, 0.0).astype(BF16)
    mix = jnp.concatenate([dot(embed[...], moved).astype(BF16), acts], axis=0)
    for net, w1, b1, gain, shift in (
        (dyn, dyn_w1, dyn_b1, dyn_gain, dyn_shift),
        (rew, rew_w1, rew_b1, rew_gain, rew_shift),
    ):
        w1[pl.ds(0, lat_width), :] = net[pl.ds(0, lat_width), :].astype(F32)
        w1[pl.ds(lat_width, n_rest), :] = dot(mix, net[pl.ds(lat_width, LANES), :], 0, 0)
        small = net[pl.ds(first, 16), :].astype(F32)
        b1[...] = small[n_act : n_act + 1]
        gain[...] = small[8:9]
        shift[...] = small[9:10]
    dyn_w2[...] = dyn[pl.ds(in_rows, lat_width), :].astype(F32).T
    n_bins = rew_w2.shape[0]
    rew_w2[...] = rew[pl.ds(in_rows, LANES), :].astype(F32)[:n_bins]
    dyn_b2[...] = sums[pl.ds(0, 1), :]
    rew_b2[...] = sums[pl.ds(1, 1), pl.ds(0, n_bins)]
    pieces = (
        (0, 32, in_rows - 32, 0),
        (32, 32, in_rows - 32, LANES),
        (64, n_task - 64, in_rows + LANES - 16, 0),
    )
    for to, count, row, col in pieces:
        grad_embed[pl.ds(to, count), :] = dot(
            rew[pl.ds(row, count), pl.ds(col, n_rest)], moved, 1, 1
        )
    pick = lax.broadcasted_iota(jnp.int32, losses.shape, 1) == 0
    both = jnp.where(pick, sums[pl.ds(2, 1), pl.ds(0, 2)], sums[pl.ds(3, 1), pl.ds(0, 2)])
    losses[...] = both * (1.0 / total_rows)


def run_finish(total_rows, lat_width, n_in, n_bins, dyn, rew, sums, embed):
    shape = jax.ShapeDtypeStruct
    shard = dyn.shape[1]
    line = shape((1, shard), F32)
    first = [shape((n_in, shard), F32), line, line, line]
    return pl.pallas_call(
        functools.partial(finish_kernel, total_rows=total_rows, lat_width=lat_width),
        out_shape=(
            shape((1, 2), F32),
            shape(embed.shape, F32),
            *first,
            *first,
            shape((shard, lat_width), F32),
            shape((1, lat_width), F32),
            shape((n_bins, shard), F32),
            shape((1, n_bins), F32),
        ),
        compiler_params=pltpu.CompilerParams(vmem_limit_bytes=32 << 20),
    )(dyn, rew, sums, embed)


def run_main(n_mp, n_dp, total_rows, args):
    latent, next_latent, w1, dyn_w2, rew_w2 = args[0], args[1], args[2], args[4], args[5]
    tok_rows, lat_width = latent.shape
    share = next_latent.shape[1]
    n_in, shard = w1.shape
    hid_width = n_mp * shard
    own = tok_rows // n_mp
    in_rows = lat_width + LANES
    n_tiles = own // TILE
    n_task = args[17].shape[0]
    any_spec = pl.BlockSpec(memory_space=pl.ANY)
    vmem_spec = pl.BlockSpec(memory_space=pltpu.VMEM)
    shape = jax.ShapeDtypeStruct
    dma = pltpu.SemaphoreType.DMA
    n_bits = n_dp.bit_length() - 1
    n_stages = 2 + 2 * n_bits
    rew_rows = (in_rows + LANES) // 2

    def room(rows):
        extra, length = 0, rows
        for _ in range(n_bits):
            length = length // 2 if length % 32 == 0 else length
            extra += length
        return 2 * rows + extra

    any_spec = pl.BlockSpec(memory_space=pl.ANY)
    vmem_spec = pl.BlockSpec(memory_space=pltpu.VMEM)
    shape = jax.ShapeDtypeStruct
    dma = pltpu.SemaphoreType.DMA
    return pl.pallas_call(
        functools.partial(main_kernel, (n_mp, n_dp, total_rows, hid_width)),
        out_shape=(
            shape((tok_rows, share), BF16),
            shape((tok_rows, share), BF16),
            shape((in_rows + lat_width, shard), BF16),
            shape((2 * rew_rows, shard), BF16),
            shape((8, lat_width), F32),
        ),
        in_specs=[any_spec] * 4 + [vmem_spec] * 16,
        out_specs=[any_spec] * 2 + [vmem_spec] * 3,
        scratch_shapes=[
            pltpu.VMEM((2 * own, in_rows), BF16),
            pltpu.VMEM((in_rows, own), BF16),
            pltpu.VMEM((n_in, 2 * hid_width), BF16),
            pltpu.VMEM((in_rows, 2 * hid_width), BF16),
            pltpu.VMEM((lat_width, hid_width), BF16),
            pltpu.VMEM((LANES, hid_width), BF16),
            pltpu.VMEM((8, 2 * hid_width), F32),
            pltpu.VMEM((lat_width, shard), BF16),
            pltpu.VMEM((LANES, shard), BF16),
            pltpu.VMEM((2, 8, shard), F32),
            pltpu.VMEM((n_task, n_in - lat_width), BF16),
            pltpu.VMEM((16, TILE), F32),
            pltpu.VMEM((lat_width, LANES), F32),
            pltpu.VMEM((LANES, LANES), F32),
            pltpu.VMEM((2, 2, own, share), BF16),
            pltpu.VMEM((lat_width, own), BF16),
            pltpu.VMEM((2 * share, own), BF16),
            pltpu.VMEM((2, 2, own, share), BF16),
            pltpu.VMEM((n_mp, own, share), BF16),
            pltpu.VMEM((own, hid_width), BF16),
            pltpu.VMEM((2, 2, lat_width, shard), BF16),
            pltpu.VMEM((2, 2, in_rows, shard), BF16),
            pltpu.VMEM((2, 2, 2, rew_rows, shard), BF16),
            pltpu.VMEM((2, room(lat_width), shard), BF16),
            pltpu.VMEM((2, room(in_rows), shard), BF16),
            pltpu.VMEM((2, 2, room(rew_rows), shard), BF16),
            pltpu.VMEM((3 + n_bits, 8, lat_width), F32),
            pltpu.VMEM((2 + n_bits, 8, lat_width), F32),
            pltpu.VMEM((in_rows, 2 * hid_width), F32),
            pltpu.VMEM((lat_width, hid_width), F32),
            pltpu.VMEM((LANES, hid_width), F32),
            pltpu.VMEM((TILE, hid_width), F32),
            pltpu.VMEM((TILE, hid_width), F32),
            pltpu.VMEM((TILE, hid_width), F32),
            pltpu.VMEM((TILE, hid_width), BF16),
            pltpu.VMEM((TILE, hid_width), BF16),
            pltpu.VMEM((2 * share, TILE), F32),
            pltpu.VMEM((2 * share, TILE), F32),
            pltpu.VMEM((LANES, TILE), BF16),
            pltpu.VMEM((TILE, LANES), F32),
            pltpu.VMEM((16, 2 * hid_width), F32),
            pltpu.VMEM((16, LANES), F32),
            pltpu.VMEM((1, TILE), F32),
            pltpu.VMEM((8, lat_width), F32),
            dma((10,)),
            dma((3, 6)),
            dma((3, 6)),
            dma((2,)),
            dma((2,)),
            dma((n_tiles,)),
            dma((n_tiles,)),
            dma((2 * n_tiles,)),
            dma((2 * n_tiles,)),
            dma((2 * n_tiles,)),
            dma((n_tiles,)),
            dma((3, n_tiles)),
            dma((3, n_tiles)),
            dma((4, n_stages)),
            dma((4, n_stages)),
            dma((2 + n_bits,)),
            dma((2 + n_bits,)),
        ],
        compiler_params=pltpu.CompilerParams(
            collective_id=0, has_side_effects=True, vmem_limit_bytes=60 << 20
        ),
    )(*args)


def on_device(
    latent,
    actions,
    task_ids,
    action_masks,
    next_latent,
    reward_bins,
    reward_frac,
    task_embed,
    dyn_w1,
    dyn_b1,
    dyn_gain,
    dyn_shift,
    rew_w1,
    rew_b1,
    rew_gain,
    rew_shift,
    dyn_w2,
    dyn_b2,
    rew_w2,
    rew_b2,
):
    n_mp, n_dp = lax.axis_size("mp"), lax.axis_size("dp")
    tok_rows, lat_width = latent.shape
    total_rows = tok_rows * n_dp

    def row(vector):
        return vector.reshape(1, -1)

    args = (
        latent,
        next_latent,
        dyn_w1,
        rew_w1,
        dyn_w2,
        rew_w2.T,
        *(row(v) for v in (dyn_b1, dyn_gain, dyn_shift, rew_b1, rew_gain, rew_shift)),
        row(task_ids),
        actions,
        action_masks.T,
        row(reward_bins),
        row(reward_frac),
        task_embed,
        row(dyn_b2),
        row(rew_b2),
    )
    latents, latent_grad, dyn, rew, sums = run_main(n_mp, n_dp, total_rows, args)
    outs = run_finish(
        total_rows, lat_width, dyn_w1.shape[0], rew_b2.shape[0], dyn, rew, sums, task_embed
    )
    outs = [out.reshape(-1) if out.shape[0] == 1 else out for out in outs]
    outs[12] = outs[12].T
    return (latents, latent_grad, *outs)


def solution(mesh):
    return jax.shard_map(
        on_device,
        mesh=mesh,
        in_specs=(
            P("dp", None),
            P(None, "dp"),
            P("dp"),
            P(),
            P("dp", "mp"),
            P("dp"),
            P("dp"),
            P(),
            P(None, "mp"),
            P("mp"),
            P("mp"),
            P("mp"),
            P(None, "mp"),
            P("mp"),
            P("mp"),
            P("mp"),
            P("mp", None),
            P(),
            P("mp", None),
            P(),
        ),
        out_specs=(
            P("dp", "mp"),
            P("dp", "mp"),
            P(),
            P(),
            P(None, "mp"),
            P("mp"),
            P("mp"),
            P("mp"),
            P(None, "mp"),
            P("mp"),
            P("mp"),
            P("mp"),
            P("mp", None),
            P(),
            P("mp", None),
            P(),
        ),
        check_vma=False,
    )
```

```python
import functools

import jax
import jax.numpy as jnp
from jax import lax
from jax.experimental import pallas as pl
from jax.experimental.pallas import tpu as pltpu
from jax.sharding import PartitionSpec as P

GROUP = 8
CONS_COEF = 20.0
REW_COEF = 0.1
EPS = 1e-05
LANES = 128
TILE = 512
SUB = 128
PART = 64
LATE = 1
PIECES = 4
EVENTS = ((0, 6, 10, 13, 99, 99), (0, 5, 9, 12, 15, 99), (0, 6, 9, 11, 13, 99))
MESH = pl.DeviceIdType.MESH
F32 = jnp.float32
BF16 = jnp.bfloat16


def dot(left, right, left_dim=1, right_dim=0):
    return lax.dot_general(
        left, right, (((left_dim,), (right_dim,)), ((), ())), preferred_element_type=F32
    )


def aligned(start, size):
    return pl.ds(pl.multiple_of(start, size), size)


def aligned_to(start, size):
    return pl.ds(pl.multiple_of(start, 16), size)


def column_groups(n_bits):
    groups = [group for group in ((0,), (1, 2)) if group[-1] < n_bits]
    return groups + [(bit,) for bit in range(sum(map(len, groups)), n_bits)]


def flips(group):
    return range(1, 1 << len(group))


def mask_of(group, flip):
    return sum(1 << bit for at, bit in enumerate(group) if flip >> at & 1)


def group_masks(group):
    return [mask_of(group, flip) for flip in flips(group)] + [1 << bit for bit in group]


def room(n_rows, n_bits):
    extra, length = 2 * n_rows, n_rows
    for group in column_groups(n_bits):
        if length % (16 << len(group)) == 0:
            length >>= len(group)
            extra += length * ((1 << len(group)) - 1)
        else:
            for _ in group:
                length = length // 2 if length % 32 == 0 else length
                extra += length
    return extra


def split_dot(left, right, left_dim, right_dim):
    high = left.astype(BF16)
    low = (left - high.astype(F32)).astype(BF16)
    return dot(high, right, left_dim, right_dim) + dot(low, right, left_dim, right_dim)


def main_kernel(
    sizes,
    latent_in,
    next_in,
    dyn_w1,
    rew_w1,
    dyn_w2,
    rew_w2,
    dyn_b1,
    dyn_gain,
    dyn_shift,
    rew_b1,
    rew_gain,
    rew_shift,
    ids_ref,
    act_ref,
    masks_ref,
    bins_ref,
    frac_ref,
    embed_ref,
    dyn_b2,
    rew_b2,
    lat_out,
    grad_out,
    fin_dyn,
    fin_rew,
    fin_sums,
    x_all,
    x_t,
    w1_raw,
    w1_c,
    w2_t,
    rw2_t,
    vecs,
    w2_own,
    rw2_own,
    vecs_own,
    embed_wide,
    extra_rows,
    b2_ref,
    rb2_ref,
    next_lat,
    dpl,
    dpl_send,
    lat_stage,
    lg_stage,
    d_dyn,
    part_a,
    part_b,
    part_c,
    part_rew,
    got_a,
    got_b,
    got_c,
    got_rew,
    sums,
    got_sums,
    g1,
    g2t,
    rg2t,
    pre,
    dh,
    dm,
    hid,
    d_pre,
    zt,
    latt,
    dlog,
    inv_ref,
    col_acc,
    sum_acc,
    row_acc,
    b2_acc,
    load_sem,
    w_send,
    w_recv,
    n_send,
    n_recv,
    d_send,
    d_recv,
    l_local,
    l_send,
    l_recv,
    g_local,
    g_send,
    g_recv,
    r_send,
    r_recv,
    s_send,
    s_recv,
):
    n_mp, n_dp, total_rows, hid_width = sizes
    n_bits = n_dp.bit_length() - 1
    mine = lax.axis_index("mp")
    column = lax.axis_index("dp")
    pair = mine // 2
    half = mine % 2
    own_rows = x_all.shape[0] // 2
    lat_width = latent_in.shape[1]
    shard = dyn_w1.shape[1]
    n_act = act_ref.shape[0]
    in_rows = g1.shape[0]
    share = next_in.shape[1]
    n_task = embed_ref.shape[0]
    chip_cols = 2 * share
    n_tiles = own_rows // TILE
    n_lane = hid_width // LANES

    def peer_of(flip):
        near = mine + 1 - 2 * half
        if flip == 1:
            return near
        across = 2 * (1 - pair)
        return across + half if flip == 2 else across + 1 - half

    def bit_of(bit):
        return (column // (1 << bit)) % 2

    def column_peer(mask):
        peer = column
        for bit in range(n_bits):
            if mask >> bit & 1:
                peer = peer + (1 - 2 * bit_of(bit)) * (1 << bit)
        return peer

    groups = column_groups(n_bits)

    def place_in(group, flip):
        place = 0
        for at, bit in enumerate(group):
            here = 1 - bit_of(bit) if flip >> at & 1 else bit_of(bit)
            place = place + here * (1 << (len(group) - 1 - at))
        return place

    def rows_of(device):
        return aligned(device * own_rows, own_rows)

    vecs_own[...] = jnp.zeros_like(vecs_own)
    for net, rows in enumerate(((dyn_b1, dyn_gain, dyn_shift), (rew_b1, rew_gain, rew_shift))):
        for line, ref in enumerate(rows):
            vecs_own[net, pl.ds(line, 1), :] = ref[...]
    w2_own[...] = dyn_w2[...].T
    n_bins = rew_w2.shape[0]
    rw2_own[...] = jnp.zeros_like(rw2_own)
    rw2_own[pl.ds(0, n_bins), :] = rew_w2[...]

    barrier = pltpu.get_barrier_semaphore()
    for flip in (1, 2, 3):
        pl.semaphore_signal(
            barrier, inc=1, device_id={"mp": peer_of(flip)}, device_id_type=MESH
        )
    masks = sorted({mask for group in groups for mask in group_masks(group)})
    for mask in masks:
        pl.semaphore_signal(
            barrier, inc=1, device_id={"dp": column_peer(mask)}, device_id_type=MESH
        )
    pl.semaphore_wait(barrier, 3 + len(masks))

    near, across = peer_of(1), peer_of(2)

    def w_pairs(block):
        pairs = []
        for net in range(2):
            cols = aligned(net * hid_width + block * shard, shard)
            pairs.append(((dyn_w1, rew_w1)[net], w1_raw.at[:, cols]))
            pairs.append((vecs_own.at[net], vecs.at[:, cols]))
        cols = aligned(block * shard, shard)
        pairs.append((w2_own, w2_t.at[:, cols]))
        pairs.append((rw2_own, rw2_t.at[:, cols]))
        return pairs

    w_needs = ((1, 0, 4), (3, 2, 5))
    own_weights = w_pairs(mine)

    def weight_copy(index, kind):
        source, target = own_weights[index]
        if kind == 2:
            source = target = w_pairs(across)[index][1]
        return pltpu.make_async_remote_copy(
            src_ref=source,
            dst_ref=target,
            send_sem=w_send.at[kind, index],
            recv_sem=w_recv.at[kind, index],
            device_id={"mp": across if kind == 1 else near},
            device_id_type=MESH,
        )

    def next_copy(slot):
        rows = near if slot == 1 else peer_of(3)
        return pltpu.make_async_remote_copy(
            src_ref=next_in.at[rows_of(rows), :],
            dst_ref=next_lat.at[slot, half],
            send_sem=n_send.at[slot],
            recv_sem=n_recv.at[slot],
            device_id={"mp": near},
            device_id_type=MESH,
        )

    loads = []
    for slot, device in ((0, across), (1, mine)):
        loads.append(
            (
                latent_in.at[rows_of(device), :],
                x_all.at[pl.ds(slot * own_rows, own_rows), pl.ds(0, lat_width)],
            )
        )
    for slot, device in ((0, across), (1, mine)):
        loads.append((next_in.at[rows_of(device), :], next_lat.at[slot, half]))
    loads += own_weights
    loads = [
        pltpu.make_async_copy(source, target, load_sem.at[i])
        for i, (source, target) in enumerate(loads)
    ]
    for copy in loads:
        copy.start()
    for index in w_needs[0] + w_needs[1]:
        weight_copy(index, 1).start()
        weight_copy(index, 0).start()
    next_copy(0).start()
    next_copy(1).start()

    for ref in (g1, g2t, rg2t, col_acc, sum_acc, row_acc, b2_acc):
        ref[...] = jnp.zeros_like(ref)

    line = lax.broadcasted_iota(jnp.int32, extra_rows.shape, 0)
    extra_rows[...] = jnp.where((line == n_act) | (line == n_act + 1), 1.0, 0.0)
    n_embed = embed_ref.shape[1]
    n_rest = n_act + n_embed
    moved = lax.broadcasted_iota(jnp.int32, (n_embed, n_rest), 1) == (
        lax.broadcasted_iota(jnp.int32, (n_embed, n_rest), 0) + n_act
    )
    embed_wide[...] = dot(embed_ref[...], jnp.where(moved, 1.0, 0.0).astype(BF16)).astype(BF16)
    b2_ref[...] = jnp.broadcast_to(dyn_b2[...], (LANES, lat_width)).T
    rb2_ref[...] = jnp.full(rb2_ref.shape, -1e30, F32)
    rb2_ref[:, pl.ds(0, n_bins)] = jnp.broadcast_to(rew_b2[...], (LANES, n_bins))
    rb2_ref[...] = rb2_ref[...].T

    for slot, device in ((0, across), (1, mine)):
        base = device * own_rows

        @pl.loop(0, n_tiles)
        def _(tile):
            lanes = aligned(base + tile * TILE, TILE)
            ids = ids_ref[:, lanes]
            tasks = lax.broadcasted_iota(jnp.int32, (n_task, TILE), 0)
            onehot = jnp.where(tasks == ids, 1.0, 0.0).astype(BF16)
            masks = dot(masks_ref[...].astype(F32).astype(BF16), onehot)
            extra_rows[pl.ds(0, n_act), :] = act_ref[:, lanes].astype(F32) * masks
            masked = extra_rows[...].astype(BF16)
            rest = LANES - n_task - masked.shape[0]
            extra = jnp.concatenate([onehot, masked, jnp.zeros((rest, TILE), BF16)], axis=0)
            rows = aligned(slot * own_rows + tile * TILE, TILE)
            x_all[rows, pl.ds(lat_width, LANES)] = extra.T
            if slot == 1:
                x_t[pl.ds(lat_width, LANES), aligned(tile * TILE, TILE)] = extra

    for copy in loads[:2]:
        copy.wait()

    @pl.loop(0, n_tiles)
    def _(tile):
        rows = aligned(own_rows + tile * TILE, TILE)
        x_t[pl.ds(0, lat_width), aligned(tile * TILE, TILE)] = x_all[
            rows, pl.ds(0, lat_width)
        ].T

    def centre(values):
        return values - jnp.sum(values, axis=1, keepdims=True) * (1.0 / hid_width)

    def gathered(indices):
        for index in indices:
            weight_copy(index, 1).wait_recv()
            weight_copy(index, 2).start()
        for index in indices:
            loads[4 + index].wait()
            weight_copy(index, 0).wait_recv()
            weight_copy(index, 2).wait_recv()

    def prepare(net):
        gathered(w_needs[net][:2])
        cols = pl.ds(net * hid_width, hid_width)

        @pl.loop(0, lat_width // PART)
        def _(step):
            rows = aligned(step * PART, PART)
            w1_c[rows, cols] = centre(w1_raw[rows, cols].astype(F32)).astype(BF16)

        table = dot(embed_wide[...], w1_raw[pl.ds(lat_width, n_rest), cols])
        w1_c[pl.ds(lat_width, n_task), cols] = centre(table).astype(BF16)
        act = centre(w1_raw[pl.ds(lat_width, 16), cols].astype(F32))
        bias = centre(vecs[pl.ds(0, 1), cols])
        high = bias.astype(BF16).astype(F32)
        row = lax.broadcasted_iota(jnp.int32, act.shape, 0)
        act = jnp.where(row < n_act, act, 0.0)
        act = jnp.where(row == n_act, high, jnp.where(row == n_act + 1, bias - high, act))
        w1_c[pl.ds(lat_width + n_task, 16), cols] = act.astype(BF16)
        rest = LANES - n_task - 16
        w1_c[pl.ds(lat_width + n_task + 16, rest), cols] = jnp.zeros((rest, hid_width), BF16)

    def forward(net, rows, keep):
        cols = pl.ds(net * hid_width, hid_width)
        values = dot(x_all[rows, :], w1_c[:, cols])
        pre[...] = values
        square = jnp.sum(values * values, axis=1, keepdims=True)
        inv_ref[...] = jnp.broadcast_to(
            lax.rsqrt(square * (1.0 / hid_width) + EPS), (TILE, LANES)
        )

        @pl.loop(0, TILE // SUB)
        def _(step):
            part = aligned(step * SUB, SUB)
            inv = inv_ref[part, :]
            for lane in range(n_lane):
                lanes = pl.ds(lane * LANES, LANES)
                wide = pl.ds(net * hid_width + lane * LANES, LANES)
                xhat = pre[part, lanes] * inv
                y = xhat * vecs[pl.ds(1, 1), wide] + vecs[pl.ds(2, 1), wide]
                e = jnp.exp(jnp.minimum(y, 20.0))
                e2 = e + 2.0
                r = 1.0 / (e * e2 + 2.0)
                u = e * r
                t = u * e2
                hid[part, lanes] = (y * t).astype(BF16)
                if keep:
                    pre[part, lanes] = xhat
                    dm[part, lanes] = t + (4.0 * y) * (u * (r + u))

    def backward(net, target, first_row):
        @pl.loop(0, TILE // SUB)
        def _(step):
            part = aligned(step * SUB, SUB)
            first = jnp.zeros((SUB, LANES), F32)
            second = jnp.zeros((SUB, LANES), F32)
            for lane in range(n_lane):
                lanes = pl.ds(lane * LANES, LANES)
                wide = pl.ds(net * hid_width + lane * LANES, LANES)
                d_y = dh[part, lanes] * dm[part, lanes]
                xhat = pre[part, lanes]
                scaled = d_y * xhat
                col_acc[pl.ds(0, 8), wide] += jnp.sum(
                    scaled.reshape(SUB // 8, 8, LANES), axis=0
                )
                col_acc[pl.ds(8, 8), wide] += jnp.sum(d_y.reshape(SUB // 8, 8, LANES), axis=0)
                gain = vecs[pl.ds(1, 1), wide]
                g = d_y * gain
                first += g
                second += scaled * gain
                dh[part, lanes] = g
            inv = inv_ref[part, :]
            first = jnp.broadcast_to(
                jnp.sum(first, axis=1, keepdims=True) * (1.0 / hid_width), (SUB, LANES)
            )
            second = jnp.broadcast_to(
                jnp.sum(second, axis=1, keepdims=True) * (1.0 / hid_width), (SUB, LANES)
            )
            first = first * inv
            second = second * inv
            for lane in range(n_lane):
                lanes = pl.ds(lane * LANES, LANES)
                value = dh[part, lanes] * inv - first - pre[part, lanes] * second
                target[aligned(first_row + step * SUB, SUB), lanes] = value.astype(BF16)

    d_scale = 2.0 * CONS_COEF / total_rows

    def simnorm(slot, tile, target, row, col):
        rows = aligned(tile * TILE, TILE)
        zt[...] = dot(w2_t[aligned(pair * chip_cols, chip_cols), :], hid[...], 1, 1)
        for side in range(2):
            latt[pl.ds(side * share, share), :] = next_lat[slot, side, rows, :].T.astype(F32)

        @pl.loop(0, chip_cols // PART)
        def _(step):
            part = aligned(step * PART, PART)
            bias = b2_ref[aligned(pair * chip_cols + step * PART, PART), :]
            for lane in range(TILE // LANES):
                lanes = pl.ds(lane * LANES, LANES)
                z = (zt[part, lanes] + bias).reshape(PART // GROUP, GROUP, LANES)
                e = jnp.exp(z - jnp.max(z, axis=1, keepdims=True))
                s = e * (1.0 / jnp.sum(e, axis=1, keepdims=True))
                error = s - latt[part, lanes].reshape(z.shape)
                sum_acc[pl.ds(0, 8), :] += jnp.sum(error * error, axis=0)
                d_lat = d_scale * error
                d_z = s * (d_lat - jnp.sum(s * d_lat, axis=1, keepdims=True))
                zt[part, lanes] = s.reshape(PART, LANES)
                b2_acc[part, :] += d_z.reshape(PART, LANES)
                target[
                    aligned(row + step * PART, PART), aligned(col + lane * LANES, LANES)
                ] = d_z.reshape(PART, LANES).astype(BF16)

        for side in range(2):
            lat_stage[slot, side, rows, :] = zt[pl.ds(side * share, share), :].astype(BF16).T

    def lat_copies(slot, tile):
        device = across if slot == 0 else mine
        rows = aligned(tile * TILE, TILE)
        out_rows = lat_out.at[aligned(device * own_rows + tile * TILE, TILE), :]
        index = slot * n_tiles + tile
        local = pltpu.make_async_copy(
            lat_stage.at[slot, half, rows, :], out_rows, l_local.at[index]
        )
        remote = pltpu.make_async_remote_copy(
            src_ref=lat_stage.at[slot, 1 - half, rows, :],
            dst_ref=out_rows,
            send_sem=l_send.at[index],
            recv_sem=l_recv.at[index],
            device_id={"mp": near},
            device_id_type=MESH,
        )
        return local, remote

    def dpl_copy(tile):
        cols = aligned(tile * TILE, TILE)
        return pltpu.make_async_remote_copy(
            src_ref=dpl_send.at[:, cols],
            dst_ref=dpl.at[aligned(pair * chip_cols, chip_cols), cols],
            send_sem=d_send.at[tile],
            recv_sem=d_recv.at[tile],
            device_id={"mp": across},
            device_id_type=MESH,
        )

    def grad_copies(tile):
        rows = aligned(tile * TILE, TILE)
        out_rows = grad_out.at[aligned(mine * own_rows + tile * TILE, TILE), :]
        remotes = []
        for flip in (2, 3, 1):
            peer = peer_of(flip)
            remotes.append(
                pltpu.make_async_remote_copy(
                    src_ref=lg_stage.at[peer, rows, :],
                    dst_ref=out_rows,
                    send_sem=g_send.at[flip - 1, tile],
                    recv_sem=g_recv.at[flip - 1, tile],
                    device_id={"mp": peer},
                    device_id_type=MESH,
                )
            )
        local = pltpu.make_async_copy(lg_stage.at[mine, rows, :], out_rows, g_local.at[tile])
        return local, remotes

    prepare(0)
    loads[2].wait()
    next_copy(0).wait_recv()

    @pl.loop(0, n_tiles)
    def _(tile):
        forward(0, aligned(tile * TILE, TILE), False)

        @pl.when(tile == 0)
        def _():
            gathered(w_needs[0][2:])

        simnorm(0, tile, dpl_send, 0, tile * TILE)
        dpl_copy(tile).start()
        local, remote = lat_copies(0, tile)
        local.start()
        remote.start()

    loads[3].wait()
    next_copy(1).wait_recv()

    @pl.loop(0, n_tiles)
    def _(tile):
        cols = aligned(tile * TILE, TILE)
        forward(0, aligned(own_rows + tile * TILE, TILE), True)
        simnorm(1, tile, dpl, pair * chip_cols, tile * TILE)
        local, remote = lat_copies(1, tile)
        local.start()
        remote.start()
        dpl_copy(tile).wait_recv()
        d_lat = dpl[:, cols]
        g2t[...] += dot(d_lat, hid[...])
        dh[...] = dot(d_lat, w2_t[...], 0, 0)
        backward(0, d_dyn, tile * TILE)
        g1[:, pl.ds(0, hid_width)] += dot(x_t[:, cols], d_dyn[cols, :])

    def add_into(target, others, n_rows):
        step_rows = next(size for size in (128, 96, 80, 64, 48, 32, 16) if n_rows % size == 0)

        @pl.loop(0, n_rows // step_rows)
        def _(step):
            rows = aligned(step * step_rows, step_rows)
            total = target[rows, :].astype(F32)
            for other in others:
                total = total + other[rows, :].astype(F32)
            target[rows, :] = total.astype(BF16)

    def reduction(key, part, got, fin, order, with_sums):
        n_rows = part.shape[2]
        stages, gathers = [], []
        offset, length, spot, both = 0, n_rows, n_rows, True

        def sides(rows, where, other_side):
            if both:
                return part.at[half, :, rows, :], got.at[:, where, :]
            return part.at[half, other_side, rows, :], got.at[0, where, :]

        def adds(rows, wheres, count):
            if both:
                return [
                    (part.at[half, k, rows, :], [got.at[k, where, :] for where in wheres], count)
                    for k in range(2)
                ]
            return [(part.at[half, pair, rows, :], [got.at[0, w, :] for w in wheres], count)]

        for what in order:
            if what == "near":
                where = pl.ds(0, n_rows)
                copies = [(part.at[1 - half], got.at[:, where, :], {"mp": near})]
                stages.append((copies, adds(pl.ds(0, n_rows), [where], n_rows), None, half))
                continue
            if what == "across":
                both = False
                rows, where = aligned_to(offset, length), pl.ds(spot, length)
                source, target = sides(rows, where, 1 - pair)
                copies = [(source, target, {"mp": across})]
                stages.append((copies, adds(rows, [where], length), None, pair))
                spot += length
                continue
            if length % (16 << len(what)) == 0:
                parts = [what]
            else:
                parts = [(bit,) for bit in what]
            for group in parts:
                whole = length % (16 << len(group)) != 0
                if not whole:
                    length >>= len(group)
                mine_at = 0 if whole else place_in(group, 0) * length
                copies, wheres = [], []
                for flip in flips(group):
                    at = 0 if whole else place_in(group, flip) * length
                    where = pl.ds(spot, length)
                    spot += length
                    source, target = sides(aligned_to(offset + at, length), where, pair)
                    copies.append((source, target, {"dp": column_peer(mask_of(group, flip))}))
                    wheres.append(where)
                keep = aligned_to(offset + mine_at, length)
                kind = "whole" if whole else None
                stages.append((copies, adds(keep, wheres, length), kind, place_in(group, 0)))
                if not whole:
                    gathers.append((group, offset + mine_at, length))
                offset = offset + mine_at
        last = len(stages)
        final = aligned_to(offset, length)
        for group, start, count in gathers[::-1]:
            rows = aligned_to(start, count)
            copies = [
                (fin.at[rows, :], fin.at[rows, :], {"dp": column_peer(mask_of(group, flip))})
                for flip in flips(group)
            ]
            stages.append((copies, [], None, None))
        firsts = [sum(len(stage[0]) for stage in stages[:i]) for i in range(len(stages))]
        slots = [sum(len(stage[0]) + 1 for stage in stages[:i]) for i in range(last)]

        def copies_of(index):
            for number, (source, target, device) in enumerate(stages[index][0]):
                at = firsts[index] + number
                yield pltpu.make_async_remote_copy(
                    src_ref=source,
                    dst_ref=target,
                    send_sem=r_send.at[key, at],
                    recv_sem=r_recv.at[key, at],
                    device_id=device,
                    device_id_type=MESH,
                )

        def sums_copies(index):
            if with_sums and index < last:
                for number, (_, _, device) in enumerate(stages[index][0]):
                    at = firsts[index] + number
                    yield pltpu.make_async_remote_copy(
                        src_ref=sums.at[index],
                        dst_ref=got_sums.at[slots[index] + stages[index][3]],
                        send_sem=s_send.at[at],
                        recv_sem=s_recv.at[at],
                        device_id=device,
                        device_id_type=MESH,
                    )

        def start(index):
            for copy in copies_of(index):
                copy.start()
            for copy in sums_copies(index):
                copy.start()

        def finish(index):
            for copy in copies_of(index):
                if stages[index][2] == "whole":
                    copy.wait_send()
                copy.wait_recv()
            for copy in sums_copies(index):
                copy.wait_recv()
            if with_sums and index < last:
                got_sums[slots[index] + stages[index][3]] = sums[index]
                total = got_sums[slots[index]]
                for other in range(len(stages[index][0])):
                    total = total + got_sums[slots[index] + 1 + other]
                sums[index + 1] = total
            for target, others, count in stages[index][1]:
                add_into(target, others, count)
            if index + 1 == last:
                fin[final, :] = part[half, pair, final, :]
            if index + 1 < len(stages):
                start(index + 1)

        def drain():
            for index, stage in enumerate(stages):
                if stage[2] != "whole":
                    for copy in copies_of(index):
                        copy.wait_send()
                for copy in sums_copies(index):
                    copy.wait_send()

        return start, finish, drain, len(stages), last

    def fill(part, net, first, count, source, base):
        for device in range(n_mp):
            cols = pl.ds(net * hid_width + device * shard, shard)
            part[device % 2, device // 2, pl.ds(first, count), :] = source[
                pl.ds(base, count), cols
            ].astype(BF16)

    def add_columns(net):
        cols = pl.ds(net * hid_width, hid_width)
        for line in range(2):
            g1[pl.ds(lat_width + n_task + 8 + line, 1), cols] = jnp.sum(
                col_acc[pl.ds(8 * line, 8), cols], axis=0, keepdims=True
            )

    def order_of(kind):
        if kind == 0:
            return ["near", "across"] + groups
        if kind == 1 or len(groups) < 2:
            return ["near"] + groups[:1] + ["across"] + groups[1:]
        return ["near", groups[1], "across", groups[0]] + groups[2:]

    split = part_b.shape[2]
    add_columns(0)
    fill(part_a, 0, 0, lat_width, g2t, 0)
    fill(part_b, 0, 0, split, g1, 0)
    fill(part_c, 0, 0, in_rows - split, g1, split)
    dyn_places = (
        (part_a, got_a, in_rows, lat_width),
        (part_b, got_b, 0, split),
        (part_c, got_c, split, in_rows - split),
    )
    chunks = [
        reduction(k, part, got, fin_dyn.at[pl.ds(first, count), :], order_of(k), False)
        for k, (part, got, first, count) in enumerate(dyn_places)
    ]
    for chunk in chunks:
        chunk[0](0)
    per_tile = 4
    inside = sorted(
        (place, chunk, index)
        for chunk, places in enumerate(EVENTS)
        for index, place in enumerate(places)
        if index < chunks[chunk][3] and place < per_tile * n_tiles
    )

    prepare(1)
    gathered(w_needs[1][2:])

    for place, chunk, index in inside:
        if place < 0:
            chunks[chunk][1](index)

    def point(tile, number):
        for place, chunk, index in inside:
            if place >= 0 and place % per_tile == number:

                @pl.when(tile == place // per_tile)
                def _():
                    chunks[chunk][1](index)

    def kept(tile):
        return aligned(jnp.maximum(tile - (n_tiles - LATE - 1), 0) * TILE, TILE)

    def latent_grads(tile):
        cols = aligned(tile * TILE, TILE)
        lat_rows = pl.ds(0, lat_width)
        lg = dot(d_dyn[cols, :], w1_raw[lat_rows, pl.ds(0, hid_width)], 1, 1)
        lg = lg + dot(d_pre[kept(tile), :], w1_raw[lat_rows, pl.ds(hid_width, hid_width)], 1, 1)
        lg = (lg * total_rows).astype(BF16)
        for device in range(n_mp):
            lg_stage[device, cols, :] = lg[:, device * share : (device + 1) * share]

    def send_grads(tile):
        local, remotes = grad_copies(tile)
        local.start()
        for remote in remotes:
            remote.start()

    @pl.loop(0, n_tiles)
    def _(tile):
        cols = aligned(tile * TILE, TILE)
        forward(1, aligned(own_rows + tile * TILE, TILE), True)
        point(tile, 0)
        bins = bins_ref[:, aligned(mine * own_rows + tile * TILE, TILE)]
        frac = frac_ref[:, aligned(mine * own_rows + tile * TILE, TILE)]
        z = dot(rw2_t[...], hid[...], 1, 1)
        bias = rb2_ref[...]
        z = z + jnp.concatenate([bias] * (TILE // LANES), axis=1)
        z = z - jnp.max(z, axis=0, keepdims=True)
        e = jnp.exp(z)
        total = jnp.sum(e, axis=0, keepdims=True)
        row = lax.broadcasted_iota(jnp.int32, z.shape, 0)
        target = jnp.where(row == bins, 1.0 - frac, 0.0) + jnp.where(row == bins + 1, frac, 0.0)
        loss = jnp.sum(target * (jnp.log(total) - z), axis=0, keepdims=True)
        row_acc[...] += loss
        d_logits = (REW_COEF / total_rows) * (e * (1.0 / total) - target)
        dlog[...] = d_logits.astype(BF16)
        sum_acc[pl.ds(8, 8), :] += dot(jnp.ones((8, TILE), BF16), dlog[...], 1, 1)
        rg2t[...] += dot(dlog[...], hid[...])
        dh[...] = dot(dlog[...], rw2_t[...], 0, 0)
        point(tile, 1)
        backward(1, d_pre, jnp.maximum(tile - (n_tiles - LATE - 1), 0) * TILE)
        point(tile, 2)
        g1[:, pl.ds(hid_width, hid_width)] += dot(x_t[:, cols], d_pre[kept(tile), :])

        if LATE < n_tiles:

            @pl.when(tile < n_tiles - LATE)
            def _():
                latent_grads(tile)

        point(tile, 3)

        if LATE < n_tiles:

            @pl.when(tile < n_tiles - LATE)
            def _():
                send_grads(tile)


    add_columns(1)
    third = part_rew.shape[3]
    for k in range(3):
        rest = min(third, in_rows - k * third)
        for device in range(n_mp):
            cols = pl.ds(hid_width + device * shard, shard)
            where = (k, device % 2, device // 2)
            part_rew[where + (pl.ds(0, rest),)] = g1[pl.ds(k * third, rest), cols].astype(BF16)
            if rest < third:
                block = pl.ds(device * shard, shard)
                part_rew[where + (pl.ds(rest, LANES),)] = rg2t[:, block].astype(BF16)
    tasks = g1[pl.ds(lat_width, n_task), :]
    table = split_dot(tasks, w1_raw[pl.ds(lat_width, n_rest), :], 1, 1).astype(BF16)
    spare = in_rows - 2 * third - 32
    for device in range(n_mp):
        where = (2, device % 2, device // 2)
        part_rew[where + (pl.ds(spare, 32), pl.ds(0, n_rest))] = table[0:32]
        part_rew[where + (pl.ds(spare, 32), pl.ds(LANES, n_rest))] = table[32:64]
        part_rew[where + (pl.ds(third - 16, 16), pl.ds(0, n_rest))] = table[64:80]
    sums[0] = jnp.zeros(sums.shape[1:], F32)
    sums[0, pl.ds(0, 1), aligned(pair * chip_cols, chip_cols)] = jnp.sum(
        b2_acc[...].T, axis=0, keepdims=True
    )
    sums[0, pl.ds(1, 1), pl.ds(0, LANES)] = sum_acc[pl.ds(8, 1), :]
    cons = jnp.sum(sum_acc[pl.ds(0, 8), :])
    rew = jnp.sum(row_acc[...])
    sums[0, pl.ds(2, 1), :] = jnp.full((1, lat_width), cons)
    sums[0, pl.ds(3, 1), :] = jnp.full((1, lat_width), rew)
    for k in range(3):
        chunks.append(
            reduction(
                3 + k,
                part_rew.at[k],
                got_rew.at[k],
                fin_rew.at[pl.ds(k * third, third), :],
                order_of(k),
                k == 0,
            )
        )
    for chunk in chunks[3:]:
        chunk[0](0)
    done = [(chunk, index) for _, chunk, index in inside]
    left = [(index, c) for c in range(3) for index in range(chunks[c][3]) if (c, index) not in done]
    base = min([index for index, _ in left], default=0)
    left = [(index - base, c, index) for index, c in left]
    left += [(index, c, index) for c in range(3, 6) for index in range(chunks[c][3])]
    late = [n_tiles - LATE + k for k in range(LATE)]
    for tile in late[:1]:
        latent_grads(tile)
    step = 0
    for when, chunk, index in sorted(left):
        if when > step:
            step = when
            for tile in late[step - 1 : step]:
                send_grads(tile)
            for tile in late[step : step + 1]:
                latent_grads(tile)
        chunks[chunk][1](index)
    fin_sums[...] = sums[chunks[3][4]]
    for chunk in chunks:
        chunk[2]()

    for index in range(6):
        for kind in range(3):
            weight_copy(index, kind).wait_send()
    for slot in range(2):
        next_copy(slot).wait_send()

        @pl.loop(0, n_tiles)
        def _(tile):
            local, remote = lat_copies(slot, tile)
            local.wait()
            remote.wait()

    @pl.loop(0, n_tiles)
    def _(tile):
        dpl_copy(tile).wait_send()
        local, remotes = grad_copies(tile)
        local.wait()
        for remote in remotes:
            remote.wait()


def finish_kernel(
    lat_in,
    grad_in,
    dyn_in,
    rew_in,
    sums_in,
    embed,
    lat_out,
    grad_out,
    losses,
    grad_embed,
    dyn_w1,
    dyn_b1,
    dyn_gain,
    dyn_shift,
    rew_w1,
    rew_b1,
    rew_gain,
    rew_shift,
    dyn_w2,
    dyn_b2,
    rew_w2,
    rew_b2,
    dyn,
    rew,
    sums,
    stage,
    sems,
    *,
    total_rows,
    lat_width,
):
    n_big = stage.shape[1]
    copies = [
        pltpu.make_async_copy(source, target, sems.at[i])
        for i, (source, target) in enumerate(((dyn_in, dyn), (rew_in, rew), (sums_in, sums)))
    ]
    rows = stage.shape[2]
    outs = []
    for k in range(n_big):
        part = pl.ds(k * rows, rows)
        for side, (source, target) in enumerate(((lat_in, lat_out), (grad_in, grad_out))):
            first, last = sems.at[3 + 4 * k + 2 * side], sems.at[4 + 4 * k + 2 * side]
            copies.append(
                pltpu.make_async_copy(source.at[part, :], stage.at[side, k], first)
            )
            outs.append(pltpu.make_async_copy(stage.at[side, k], target.at[part, :], last))
    for copy in copies:
        copy.start()
    for copy, out in zip(copies[3:], outs):
        copy.wait()
        out.start()
    for copy in copies[:3]:
        copy.wait()
    n_task, n_embed = embed.shape
    n_rest = dyn_w1.shape[0] - lat_width
    n_act = n_rest - n_embed
    in_rows = lat_width + LANES
    first = lat_width + n_task
    moved = lax.broadcasted_iota(jnp.int32, (n_embed, n_rest), 1) == (
        lax.broadcasted_iota(jnp.int32, (n_embed, n_rest), 0) + n_act
    )
    moved = jnp.where(moved, 1.0, 0.0).astype(BF16)
    line = lax.broadcasted_iota(jnp.int32, (LANES - n_task, n_rest), 0)
    lane = lax.broadcasted_iota(jnp.int32, (LANES - n_task, n_rest), 1)
    acts = jnp.where((line == lane) & (line < n_act), 1.0, 0.0).astype(BF16)
    mix = jnp.concatenate([dot(embed[...], moved).astype(BF16), acts], axis=0)
    for net, w1, b1, gain, shift in (
        (dyn, dyn_w1, dyn_b1, dyn_gain, dyn_shift),
        (rew, rew_w1, rew_b1, rew_gain, rew_shift),
    ):
        w1[pl.ds(0, lat_width), :] = net[pl.ds(0, lat_width), :].astype(F32)
        w1[pl.ds(lat_width, n_rest), :] = dot(mix, net[pl.ds(lat_width, LANES), :], 0, 0)
        small = net[pl.ds(first, 16), :].astype(F32)
        b1[...] = small[n_act : n_act + 1]
        gain[...] = small[8:9]
        shift[...] = small[9:10]
    dyn_w2[...] = dyn[pl.ds(in_rows, lat_width), :].astype(F32).T
    n_bins = rew_w2.shape[0]
    rew_w2[...] = rew[pl.ds(in_rows, LANES), :].astype(F32)[:n_bins]
    dyn_b2[...] = sums[pl.ds(0, 1), :]
    rew_b2[...] = sums[pl.ds(1, 1), pl.ds(0, n_bins)]
    pieces = (
        (0, 32, in_rows - 32, 0),
        (32, 32, in_rows - 32, LANES),
        (64, n_task - 64, in_rows + LANES - 16, 0),
    )
    for to, count, row, col in pieces:
        grad_embed[pl.ds(to, count), :] = dot(
            rew[pl.ds(row, count), pl.ds(col, n_rest)], moved, 1, 1
        )
    pick = lax.broadcasted_iota(jnp.int32, losses.shape, 1) == 0
    both = jnp.where(pick, sums[pl.ds(2, 1), pl.ds(0, 2)], sums[pl.ds(3, 1), pl.ds(0, 2)])
    losses[...] = both * (1.0 / total_rows)
    for out in outs:
        out.wait()


def run_finish(total_rows, lat_width, n_in, n_bins, lat, grad, dyn, rew, sums, embed):
    shape = jax.ShapeDtypeStruct
    shard = dyn.shape[1]
    line = shape((1, shard), F32)
    first = [shape((n_in, shard), F32), line, line, line]
    any_spec = pl.BlockSpec(memory_space=pl.ANY)
    vmem_spec = pl.BlockSpec(memory_space=pltpu.VMEM)
    return pl.pallas_call(
        functools.partial(finish_kernel, total_rows=total_rows, lat_width=lat_width),
        out_shape=(
            shape(lat.shape, BF16),
            shape(grad.shape, BF16),
            shape((1, 2), F32),
            shape(embed.shape, F32),
            *first,
            *first,
            shape((shard, lat_width), F32),
            shape((1, lat_width), F32),
            shape((n_bins, shard), F32),
            shape((1, n_bins), F32),
        ),
        in_specs=[any_spec] * 5 + [vmem_spec],
        out_specs=[any_spec] * 2 + [vmem_spec] * 14,
        scratch_shapes=[
            pltpu.VMEM(dyn.shape, BF16),
            pltpu.VMEM(rew.shape, BF16),
            pltpu.VMEM(sums.shape, F32),
            pltpu.VMEM((2, PIECES, lat.shape[0] // PIECES, lat.shape[1]), BF16),
            pltpu.SemaphoreType.DMA((3 + 4 * PIECES,)),
        ],
        compiler_params=pltpu.CompilerParams(vmem_limit_bytes=60 << 20),
    )(lat, grad, dyn, rew, sums, embed)


def run_main(n_mp, n_dp, total_rows, args):
    latent, next_latent, w1, dyn_w2, rew_w2 = args[0], args[1], args[2], args[4], args[5]
    tok_rows, lat_width = latent.shape
    share = next_latent.shape[1]
    n_in, shard = w1.shape
    hid_width = n_mp * shard
    own = tok_rows // n_mp
    in_rows = lat_width + LANES
    n_tiles = own // TILE
    n_task = args[17].shape[0]
    any_spec = pl.BlockSpec(memory_space=pl.ANY)
    vmem_spec = pl.BlockSpec(memory_space=pltpu.VMEM)
    shape = jax.ShapeDtypeStruct
    dma = pltpu.SemaphoreType.DMA
    n_bits = n_dp.bit_length() - 1
    n_copies = 2 + 2 * sum(len(flips(group)) for group in column_groups(n_bits))
    third = (in_rows + LANES) // 3
    split = 3 * in_rows // 5
    return pl.pallas_call(
        functools.partial(main_kernel, (n_mp, n_dp, total_rows, hid_width)),
        out_shape=(
            shape((tok_rows, share), BF16),
            shape((tok_rows, share), BF16),
            shape((in_rows + lat_width, shard), BF16),
            shape((3 * third, shard), BF16),
            shape((8, lat_width), F32),
        ),
        in_specs=[any_spec] * 4 + [vmem_spec] * 16,
        out_specs=[any_spec] * 2 + [vmem_spec] * 3,
        scratch_shapes=[
            pltpu.VMEM((2 * own, in_rows), BF16),
            pltpu.VMEM((in_rows, own), BF16),
            pltpu.VMEM((n_in, 2 * hid_width), BF16),
            pltpu.VMEM((in_rows, 2 * hid_width), BF16),
            pltpu.VMEM((lat_width, hid_width), BF16),
            pltpu.VMEM((LANES, hid_width), BF16),
            pltpu.VMEM((8, 2 * hid_width), F32),
            pltpu.VMEM((lat_width, shard), BF16),
            pltpu.VMEM((LANES, shard), BF16),
            pltpu.VMEM((2, 8, shard), F32),
            pltpu.VMEM((n_task, n_in - lat_width), BF16),
            pltpu.VMEM((16, TILE), F32),
            pltpu.VMEM((lat_width, LANES), F32),
            pltpu.VMEM((LANES, LANES), F32),
            pltpu.VMEM((2, 2, own, share), BF16),
            pltpu.VMEM((lat_width, own), BF16),
            pltpu.VMEM((2 * share, own), BF16),
            pltpu.VMEM((2, 2, own, share), BF16),
            pltpu.VMEM((n_mp, own, share), BF16),
            pltpu.VMEM((own, hid_width), BF16),
            pltpu.VMEM((2, 2, lat_width, shard), BF16),
            pltpu.VMEM((2, 2, split, shard), BF16),
            pltpu.VMEM((2, 2, in_rows - split, shard), BF16),
            pltpu.VMEM((3, 2, 2, third, shard), BF16),
            pltpu.VMEM((2, room(lat_width, n_bits), shard), BF16),
            pltpu.VMEM((2, room(split, n_bits), shard), BF16),
            pltpu.VMEM((2, room(in_rows - split, n_bits), shard), BF16),
            pltpu.VMEM((3, 2, room(third, n_bits), shard), BF16),
            pltpu.VMEM((3 + n_bits, 8, lat_width), F32),
            pltpu.VMEM((4 + 2 * n_bits, 8, lat_width), F32),
            pltpu.VMEM((in_rows, 2 * hid_width), F32),
            pltpu.VMEM((lat_width, hid_width), F32),
            pltpu.VMEM((LANES, hid_width), F32),
            pltpu.VMEM((TILE, hid_width), F32),
            pltpu.VMEM((TILE, hid_width), F32),
            pltpu.VMEM((TILE, hid_width), F32),
            pltpu.VMEM((TILE, hid_width), BF16),
            pltpu.VMEM(((LATE + 1) * TILE, hid_width), BF16),
            pltpu.VMEM((2 * share, TILE), F32),
            pltpu.VMEM((2 * share, TILE), F32),
            pltpu.VMEM((LANES, TILE), BF16),
            pltpu.VMEM((TILE, LANES), F32),
            pltpu.VMEM((16, 2 * hid_width), F32),
            pltpu.VMEM((16, LANES), F32),
            pltpu.VMEM((1, TILE), F32),
            pltpu.VMEM((2 * share, LANES), F32),
            dma((10,)),
            dma((3, 6)),
            dma((3, 6)),
            dma((2,)),
            dma((2,)),
            dma((n_tiles,)),
            dma((n_tiles,)),
            dma((2 * n_tiles,)),
            dma((2 * n_tiles,)),
            dma((2 * n_tiles,)),
            dma((n_tiles,)),
            dma((3, n_tiles)),
            dma((3, n_tiles)),
            dma((6, n_copies)),
            dma((6, n_copies)),
            dma((n_copies,)),
            dma((n_copies,)),
        ],
        compiler_params=pltpu.CompilerParams(
            collective_id=0, has_side_effects=True, vmem_limit_bytes=60 << 20
        ),
    )(*args)


def on_device(
    latent,
    actions,
    task_ids,
    action_masks,
    next_latent,
    reward_bins,
    reward_frac,
    task_embed,
    dyn_w1,
    dyn_b1,
    dyn_gain,
    dyn_shift,
    rew_w1,
    rew_b1,
    rew_gain,
    rew_shift,
    dyn_w2,
    dyn_b2,
    rew_w2,
    rew_b2,
):
    n_mp, n_dp = lax.axis_size("mp"), lax.axis_size("dp")
    tok_rows, lat_width = latent.shape
    total_rows = tok_rows * n_dp

    def row(vector):
        return vector.reshape(1, -1)

    args = (
        latent,
        next_latent,
        dyn_w1,
        rew_w1,
        dyn_w2,
        rew_w2.T,
        *(row(v) for v in (dyn_b1, dyn_gain, dyn_shift, rew_b1, rew_gain, rew_shift)),
        row(task_ids),
        actions,
        action_masks.T,
        row(reward_bins),
        row(reward_frac),
        task_embed,
        row(dyn_b2),
        row(rew_b2),
    )
    latents, latent_grad, dyn, rew, sums = run_main(n_mp, n_dp, total_rows, args)
    n_bins = rew_b2.shape[0]
    n_in = dyn_w1.shape[0]
    outs = run_finish(
        total_rows, lat_width, n_in, n_bins, latents, latent_grad, dyn, rew, sums, task_embed
    )
    outs = [out.reshape(-1) if out.shape[0] == 1 else out for out in outs]
    outs[14] = outs[14].T
    return tuple(outs)


def solution(mesh):
    return jax.shard_map(
        on_device,
        mesh=mesh,
        in_specs=(
            P("dp", None),
            P(None, "dp"),
            P("dp"),
            P(),
            P("dp", "mp"),
            P("dp"),
            P("dp"),
            P(),
            P(None, "mp"),
            P("mp"),
            P("mp"),
            P("mp"),
            P(None, "mp"),
            P("mp"),
            P("mp"),
            P("mp"),
            P("mp", None),
            P(),
            P("mp", None),
            P(),
        ),
        out_specs=(
            P("dp", "mp"),
            P("dp", "mp"),
            P(),
            P(),
            P(None, "mp"),
            P("mp"),
            P("mp"),
            P("mp"),
            P(None, "mp"),
            P("mp"),
            P("mp"),
            P("mp"),
            P("mp", None),
            P(),
            P("mp", None),
            P(),
        ),
        check_vma=False,
    )
```

```python
import functools

import jax
import jax.numpy as jnp
from jax import lax
from jax.experimental import pallas as pl
from jax.experimental.pallas import tpu as pltpu
from jax.sharding import PartitionSpec as P

GROUP = 8
CONS_COEF = 20.0
REW_COEF = 0.1
EPS = 1e-05
LANES = 128
TILE = 512
SUB = 128
PART = 64
LATE = 1
PIECES = 2
EVENTS = ((-1, 6, 10, 13, 99, 99), (0, 5, 9, 12, 15, 99), (0, 4, 9, 11, 13, 99))
MESH = pl.DeviceIdType.MESH
F32 = jnp.float32
BF16 = jnp.bfloat16


def dot(left, right, left_dim=1, right_dim=0):
    return lax.dot_general(
        left, right, (((left_dim,), (right_dim,)), ((), ())), preferred_element_type=F32
    )


def aligned(start, size):
    return pl.ds(pl.multiple_of(start, size), size)


def aligned_to(start, size):
    return pl.ds(pl.multiple_of(start, 16), size)


def column_groups(n_bits):
    groups = [group for group in ((0,), (1, 2)) if group[-1] < n_bits]
    return groups + [(bit,) for bit in range(sum(map(len, groups)), n_bits)]


def flips(group):
    return range(1, 1 << len(group))


def mask_of(group, flip):
    return sum(1 << bit for at, bit in enumerate(group) if flip >> at & 1)


def group_masks(group):
    return [mask_of(group, flip) for flip in flips(group)] + [1 << bit for bit in group]


def room(n_rows, n_bits):
    extra, length = 2 * n_rows, n_rows
    for group in column_groups(n_bits):
        if length % (16 << len(group)) == 0:
            length >>= len(group)
            extra += length * ((1 << len(group)) - 1)
        else:
            for _ in group:
                length = length // 2 if length % 32 == 0 else length
                extra += length
    return extra


def split_dot(left, right, left_dim, right_dim):
    high = left.astype(BF16)
    low = (left - high.astype(F32)).astype(BF16)
    return dot(high, right, left_dim, right_dim) + dot(low, right, left_dim, right_dim)


def main_kernel(
    sizes,
    latent_in,
    next_in,
    dyn_w1,
    rew_w1,
    dyn_w2,
    rew_w2,
    dyn_b1,
    dyn_gain,
    dyn_shift,
    rew_b1,
    rew_gain,
    rew_shift,
    ids_ref,
    act_ref,
    masks_ref,
    bins_ref,
    frac_ref,
    embed_ref,
    dyn_b2,
    rew_b2,
    lat_out,
    grad_out,
    fin_dyn,
    fin_rew,
    fin_sums,
    x_all,
    x_t,
    w1_raw,
    w1_c,
    w2_t,
    rw2_t,
    w2_g,
    rw2_g,
    vecs,
    w2_own,
    rw2_own,
    vecs_own,
    embed_wide,
    extra_rows,
    b2_ref,
    rb2_ref,
    next_lat,
    dpl,
    dpl_send,
    lat_stage,
    lg_stage,
    d_dyn,
    part_a,
    part_b,
    part_c,
    part_rew,
    got_a,
    got_b,
    got_c,
    got_rew,
    sums,
    got_sums,
    g1,
    g2t,
    rg2t,
    pre,
    dh,
    dm,
    hid,
    d_pre,
    zt,
    latt,
    dlog,
    inv_ref,
    col_acc,
    sum_acc,
    row_acc,
    b2_acc,
    load_sem,
    w_send,
    w_recv,
    n_send,
    n_recv,
    d_send,
    d_recv,
    l_local,
    l_send,
    l_recv,
    g_local,
    g_send,
    g_recv,
    r_send,
    r_recv,
    s_send,
    s_recv,
):
    n_mp, n_dp, total_rows, hid_width = sizes
    n_bits = n_dp.bit_length() - 1
    mine = lax.axis_index("mp")
    column = lax.axis_index("dp")
    pair = mine // 2
    half = mine % 2
    own_rows = x_all.shape[0] // 2
    lat_width = latent_in.shape[1]
    shard = dyn_w1.shape[1]
    n_act = act_ref.shape[0]
    in_rows = g1.shape[0]
    share = next_in.shape[1]
    n_task = embed_ref.shape[0]
    chip_cols = 2 * share
    n_tiles = own_rows // TILE
    n_lane = hid_width // LANES

    def peer_of(flip):
        near = mine + 1 - 2 * half
        if flip == 1:
            return near
        across = 2 * (1 - pair)
        return across + half if flip == 2 else across + 1 - half

    def bit_of(bit):
        return (column // (1 << bit)) % 2

    def column_peer(mask):
        peer = column
        for bit in range(n_bits):
            if mask >> bit & 1:
                peer = peer + (1 - 2 * bit_of(bit)) * (1 << bit)
        return peer

    groups = column_groups(n_bits)

    def place_in(group, flip):
        place = 0
        for at, bit in enumerate(group):
            here = 1 - bit_of(bit) if flip >> at & 1 else bit_of(bit)
            place = place + here * (1 << (len(group) - 1 - at))
        return place

    def rows_of(device):
        return aligned(device * own_rows, own_rows)

    barrier = pltpu.get_barrier_semaphore()
    for flip in (1, 2, 3):
        pl.semaphore_signal(
            barrier, inc=1, device_id={"mp": peer_of(flip)}, device_id_type=MESH
        )
    masks = sorted({mask for group in groups for mask in group_masks(group)})
    for mask in masks:
        pl.semaphore_signal(
            barrier, inc=1, device_id={"dp": column_peer(mask)}, device_id_type=MESH
        )

    vecs_own[...] = jnp.zeros_like(vecs_own)
    for net, rows in enumerate(((dyn_b1, dyn_gain, dyn_shift), (rew_b1, rew_gain, rew_shift))):
        for line, ref in enumerate(rows):
            vecs_own[net, pl.ds(line, 1), :] = ref[...]
    w2_own[...] = dyn_w2[...].T
    n_bins = rew_w2.shape[0]
    rw2_own[...] = jnp.zeros_like(rw2_own)
    rw2_own[pl.ds(0, n_bins), :] = rew_w2[...]

    near, across = peer_of(1), peer_of(2)

    def w_pairs(block, rows_first):
        pairs = []
        for net in range(2):
            cols = aligned(net * hid_width + block * shard, shard)
            pairs.append(((dyn_w1, rew_w1)[net], w1_raw.at[:, cols]))
            pairs.append((vecs_own.at[net], vecs.at[:, cols]))
        cols = aligned(block * shard, shard)
        for side in (rows_first, 1 - rows_first):
            rows = aligned(side * chip_cols, chip_cols)
            pairs.append((w2_own.at[rows, :], w2_t.at[rows, cols]))
        pairs.append((rw2_own, rw2_t.at[:, cols]))
        return pairs

    w_needs = ((1, 0, 4, 5), (3, 2, 6))
    n_weights = 7

    def weight_copy(index, kind):
        source, target = w_pairs(mine, 1 - pair if kind == 1 else pair)[index]
        if kind == 2:
            source = target = w_pairs(across, pair)[index][1]
        return pltpu.make_async_remote_copy(
            src_ref=source,
            dst_ref=target,
            send_sem=w_send.at[kind, index],
            recv_sem=w_recv.at[kind, index],
            device_id={"mp": across if kind == 1 else near},
            device_id_type=MESH,
        )

    def next_copy(slot):
        rows = near if slot == 1 else peer_of(3)
        return pltpu.make_async_remote_copy(
            src_ref=next_in.at[rows_of(rows), :],
            dst_ref=next_lat.at[slot, half],
            send_sem=n_send.at[slot],
            recv_sem=n_recv.at[slot],
            device_id={"mp": near},
            device_id_type=MESH,
        )

    loads = []
    for slot, device in ((0, across), (1, mine)):
        loads.append(
            (
                latent_in.at[rows_of(device), :],
                x_all.at[pl.ds(slot * own_rows, own_rows), pl.ds(0, lat_width)],
            )
        )
    for slot, device in ((0, across), (1, mine)):
        loads.append((next_in.at[rows_of(device), :], next_lat.at[slot, half]))
    loads += w_pairs(mine, pair)
    loads = [
        pltpu.make_async_copy(source, target, load_sem.at[i])
        for i, (source, target) in enumerate(loads)
    ]
    for copy in loads:
        copy.start()
    pl.semaphore_wait(barrier, 3 + len(masks))
    for index in w_needs[0] + w_needs[1]:
        weight_copy(index, 1).start()
        weight_copy(index, 0).start()
    next_copy(0).start()
    next_copy(1).start()

    for ref in (g1, g2t, rg2t, col_acc, sum_acc, row_acc, b2_acc):
        ref[...] = jnp.zeros_like(ref)

    line = lax.broadcasted_iota(jnp.int32, extra_rows.shape, 0)
    extra_rows[...] = jnp.where((line == n_act) | (line == n_act + 1), 1.0, 0.0)
    n_embed = embed_ref.shape[1]
    n_rest = n_act + n_embed
    moved = lax.broadcasted_iota(jnp.int32, (n_embed, n_rest), 1) == (
        lax.broadcasted_iota(jnp.int32, (n_embed, n_rest), 0) + n_act
    )
    embed_wide[...] = dot(embed_ref[...], jnp.where(moved, 1.0, 0.0).astype(BF16)).astype(BF16)
    b2_ref[...] = jnp.broadcast_to(dyn_b2[...], (LANES, lat_width)).T
    rb2_ref[...] = jnp.full(rb2_ref.shape, -1e30, F32)
    rb2_ref[:, pl.ds(0, n_bins)] = jnp.broadcast_to(rew_b2[...], (LANES, n_bins))
    rb2_ref[...] = rb2_ref[...].T

    for slot, device in ((0, across), (1, mine)):
        base = device * own_rows

        @pl.loop(0, n_tiles)
        def _(tile):
            lanes = aligned(base + tile * TILE, TILE)
            ids = ids_ref[:, lanes]
            tasks = lax.broadcasted_iota(jnp.int32, (n_task, TILE), 0)
            onehot = jnp.where(tasks == ids, 1.0, 0.0).astype(BF16)
            masks = dot(masks_ref[...].astype(F32).astype(BF16), onehot)
            extra_rows[pl.ds(0, n_act), :] = act_ref[:, lanes].astype(F32) * masks
            masked = extra_rows[...].astype(BF16)
            rest = LANES - n_task - masked.shape[0]
            extra = jnp.concatenate([onehot, masked, jnp.zeros((rest, TILE), BF16)], axis=0)
            rows = aligned(slot * own_rows + tile * TILE, TILE)
            x_all[rows, pl.ds(lat_width, LANES)] = extra.T
            if slot == 1:
                x_t[pl.ds(lat_width, LANES), aligned(tile * TILE, TILE)] = extra

    for copy in loads[:2]:
        copy.wait()

    @pl.loop(0, n_tiles)
    def _(tile):
        rows = aligned(own_rows + tile * TILE, TILE)
        x_t[pl.ds(0, lat_width), aligned(tile * TILE, TILE)] = x_all[
            rows, pl.ds(0, lat_width)
        ].T

    def centre(values):
        return values - jnp.sum(values, axis=1, keepdims=True) * (1.0 / hid_width)

    def gathered(indices):
        for index in indices:
            weight_copy(index, 1).wait_recv()
            weight_copy(index, 2).start()
        for index in indices:
            loads[4 + index].wait()
            weight_copy(index, 0).wait_recv()
            weight_copy(index, 2).wait_recv()

    def with_gain(weights, scaled, net):
        gain = vecs[pl.ds(1, 1), pl.ds(net * hid_width, hid_width)]

        @pl.loop(0, weights.shape[0] // PART)
        def _(step):
            rows = aligned(step * PART, PART)
            scaled[rows, :] = (weights[rows, :].astype(F32) * gain).astype(BF16)

    def prepare(net):
        gathered(w_needs[net][:2])
        cols = pl.ds(net * hid_width, hid_width)

        @pl.loop(0, lat_width // PART)
        def _(step):
            rows = aligned(step * PART, PART)
            w1_c[rows, cols] = centre(w1_raw[rows, cols].astype(F32)).astype(BF16)

        table = dot(embed_wide[...], w1_raw[pl.ds(lat_width, n_rest), cols])
        w1_c[pl.ds(lat_width, n_task), cols] = centre(table).astype(BF16)
        act = centre(w1_raw[pl.ds(lat_width, 16), cols].astype(F32))
        bias = centre(vecs[pl.ds(0, 1), cols])
        high = bias.astype(BF16).astype(F32)
        row = lax.broadcasted_iota(jnp.int32, act.shape, 0)
        act = jnp.where(row < n_act, act, 0.0)
        act = jnp.where(row == n_act, high, jnp.where(row == n_act + 1, bias - high, act))
        w1_c[pl.ds(lat_width + n_task, 16), cols] = act.astype(BF16)
        rest = LANES - n_task - 16
        w1_c[pl.ds(lat_width + n_task + 16, rest), cols] = jnp.zeros((rest, hid_width), BF16)

    def forward(net, rows, keep):
        cols = pl.ds(net * hid_width, hid_width)
        values = dot(x_all[rows, :], w1_c[:, cols])
        pre[...] = values
        square = jnp.sum(values * values, axis=1, keepdims=True)
        inv_ref[...] = jnp.broadcast_to(
            lax.rsqrt(square * (1.0 / hid_width) + EPS), (TILE, LANES)
        )

        @pl.loop(0, TILE // SUB)
        def _(step):
            part = aligned(step * SUB, SUB)
            inv = inv_ref[part, :]
            for lane in range(n_lane):
                lanes = pl.ds(lane * LANES, LANES)
                wide = pl.ds(net * hid_width + lane * LANES, LANES)
                xhat = pre[part, lanes] * inv
                y = xhat * vecs[pl.ds(1, 1), wide] + vecs[pl.ds(2, 1), wide]
                if keep:
                    pre[part, lanes] = xhat
                y = y.astype(BF16)
                e = jnp.exp(jnp.minimum(y, 20.0))
                e2 = e + 2.0
                r = 1.0 / (e * e2 + 2.0)
                u = e * r
                t = u * e2
                hid[part, lanes] = y * t
                if keep:
                    dm[part, lanes] = t + (4.0 * y) * (u * (r + u))

    def backward(net, target, first_row):
        @pl.loop(0, TILE // SUB)
        def _(step):
            part = aligned(step * SUB, SUB)
            first = jnp.zeros((SUB, LANES), F32)
            second = jnp.zeros((SUB, LANES), F32)
            for lane in range(n_lane):
                lanes = pl.ds(lane * LANES, LANES)
                wide = pl.ds(net * hid_width + lane * LANES, LANES)
                g = dh[part, lanes] * dm[part, lanes].astype(F32)
                scaled = g * pre[part, lanes]
                col_acc[pl.ds(0, 8), wide] += jnp.sum(
                    scaled.reshape(SUB // 8, 8, LANES), axis=0
                )
                col_acc[pl.ds(8, 8), wide] += jnp.sum(g.reshape(SUB // 8, 8, LANES), axis=0)
                first += g
                second += scaled
                dh[part, lanes] = g
            inv = inv_ref[part, :]
            first = jnp.broadcast_to(
                jnp.sum(first, axis=1, keepdims=True) * (1.0 / hid_width), (SUB, LANES)
            )
            second = jnp.broadcast_to(
                jnp.sum(second, axis=1, keepdims=True) * (1.0 / hid_width), (SUB, LANES)
            )
            first = first * inv
            second = second * inv
            for lane in range(n_lane):
                lanes = pl.ds(lane * LANES, LANES)
                value = dh[part, lanes] * inv - first - pre[part, lanes] * second
                target[aligned(first_row + step * SUB, SUB), lanes] = value.astype(BF16)

    d_scale = 2.0 * CONS_COEF / total_rows

    def simnorm(slot, tile, target, row, col):
        rows = aligned(tile * TILE, TILE)
        zt[...] = dot(w2_t[aligned(pair * chip_cols, chip_cols), :], hid[...], 1, 1)
        for side in range(2):
            latt[pl.ds(side * share, share), :] = next_lat[slot, side, rows, :].T.astype(F32)

        @pl.loop(0, chip_cols // PART)
        def _(step):
            part = aligned(step * PART, PART)
            bias = b2_ref[aligned(pair * chip_cols + step * PART, PART), :]
            for lane in range(TILE // LANES):
                lanes = pl.ds(lane * LANES, LANES)
                z = (zt[part, lanes] + bias).reshape(PART // GROUP, GROUP, LANES)
                e = jnp.exp(z - jnp.max(z, axis=1, keepdims=True))
                s = e * (1.0 / jnp.sum(e, axis=1, keepdims=True))
                error = s - latt[part, lanes].reshape(z.shape)
                sum_acc[pl.ds(0, 8), :] += jnp.sum(error * error, axis=0)
                d_lat = d_scale * error
                d_z = s * (d_lat - jnp.sum(s * d_lat, axis=1, keepdims=True))
                zt[part, lanes] = s.reshape(PART, LANES)
                b2_acc[part, :] += d_z.reshape(PART, LANES)
                target[
                    aligned(row + step * PART, PART), aligned(col + lane * LANES, LANES)
                ] = d_z.reshape(PART, LANES).astype(BF16)

        for side in range(2):
            lat_stage[slot, side, rows, :] = zt[pl.ds(side * share, share), :].astype(BF16).T

    def lat_copies(slot, tile):
        device = across if slot == 0 else mine
        rows = aligned(tile * TILE, TILE)
        out_rows = lat_out.at[aligned(device * own_rows + tile * TILE, TILE), :]
        index = slot * n_tiles + tile
        local = pltpu.make_async_copy(
            lat_stage.at[slot, half, rows, :], out_rows, l_local.at[index]
        )
        remote = pltpu.make_async_remote_copy(
            src_ref=lat_stage.at[slot, 1 - half, rows, :],
            dst_ref=out_rows,
            send_sem=l_send.at[index],
            recv_sem=l_recv.at[index],
            device_id={"mp": near},
            device_id_type=MESH,
        )
        return local, remote

    def dpl_copy(tile):
        cols = aligned(tile * TILE, TILE)
        return pltpu.make_async_remote_copy(
            src_ref=dpl_send.at[:, cols],
            dst_ref=dpl.at[aligned(pair * chip_cols, chip_cols), cols],
            send_sem=d_send.at[tile],
            recv_sem=d_recv.at[tile],
            device_id={"mp": across},
            device_id_type=MESH,
        )

    def grad_copies(tile):
        rows = aligned(tile * TILE, TILE)
        out_rows = grad_out.at[aligned(mine * own_rows + tile * TILE, TILE), :]
        remotes = []
        for flip in (2, 3, 1):
            peer = peer_of(flip)
            remotes.append(
                pltpu.make_async_remote_copy(
                    src_ref=lg_stage.at[peer, rows, :],
                    dst_ref=out_rows,
                    send_sem=g_send.at[flip - 1, tile],
                    recv_sem=g_recv.at[flip - 1, tile],
                    device_id={"mp": peer},
                    device_id_type=MESH,
                )
            )
        local = pltpu.make_async_copy(lg_stage.at[mine, rows, :], out_rows, g_local.at[tile])
        return local, remotes

    prepare(0)
    loads[2].wait()
    next_copy(0).wait_recv()

    @pl.loop(0, n_tiles)
    def _(tile):
        forward(0, aligned(tile * TILE, TILE), False)

        @pl.when(tile == 0)
        def _():
            gathered(w_needs[0][2:3])

        simnorm(0, tile, dpl_send, 0, tile * TILE)
        dpl_copy(tile).start()
        local, remote = lat_copies(0, tile)
        local.start()
        remote.start()

    gathered(w_needs[0][3:])
    with_gain(w2_t, w2_g, 0)
    loads[3].wait()
    next_copy(1).wait_recv()

    @pl.loop(0, n_tiles)
    def _(tile):
        cols = aligned(tile * TILE, TILE)
        forward(0, aligned(own_rows + tile * TILE, TILE), True)
        simnorm(1, tile, dpl, pair * chip_cols, tile * TILE)
        local, remote = lat_copies(1, tile)
        local.start()
        remote.start()
        dpl_copy(tile).wait_recv()
        d_lat = dpl[:, cols]
        g2t[...] += dot(d_lat, hid[...])
        dh[...] = dot(d_lat, w2_g[...], 0, 0)
        backward(0, d_dyn, tile * TILE)
        g1[:, pl.ds(0, hid_width)] += dot(x_t[:, cols], d_dyn[cols, :])

    def add_into(target, others, n_rows):
        step_rows = next(size for size in (128, 96, 80, 64, 48, 32, 16) if n_rows % size == 0)

        @pl.loop(0, n_rows // step_rows)
        def _(step):
            rows = aligned(step * step_rows, step_rows)
            total = target[rows, :].astype(F32)
            for other in others:
                total = total + other[rows, :].astype(F32)
            target[rows, :] = total.astype(BF16)

    def reduction(key, part, got, fin, order, with_sums):
        n_rows = part.shape[2]
        stages, gathers = [], []
        offset, length, spot, both = 0, n_rows, n_rows, True

        def sides(rows, where, other_side):
            if both:
                return part.at[half, :, rows, :], got.at[:, where, :]
            return part.at[half, other_side, rows, :], got.at[0, where, :]

        def adds(rows, wheres, count):
            if both:
                return [
                    (part.at[half, k, rows, :], [got.at[k, where, :] for where in wheres], count)
                    for k in range(2)
                ]
            return [(part.at[half, pair, rows, :], [got.at[0, w, :] for w in wheres], count)]

        for what in order:
            if what == "near":
                where = pl.ds(0, n_rows)
                copies = [(part.at[1 - half], got.at[:, where, :], {"mp": near})]
                stages.append((copies, adds(pl.ds(0, n_rows), [where], n_rows), None, half))
                continue
            if what == "across":
                both = False
                rows, where = aligned_to(offset, length), pl.ds(spot, length)
                source, target = sides(rows, where, 1 - pair)
                copies = [(source, target, {"mp": across})]
                stages.append((copies, adds(rows, [where], length), None, pair))
                spot += length
                continue
            if length % (16 << len(what)) == 0:
                parts = [what]
            else:
                parts = [(bit,) for bit in what]
            for group in parts:
                whole = length % (16 << len(group)) != 0
                if not whole:
                    length >>= len(group)
                mine_at = 0 if whole else place_in(group, 0) * length
                copies, wheres = [], []
                for flip in flips(group):
                    at = 0 if whole else place_in(group, flip) * length
                    where = pl.ds(spot, length)
                    spot += length
                    source, target = sides(aligned_to(offset + at, length), where, pair)
                    copies.append((source, target, {"dp": column_peer(mask_of(group, flip))}))
                    wheres.append(where)
                keep = aligned_to(offset + mine_at, length)
                kind = "whole" if whole else None
                stages.append((copies, adds(keep, wheres, length), kind, place_in(group, 0)))
                if not whole:
                    gathers.append((group, offset + mine_at, length))
                offset = offset + mine_at
        last = len(stages)
        final = aligned_to(offset, length)
        for group, start, count in gathers[::-1]:
            rows = aligned_to(start, count)
            copies = [
                (fin.at[rows, :], fin.at[rows, :], {"dp": column_peer(mask_of(group, flip))})
                for flip in flips(group)
            ]
            stages.append((copies, [], None, None))
        firsts = [sum(len(stage[0]) for stage in stages[:i]) for i in range(len(stages))]
        slots = [sum(len(stage[0]) + 1 for stage in stages[:i]) for i in range(last)]

        def copies_of(index):
            for number, (source, target, device) in enumerate(stages[index][0]):
                at = firsts[index] + number
                yield pltpu.make_async_remote_copy(
                    src_ref=source,
                    dst_ref=target,
                    send_sem=r_send.at[key, at],
                    recv_sem=r_recv.at[key, at],
                    device_id=device,
                    device_id_type=MESH,
                )

        def sums_copies(index):
            if with_sums and index < last:
                for number, (_, _, device) in enumerate(stages[index][0]):
                    at = firsts[index] + number
                    yield pltpu.make_async_remote_copy(
                        src_ref=sums.at[index],
                        dst_ref=got_sums.at[slots[index] + stages[index][3]],
                        send_sem=s_send.at[at],
                        recv_sem=s_recv.at[at],
                        device_id=device,
                        device_id_type=MESH,
                    )

        def start(index):
            for copy in copies_of(index):
                copy.start()
            for copy in sums_copies(index):
                copy.start()

        def finish(index):
            for copy in copies_of(index):
                if stages[index][2] == "whole":
                    copy.wait_send()
                copy.wait_recv()
            for copy in sums_copies(index):
                copy.wait_recv()
            if with_sums and index < last:
                got_sums[slots[index] + stages[index][3]] = sums[index]
                total = got_sums[slots[index]]
                for other in range(len(stages[index][0])):
                    total = total + got_sums[slots[index] + 1 + other]
                sums[index + 1] = total
            for target, others, count in stages[index][1]:
                add_into(target, others, count)
            if index + 1 == last:
                fin[final, :] = part[half, pair, final, :]
            if index + 1 < len(stages):
                start(index + 1)

        def drain():
            for index, stage in enumerate(stages):
                if stage[2] != "whole":
                    for copy in copies_of(index):
                        copy.wait_send()
                for copy in sums_copies(index):
                    copy.wait_send()

        return start, finish, drain, len(stages), last

    def fill(part, net, first, count, source, base):
        for device in range(n_mp):
            cols = pl.ds(net * hid_width + device * shard, shard)
            part[device % 2, device // 2, pl.ds(first, count), :] = source[
                pl.ds(base, count), cols
            ].astype(BF16)

    def add_columns(net):
        cols = pl.ds(net * hid_width, hid_width)
        for line in range(2):
            total = jnp.sum(col_acc[pl.ds(8 * line, 8), cols], axis=0, keepdims=True)
            g1[pl.ds(lat_width + n_task + 8 + line, 1), cols] = total / vecs[pl.ds(1, 1), cols]

    def order_of(kind):
        if kind == 0:
            return ["near", "across"] + groups
        if kind == 1 or len(groups) < 2:
            return ["near"] + groups[:1] + ["across"] + groups[1:]
        return ["near", groups[1], "across", groups[0]] + groups[2:]

    split = part_b.shape[2]
    add_columns(0)
    fill(part_a, 0, 0, lat_width, g2t, 0)
    fill(part_b, 0, 0, split, g1, 0)
    fill(part_c, 0, 0, in_rows - split, g1, split)
    dyn_places = (
        (part_a, got_a, in_rows, lat_width),
        (part_b, got_b, 0, split),
        (part_c, got_c, split, in_rows - split),
    )
    chunks = [
        reduction(k, part, got, fin_dyn.at[pl.ds(first, count), :], order_of(k), False)
        for k, (part, got, first, count) in enumerate(dyn_places)
    ]
    for chunk in chunks:
        chunk[0](0)
    per_tile = 4
    inside = sorted(
        (place, chunk, index)
        for chunk, places in enumerate(EVENTS)
        for index, place in enumerate(places)
        if index < chunks[chunk][3] and place < per_tile * n_tiles
    )

    prepare(1)
    gathered(w_needs[1][2:])
    with_gain(rw2_t, rw2_g, 1)

    for place, chunk, index in inside:
        if place < 0:
            chunks[chunk][1](index)

    def point(tile, number):
        for place, chunk, index in inside:
            if place >= 0 and place % per_tile == number:

                @pl.when(tile == place // per_tile)
                def _():
                    chunks[chunk][1](index)

    def kept(tile):
        return aligned(jnp.maximum(tile - (n_tiles - LATE - 1), 0) * TILE, TILE)

    def latent_grads(tile):
        cols = aligned(tile * TILE, TILE)
        lat_rows = pl.ds(0, lat_width)
        lg = dot(d_dyn[cols, :], w1_raw[lat_rows, pl.ds(0, hid_width)], 1, 1)
        lg = lg + dot(d_pre[kept(tile), :], w1_raw[lat_rows, pl.ds(hid_width, hid_width)], 1, 1)
        lg = (lg * total_rows).astype(BF16)
        for device in range(n_mp):
            lg_stage[device, cols, :] = lg[:, device * share : (device + 1) * share]

    def send_grads(tile):
        local, remotes = grad_copies(tile)
        local.start()
        for remote in remotes:
            remote.start()

    @pl.loop(0, n_tiles)
    def _(tile):
        cols = aligned(tile * TILE, TILE)
        forward(1, aligned(own_rows + tile * TILE, TILE), True)
        point(tile, 0)
        bins = bins_ref[:, aligned(mine * own_rows + tile * TILE, TILE)]
        frac = frac_ref[:, aligned(mine * own_rows + tile * TILE, TILE)]
        z = dot(rw2_t[...], hid[...], 1, 1)
        bias = rb2_ref[...]
        z = z + jnp.concatenate([bias] * (TILE // LANES), axis=1)
        z = z - jnp.max(z, axis=0, keepdims=True)
        e = jnp.exp(z)
        total = jnp.sum(e, axis=0, keepdims=True)
        row = lax.broadcasted_iota(jnp.int32, z.shape, 0)
        target = jnp.where(row == bins, 1.0 - frac, 0.0) + jnp.where(row == bins + 1, frac, 0.0)
        loss = jnp.sum(target * (jnp.log(total) - z), axis=0, keepdims=True)
        row_acc[...] += loss
        d_logits = (REW_COEF / total_rows) * (e * (1.0 / total) - target)
        dlog[...] = d_logits.astype(BF16)
        sum_acc[pl.ds(8, 8), :] += dot(jnp.ones((8, TILE), BF16), dlog[...], 1, 1)
        rg2t[...] += dot(dlog[...], hid[...])
        dh[...] = dot(dlog[...], rw2_g[...], 0, 0)
        point(tile, 1)
        backward(1, d_pre, jnp.maximum(tile - (n_tiles - LATE - 1), 0) * TILE)
        point(tile, 2)
        g1[:, pl.ds(hid_width, hid_width)] += dot(x_t[:, cols], d_pre[kept(tile), :])

        if LATE < n_tiles:

            @pl.when(tile < n_tiles - LATE)
            def _():
                latent_grads(tile)

        point(tile, 3)

        if LATE < n_tiles:

            @pl.when(tile < n_tiles - LATE)
            def _():
                send_grads(tile)


    add_columns(1)
    third = part_rew.shape[3]
    spare = in_rows - 2 * third - 32
    for k in range(3):
        chunks.append(
            reduction(
                3 + k,
                part_rew.at[k],
                got_rew.at[k],
                fin_rew.at[pl.ds(k * third, third), :],
                order_of(k),
                k == 2,
            )
        )
    for k in range(3):
        rest = min(third, in_rows - k * third)
        for device in range(n_mp):
            cols = pl.ds(hid_width + device * shard, shard)
            where = (k, device % 2, device // 2)
            part_rew[where + (pl.ds(0, rest),)] = g1[pl.ds(k * third, rest), cols].astype(BF16)
            if rest < third:
                block = pl.ds(device * shard, shard)
                part_rew[where + (pl.ds(rest, LANES),)] = rg2t[:, block].astype(BF16)
        if k < 2:
            chunks[3 + k][0](0)
    tasks = g1[pl.ds(lat_width, n_task), :]
    table = split_dot(tasks, w1_raw[pl.ds(lat_width, n_rest), :], 1, 1).astype(BF16)
    for device in range(n_mp):
        where = (2, device % 2, device // 2)
        part_rew[where + (pl.ds(spare, 32), pl.ds(0, n_rest))] = table[0:32]
        part_rew[where + (pl.ds(spare, 32), pl.ds(LANES, n_rest))] = table[32:64]
        part_rew[where + (pl.ds(third - 16, 16), pl.ds(0, n_rest))] = table[64:80]
    sums[0] = jnp.zeros(sums.shape[1:], F32)
    sums[0, pl.ds(0, 1), aligned(pair * chip_cols, chip_cols)] = jnp.sum(
        b2_acc[...].T, axis=0, keepdims=True
    )
    sums[0, pl.ds(1, 1), pl.ds(0, LANES)] = sum_acc[pl.ds(8, 1), :]
    cons = jnp.sum(sum_acc[pl.ds(0, 8), :])
    rew = jnp.sum(row_acc[...])
    sums[0, pl.ds(2, 1), :] = jnp.full((1, lat_width), cons)
    sums[0, pl.ds(3, 1), :] = jnp.full((1, lat_width), rew)
    chunks[5][0](0)
    done = [(chunk, index) for _, chunk, index in inside]
    left = [(index, c) for c in range(3) for index in range(chunks[c][3]) if (c, index) not in done]
    base = min([index for index, _ in left], default=0)
    left = [(index - base, c, index) for index, c in left]
    left += [(index, c, index) for c in range(3, 6) for index in range(chunks[c][3])]
    late = [n_tiles - LATE + k for k in range(LATE)]
    for tile in late[:1]:
        latent_grads(tile)
    step = 0
    for when, chunk, index in sorted(left):
        if when > step:
            step = when
            for tile in late[step - 1 : step]:
                send_grads(tile)
            for tile in late[step : step + 1]:
                latent_grads(tile)
        chunks[chunk][1](index)
    fin_sums[...] = sums[chunks[5][4]]
    for chunk in chunks:
        chunk[2]()

    for index in range(n_weights):
        for kind in range(3):
            weight_copy(index, kind).wait_send()
    for slot in range(2):
        next_copy(slot).wait_send()

        @pl.loop(0, n_tiles)
        def _(tile):
            local, remote = lat_copies(slot, tile)
            local.wait()
            remote.wait()

    @pl.loop(0, n_tiles)
    def _(tile):
        dpl_copy(tile).wait_send()
        local, remotes = grad_copies(tile)
        local.wait()
        for remote in remotes:
            remote.wait()


def finish_kernel(
    lat_in,
    grad_in,
    dyn_in,
    rew_in,
    sums_in,
    embed,
    lat_out,
    grad_out,
    losses,
    grad_embed,
    dyn_w1,
    dyn_b1,
    dyn_gain,
    dyn_shift,
    rew_w1,
    rew_b1,
    rew_gain,
    rew_shift,
    dyn_w2,
    dyn_b2,
    rew_w2,
    rew_b2,
    dyn,
    rew,
    sums,
    stage,
    sems,
    *,
    total_rows,
    lat_width,
):
    n_big = stage.shape[1]
    copies = [
        pltpu.make_async_copy(source, target, sems.at[i])
        for i, (source, target) in enumerate(((dyn_in, dyn), (rew_in, rew), (sums_in, sums)))
    ]
    rows = stage.shape[2]
    outs = []
    for k in range(n_big):
        part = pl.ds(k * rows, rows)
        for side, (source, target) in enumerate(((lat_in, lat_out), (grad_in, grad_out))):
            first, last = sems.at[3 + 4 * k + 2 * side], sems.at[4 + 4 * k + 2 * side]
            copies.append(
                pltpu.make_async_copy(source.at[part, :], stage.at[side, k], first)
            )
            outs.append(pltpu.make_async_copy(stage.at[side, k], target.at[part, :], last))
    for copy in copies:
        copy.start()
    for copy, out in zip(copies[3:], outs):
        copy.wait()
        out.start()
    for copy in copies[:3]:
        copy.wait()
    n_task, n_embed = embed.shape
    n_rest = dyn_w1.shape[0] - lat_width
    n_act = n_rest - n_embed
    in_rows = lat_width + LANES
    first = lat_width + n_task
    moved = lax.broadcasted_iota(jnp.int32, (n_embed, n_rest), 1) == (
        lax.broadcasted_iota(jnp.int32, (n_embed, n_rest), 0) + n_act
    )
    moved = jnp.where(moved, 1.0, 0.0).astype(BF16)
    line = lax.broadcasted_iota(jnp.int32, (LANES - n_task, n_rest), 0)
    lane = lax.broadcasted_iota(jnp.int32, (LANES - n_task, n_rest), 1)
    acts = jnp.where((line == lane) & (line < n_act), 1.0, 0.0).astype(BF16)
    mix = jnp.concatenate([dot(embed[...], moved).astype(BF16), acts], axis=0)
    for net, w1, b1, gain, shift in (
        (dyn, dyn_w1, dyn_b1, dyn_gain, dyn_shift),
        (rew, rew_w1, rew_b1, rew_gain, rew_shift),
    ):
        w1[pl.ds(0, lat_width), :] = net[pl.ds(0, lat_width), :].astype(F32)
        w1[pl.ds(lat_width, n_rest), :] = dot(mix, net[pl.ds(lat_width, LANES), :], 0, 0)
        small = net[pl.ds(first, 16), :].astype(F32)
        b1[...] = small[n_act : n_act + 1]
        gain[...] = small[8:9]
        shift[...] = small[9:10]
    dyn_w2[...] = dyn[pl.ds(in_rows, lat_width), :].astype(F32).T
    n_bins = rew_w2.shape[0]
    rew_w2[...] = rew[pl.ds(in_rows, LANES), :].astype(F32)[:n_bins]
    dyn_b2[...] = sums[pl.ds(0, 1), :]
    rew_b2[...] = sums[pl.ds(1, 1), pl.ds(0, n_bins)]
    pieces = (
        (0, 32, in_rows - 32, 0),
        (32, 32, in_rows - 32, LANES),
        (64, n_task - 64, in_rows + LANES - 16, 0),
    )
    for to, count, row, col in pieces:
        grad_embed[pl.ds(to, count), :] = dot(
            rew[pl.ds(row, count), pl.ds(col, n_rest)], moved, 1, 1
        )
    pick = lax.broadcasted_iota(jnp.int32, losses.shape, 1) == 0
    both = jnp.where(pick, sums[pl.ds(2, 1), pl.ds(0, 2)], sums[pl.ds(3, 1), pl.ds(0, 2)])
    losses[...] = both * (1.0 / total_rows)
    for out in outs:
        out.wait()


def run_finish(total_rows, lat_width, n_in, n_bins, lat, grad, dyn, rew, sums, embed):
    shape = jax.ShapeDtypeStruct
    shard = dyn.shape[1]
    line = shape((1, shard), F32)
    first = [shape((n_in, shard), F32), line, line, line]
    any_spec = pl.BlockSpec(memory_space=pl.ANY)
    vmem_spec = pl.BlockSpec(memory_space=pltpu.VMEM)
    return pl.pallas_call(
        functools.partial(finish_kernel, total_rows=total_rows, lat_width=lat_width),
        out_shape=(
            shape(lat.shape, BF16),
            shape(grad.shape, BF16),
            shape((1, 2), F32),
            shape(embed.shape, F32),
            *first,
            *first,
            shape((shard, lat_width), F32),
            shape((1, lat_width), F32),
            shape((n_bins, shard), F32),
            shape((1, n_bins), F32),
        ),
        in_specs=[any_spec] * 5 + [vmem_spec],
        out_specs=[any_spec] * 2 + [vmem_spec] * 14,
        scratch_shapes=[
            pltpu.VMEM(dyn.shape, BF16),
            pltpu.VMEM(rew.shape, BF16),
            pltpu.VMEM(sums.shape, F32),
            pltpu.VMEM((2, PIECES, lat.shape[0] // PIECES, lat.shape[1]), BF16),
            pltpu.SemaphoreType.DMA((3 + 4 * PIECES,)),
        ],
        compiler_params=pltpu.CompilerParams(vmem_limit_bytes=60 << 20),
    )(lat, grad, dyn, rew, sums, embed)


def run_main(n_mp, n_dp, total_rows, args):
    latent, next_latent, w1, dyn_w2, rew_w2 = args[0], args[1], args[2], args[4], args[5]
    tok_rows, lat_width = latent.shape
    share = next_latent.shape[1]
    n_in, shard = w1.shape
    hid_width = n_mp * shard
    own = tok_rows // n_mp
    in_rows = lat_width + LANES
    n_tiles = own // TILE
    n_task = args[17].shape[0]
    any_spec = pl.BlockSpec(memory_space=pl.ANY)
    vmem_spec = pl.BlockSpec(memory_space=pltpu.VMEM)
    shape = jax.ShapeDtypeStruct
    dma = pltpu.SemaphoreType.DMA
    n_bits = n_dp.bit_length() - 1
    n_copies = 2 + 2 * sum(len(flips(group)) for group in column_groups(n_bits))
    third = (in_rows + LANES) // 3
    split = 3 * in_rows // 5
    return pl.pallas_call(
        functools.partial(main_kernel, (n_mp, n_dp, total_rows, hid_width)),
        out_shape=(
            shape((tok_rows, share), BF16),
            shape((tok_rows, share), BF16),
            shape((in_rows + lat_width, shard), BF16),
            shape((3 * third, shard), BF16),
            shape((8, lat_width), F32),
        ),
        in_specs=[any_spec] * 4 + [vmem_spec] * 16,
        out_specs=[any_spec] * 2 + [vmem_spec] * 3,
        scratch_shapes=[
            pltpu.VMEM((2 * own, in_rows), BF16),
            pltpu.VMEM((in_rows, own), BF16),
            pltpu.VMEM((n_in, 2 * hid_width), BF16),
            pltpu.VMEM((in_rows, 2 * hid_width), BF16),
            pltpu.VMEM((lat_width, hid_width), BF16),
            pltpu.VMEM((LANES, hid_width), BF16),
            pltpu.VMEM((lat_width, hid_width), BF16),
            pltpu.VMEM((LANES, hid_width), BF16),
            pltpu.VMEM((8, 2 * hid_width), F32),
            pltpu.VMEM((lat_width, shard), BF16),
            pltpu.VMEM((LANES, shard), BF16),
            pltpu.VMEM((2, 8, shard), F32),
            pltpu.VMEM((n_task, n_in - lat_width), BF16),
            pltpu.VMEM((16, TILE), F32),
            pltpu.VMEM((lat_width, LANES), F32),
            pltpu.VMEM((LANES, LANES), F32),
            pltpu.VMEM((2, 2, own, share), BF16),
            pltpu.VMEM((lat_width, own), BF16),
            pltpu.VMEM((2 * share, own), BF16),
            pltpu.VMEM((2, 2, own, share), BF16),
            pltpu.VMEM((n_mp, own, share), BF16),
            pltpu.VMEM((own, hid_width), BF16),
            pltpu.VMEM((2, 2, lat_width, shard), BF16),
            pltpu.VMEM((2, 2, split, shard), BF16),
            pltpu.VMEM((2, 2, in_rows - split, shard), BF16),
            pltpu.VMEM((3, 2, 2, third, shard), BF16),
            pltpu.VMEM((2, room(lat_width, n_bits), shard), BF16),
            pltpu.VMEM((2, room(split, n_bits), shard), BF16),
            pltpu.VMEM((2, room(in_rows - split, n_bits), shard), BF16),
            pltpu.VMEM((3, 2, room(third, n_bits), shard), BF16),
            pltpu.VMEM((3 + n_bits, 8, lat_width), F32),
            pltpu.VMEM((4 + 2 * n_bits, 8, lat_width), F32),
            pltpu.VMEM((in_rows, 2 * hid_width), F32),
            pltpu.VMEM((lat_width, hid_width), F32),
            pltpu.VMEM((LANES, hid_width), F32),
            pltpu.VMEM((TILE, hid_width), F32),
            pltpu.VMEM((TILE, hid_width), F32),
            pltpu.VMEM((TILE, hid_width), BF16),
            pltpu.VMEM((TILE, hid_width), BF16),
            pltpu.VMEM(((LATE + 1) * TILE, hid_width), BF16),
            pltpu.VMEM((2 * share, TILE), F32),
            pltpu.VMEM((2 * share, TILE), F32),
            pltpu.VMEM((LANES, TILE), BF16),
            pltpu.VMEM((TILE, LANES), F32),
            pltpu.VMEM((16, 2 * hid_width), F32),
            pltpu.VMEM((16, LANES), F32),
            pltpu.VMEM((1, TILE), F32),
            pltpu.VMEM((2 * share, LANES), F32),
            dma((11,)),
            dma((3, 7)),
            dma((3, 7)),
            dma((2,)),
            dma((2,)),
            dma((n_tiles,)),
            dma((n_tiles,)),
            dma((2 * n_tiles,)),
            dma((2 * n_tiles,)),
            dma((2 * n_tiles,)),
            dma((n_tiles,)),
            dma((3, n_tiles)),
            dma((3, n_tiles)),
            dma((6, n_copies)),
            dma((6, n_copies)),
            dma((n_copies,)),
            dma((n_copies,)),
        ],
        compiler_params=pltpu.CompilerParams(
            collective_id=0, has_side_effects=True, vmem_limit_bytes=62 << 20
        ),
    )(*args)


def on_device(
    latent,
    actions,
    task_ids,
    action_masks,
    next_latent,
    reward_bins,
    reward_frac,
    task_embed,
    dyn_w1,
    dyn_b1,
    dyn_gain,
    dyn_shift,
    rew_w1,
    rew_b1,
    rew_gain,
    rew_shift,
    dyn_w2,
    dyn_b2,
    rew_w2,
    rew_b2,
):
    n_mp, n_dp = lax.axis_size("mp"), lax.axis_size("dp")
    tok_rows, lat_width = latent.shape
    total_rows = tok_rows * n_dp

    def row(vector):
        return vector.reshape(1, -1)

    args = (
        latent,
        next_latent,
        dyn_w1,
        rew_w1,
        dyn_w2,
        rew_w2.T,
        *(row(v) for v in (dyn_b1, dyn_gain, dyn_shift, rew_b1, rew_gain, rew_shift)),
        row(task_ids),
        actions,
        action_masks.T,
        row(reward_bins),
        row(reward_frac),
        task_embed,
        row(dyn_b2),
        row(rew_b2),
    )
    latents, latent_grad, dyn, rew, sums = run_main(n_mp, n_dp, total_rows, args)
    n_bins = rew_b2.shape[0]
    n_in = dyn_w1.shape[0]
    outs = run_finish(
        total_rows, lat_width, n_in, n_bins, latents, latent_grad, dyn, rew, sums, task_embed
    )
    outs = [out.reshape(-1) if out.shape[0] == 1 else out for out in outs]
    outs[14] = outs[14].T
    return tuple(outs)


def solution(mesh):
    return jax.shard_map(
        on_device,
        mesh=mesh,
        in_specs=(
            P("dp", None),
            P(None, "dp"),
            P("dp"),
            P(),
            P("dp", "mp"),
            P("dp"),
            P("dp"),
            P(),
            P(None, "mp"),
            P("mp"),
            P("mp"),
            P("mp"),
            P(None, "mp"),
            P("mp"),
            P("mp"),
            P("mp"),
            P("mp", None),
            P(),
            P("mp", None),
            P(),
        ),
        out_specs=(
            P("dp", "mp"),
            P("dp", "mp"),
            P(),
            P(),
            P(None, "mp"),
            P("mp"),
            P("mp"),
            P("mp"),
            P(None, "mp"),
            P("mp"),
            P("mp"),
            P("mp"),
            P("mp", None),
            P(),
            P("mp", None),
            P(),
        ),
        check_vma=False,
    )
```

```python
import functools

import jax
import jax.numpy as jnp
from jax import lax
from jax.experimental import pallas as pl
from jax.experimental.pallas import tpu as pltpu
from jax.sharding import PartitionSpec as P

GROUP = 8
CONS_COEF = 20.0
REW_COEF = 0.1
EPS = 1e-05
LANES = 128
TILE = 512
SUB = 128
PART = 64
LATE = 2
PIECES = 2
DYN_KINDS = (0, 1, 0)
REW_KINDS = (0, 1, 0)
EVENTS = ((-1, 4, 9, 13, 99), (0, 6, 10, 14, 99), (0, 7, 11, 99, 99))
MESH = pl.DeviceIdType.MESH
F32 = jnp.float32
BF16 = jnp.bfloat16


def dot(left, right, left_dim=1, right_dim=0):
    return lax.dot_general(
        left, right, (((left_dim,), (right_dim,)), ((), ())), preferred_element_type=F32
    )


def aligned(start, size):
    return pl.ds(pl.multiple_of(start, size), size)


def aligned_to(start, size):
    return pl.ds(pl.multiple_of(start, 16), size)


def column_groups(n_bits):
    groups = [group for group in ((0,), (1, 2)) if group[-1] < n_bits]
    return groups + [(bit,) for bit in range(sum(map(len, groups)), n_bits)]


def flips(group):
    return range(1, 1 << len(group))


def mask_of(group, flip):
    return sum(1 << bit for at, bit in enumerate(group) if flip >> at & 1)


def group_masks(group):
    return [mask_of(group, flip) for flip in flips(group)] + [1 << bit for bit in group]


def room(n_rows, n_bits):
    extra, length = 2 * n_rows, n_rows
    for group in column_groups(n_bits):
        if length % (16 << len(group)) == 0:
            length >>= len(group)
            extra += length * ((1 << len(group)) - 1)
        else:
            for _ in group:
                length = length // 2 if length % 32 == 0 else length
                extra += length
    return extra


def split_dot(left, right, left_dim, right_dim):
    high = left.astype(BF16)
    low = (left - high.astype(F32)).astype(BF16)
    return dot(high, right, left_dim, right_dim) + dot(low, right, left_dim, right_dim)


def main_kernel(
    sizes,
    latent_in,
    next_in,
    dyn_w1,
    rew_w1,
    dyn_w2,
    rew_w2,
    dyn_b1,
    dyn_gain,
    dyn_shift,
    rew_b1,
    rew_gain,
    rew_shift,
    ids_ref,
    act_ref,
    masks_ref,
    bins_ref,
    frac_ref,
    embed_ref,
    dyn_b2,
    rew_b2,
    lat_out,
    grad_out,
    fin_dyn,
    fin_rew,
    fin_sums,
    x_all,
    x_t,
    w1_raw,
    w1_c,
    w2_t,
    rw2_t,
    w2_g,
    rw2_g,
    vecs,
    w2_own,
    rw2_own,
    vecs_own,
    embed_wide,
    extra_rows,
    b2_ref,
    rb2_ref,
    next_lat,
    dpl,
    dpl_send,
    lat_stage,
    lg_stage,
    d_dyn,
    part_a,
    part_b,
    part_c,
    part_rew,
    got_a,
    got_b,
    got_c,
    got_rew,
    sums,
    got_sums,
    g1,
    g2t,
    rg2t,
    pre,
    dh,
    dm,
    hid,
    d_pre,
    zt,
    latt,
    dlog,
    inv_ref,
    col_acc,
    sum_acc,
    row_acc,
    b2_acc,
    load_sem,
    w_send,
    w_recv,
    n_send,
    n_recv,
    d_send,
    d_recv,
    l_local,
    l_send,
    l_recv,
    g_local,
    g_send,
    g_recv,
    r_send,
    r_recv,
    s_send,
    s_recv,
):
    n_mp, n_dp, total_rows, hid_width = sizes
    n_bits = n_dp.bit_length() - 1
    mine = lax.axis_index("mp")
    column = lax.axis_index("dp")
    pair = mine // 2
    half = mine % 2
    own_rows = x_all.shape[0] // 2
    lat_width = latent_in.shape[1]
    shard = dyn_w1.shape[1]
    n_act = act_ref.shape[0]
    in_rows = g1.shape[0]
    share = next_in.shape[1]
    n_task = embed_ref.shape[0]
    chip_cols = 2 * share
    n_tiles = own_rows // TILE
    n_lane = hid_width // LANES

    def peer_of(flip):
        near = mine + 1 - 2 * half
        if flip == 1:
            return near
        across = 2 * (1 - pair)
        return across + half if flip == 2 else across + 1 - half

    def bit_of(bit):
        return (column // (1 << bit)) % 2

    def column_peer(mask):
        peer = column
        for bit in range(n_bits):
            if mask >> bit & 1:
                peer = peer + (1 - 2 * bit_of(bit)) * (1 << bit)
        return peer

    groups = column_groups(n_bits)

    def place_in(group, flip):
        place = 0
        for at, bit in enumerate(group):
            here = 1 - bit_of(bit) if flip >> at & 1 else bit_of(bit)
            place = place + here * (1 << (len(group) - 1 - at))
        return place

    def rows_of(device):
        return aligned(device * own_rows, own_rows)

    barrier = pltpu.get_barrier_semaphore()
    for flip in (1, 2, 3):
        pl.semaphore_signal(
            barrier, inc=1, device_id={"mp": peer_of(flip)}, device_id_type=MESH
        )
    aslant = {"mp": peer_of(2), "dp": column_peer(1)}
    pl.semaphore_signal(barrier, inc=1, device_id=aslant, device_id_type=MESH)
    masks = sorted({mask for group in groups for mask in group_masks(group)})
    for mask in masks:
        pl.semaphore_signal(
            barrier, inc=1, device_id={"dp": column_peer(mask)}, device_id_type=MESH
        )

    vecs_own[...] = jnp.zeros_like(vecs_own)
    for net, rows in enumerate(((dyn_b1, dyn_gain, dyn_shift), (rew_b1, rew_gain, rew_shift))):
        for line, ref in enumerate(rows):
            vecs_own[net, pl.ds(line, 1), :] = ref[...]
    w2_own[...] = dyn_w2[...].T
    n_bins = rew_w2.shape[0]
    rw2_own[...] = jnp.zeros_like(rw2_own)
    rw2_own[pl.ds(0, n_bins), :] = rew_w2[...]

    near, across = peer_of(1), peer_of(2)

    def w_pairs(block, rows_first):
        pairs = []
        for net in range(2):
            cols = aligned(net * hid_width + block * shard, shard)
            pairs.append(((dyn_w1, rew_w1)[net], w1_raw.at[:, cols]))
            pairs.append((vecs_own.at[net], vecs.at[:, cols]))
        cols = aligned(block * shard, shard)
        for side in (rows_first, 1 - rows_first):
            rows = aligned(side * chip_cols, chip_cols)
            pairs.append((w2_own.at[rows, :], w2_t.at[rows, cols]))
        pairs.append((rw2_own, rw2_t.at[:, cols]))
        return pairs

    w_needs = ((1, 0, 4, 5), (3, 2, 6))
    n_weights = 7

    def weight_copy(index, kind):
        source, target = w_pairs(mine, 1 - pair if kind == 1 else pair)[index]
        if kind == 2:
            source = target = w_pairs(across, pair)[index][1]
        return pltpu.make_async_remote_copy(
            src_ref=source,
            dst_ref=target,
            send_sem=w_send.at[kind, index],
            recv_sem=w_recv.at[kind, index],
            device_id={"mp": across if kind == 1 else near},
            device_id_type=MESH,
        )

    def next_copy(slot):
        rows = near if slot == 1 else peer_of(3)
        return pltpu.make_async_remote_copy(
            src_ref=next_in.at[rows_of(rows), :],
            dst_ref=next_lat.at[slot, half],
            send_sem=n_send.at[slot],
            recv_sem=n_recv.at[slot],
            device_id={"mp": near},
            device_id_type=MESH,
        )

    loads = []
    for slot, device in ((0, across), (1, mine)):
        loads.append(
            (
                latent_in.at[rows_of(device), :],
                x_all.at[pl.ds(slot * own_rows, own_rows), pl.ds(0, lat_width)],
            )
        )
    for slot, device in ((0, across), (1, mine)):
        loads.append((next_in.at[rows_of(device), :], next_lat.at[slot, half]))
    loads += w_pairs(mine, pair)
    loads = [
        pltpu.make_async_copy(source, target, load_sem.at[i])
        for i, (source, target) in enumerate(loads)
    ]
    for copy in loads:
        copy.start()
    pl.semaphore_wait(barrier, 4 + len(masks))
    for index in w_needs[0] + w_needs[1]:
        weight_copy(index, 1).start()
        weight_copy(index, 0).start()
    next_copy(0).start()
    next_copy(1).start()

    for ref in (g1, g2t, rg2t, col_acc, sum_acc, row_acc, b2_acc):
        ref[...] = jnp.zeros_like(ref)

    line = lax.broadcasted_iota(jnp.int32, extra_rows.shape, 0)
    extra_rows[...] = jnp.where((line == n_act) | (line == n_act + 1), 1.0, 0.0)
    n_embed = embed_ref.shape[1]
    n_rest = n_act + n_embed
    moved = lax.broadcasted_iota(jnp.int32, (n_embed, n_rest), 1) == (
        lax.broadcasted_iota(jnp.int32, (n_embed, n_rest), 0) + n_act
    )
    embed_wide[...] = dot(embed_ref[...], jnp.where(moved, 1.0, 0.0).astype(BF16)).astype(BF16)
    b2_ref[...] = jnp.broadcast_to(dyn_b2[...], (LANES, lat_width)).T
    rb2_ref[...] = jnp.full(rb2_ref.shape, -1e30, F32)
    rb2_ref[:, pl.ds(0, n_bins)] = jnp.broadcast_to(rew_b2[...], (LANES, n_bins))
    rb2_ref[...] = rb2_ref[...].T

    for slot, device in ((0, across), (1, mine)):
        base = device * own_rows

        @pl.loop(0, n_tiles)
        def _(tile):
            lanes = aligned(base + tile * TILE, TILE)
            ids = ids_ref[:, lanes]
            tasks = lax.broadcasted_iota(jnp.int32, (n_task, TILE), 0)
            onehot = jnp.where(tasks == ids, 1.0, 0.0).astype(BF16)
            masks = dot(masks_ref[...].astype(F32).astype(BF16), onehot)
            extra_rows[pl.ds(0, n_act), :] = act_ref[:, lanes].astype(F32) * masks
            masked = extra_rows[...].astype(BF16)
            rest = LANES - n_task - masked.shape[0]
            extra = jnp.concatenate([onehot, masked, jnp.zeros((rest, TILE), BF16)], axis=0)
            rows = aligned(slot * own_rows + tile * TILE, TILE)
            x_all[rows, pl.ds(lat_width, LANES)] = extra.T
            if slot == 1:
                x_t[pl.ds(lat_width, LANES), aligned(tile * TILE, TILE)] = extra

    for copy in loads[:2]:
        copy.wait()

    @pl.loop(0, n_tiles)
    def _(tile):
        rows = aligned(own_rows + tile * TILE, TILE)
        x_t[pl.ds(0, lat_width), aligned(tile * TILE, TILE)] = x_all[
            rows, pl.ds(0, lat_width)
        ].T

    def centre(values):
        return values - jnp.sum(values, axis=1, keepdims=True) * (1.0 / hid_width)

    def gathered(indices):
        for index in indices:
            weight_copy(index, 1).wait_recv()
            weight_copy(index, 2).start()
        for index in indices:
            loads[4 + index].wait()
            weight_copy(index, 0).wait_recv()
            weight_copy(index, 2).wait_recv()

    def with_gain(weights, scaled, net):
        gain = vecs[pl.ds(1, 1), pl.ds(net * hid_width, hid_width)]

        @pl.loop(0, weights.shape[0] // PART)
        def _(step):
            rows = aligned(step * PART, PART)
            scaled[rows, :] = (weights[rows, :].astype(F32) * gain).astype(BF16)

    def prepare(net):
        gathered(w_needs[net][:2])
        cols = pl.ds(net * hid_width, hid_width)

        @pl.loop(0, lat_width // PART)
        def _(step):
            rows = aligned(step * PART, PART)
            w1_c[rows, cols] = centre(w1_raw[rows, cols].astype(F32)).astype(BF16)

        table = dot(embed_wide[...], w1_raw[pl.ds(lat_width, n_rest), cols])
        w1_c[pl.ds(lat_width, n_task), cols] = centre(table).astype(BF16)
        act = centre(w1_raw[pl.ds(lat_width, 16), cols].astype(F32))
        bias = centre(vecs[pl.ds(0, 1), cols])
        high = bias.astype(BF16).astype(F32)
        row = lax.broadcasted_iota(jnp.int32, act.shape, 0)
        act = jnp.where(row < n_act, act, 0.0)
        act = jnp.where(row == n_act, high, jnp.where(row == n_act + 1, bias - high, act))
        w1_c[pl.ds(lat_width + n_task, 16), cols] = act.astype(BF16)
        rest = LANES - n_task - 16
        w1_c[pl.ds(lat_width + n_task + 16, rest), cols] = jnp.zeros((rest, hid_width), BF16)

    def forward(net, rows, keep):
        cols = pl.ds(net * hid_width, hid_width)
        values = dot(x_all[rows, :], w1_c[:, cols])
        pre[...] = values
        square = jnp.sum(values * values, axis=1, keepdims=True)
        inv_ref[...] = jnp.broadcast_to(
            lax.rsqrt(square * (1.0 / hid_width) + EPS), (TILE, LANES)
        )

        @pl.loop(0, TILE // SUB)
        def _(step):
            part = aligned(step * SUB, SUB)
            inv = inv_ref[part, :]
            for lane in range(n_lane):
                lanes = pl.ds(lane * LANES, LANES)
                wide = pl.ds(net * hid_width + lane * LANES, LANES)
                xhat = pre[part, lanes] * inv
                y = xhat * vecs[pl.ds(1, 1), wide] + vecs[pl.ds(2, 1), wide]
                if keep:
                    pre[part, lanes] = xhat
                y = y.astype(BF16)
                e = jnp.exp(jnp.minimum(y, 20.0))
                e2 = e + 2.0
                r = 1.0 / (e * e2 + 2.0)
                u = e * r
                t = u * e2
                hid[part, lanes] = y * t
                if keep:
                    dm[part, lanes] = t + (4.0 * y) * (u * (r + u))

    def backward(net, target, first_row):
        @pl.loop(0, TILE // SUB)
        def _(step):
            part = aligned(step * SUB, SUB)
            first = jnp.zeros((SUB, LANES), F32)
            second = jnp.zeros((SUB, LANES), F32)
            for lane in range(n_lane):
                lanes = pl.ds(lane * LANES, LANES)
                wide = pl.ds(net * hid_width + lane * LANES, LANES)
                g = dh[part, lanes] * dm[part, lanes].astype(F32)
                scaled = g * pre[part, lanes]
                col_acc[pl.ds(0, 8), wide] += jnp.sum(
                    scaled.reshape(SUB // 8, 8, LANES), axis=0
                )
                col_acc[pl.ds(8, 8), wide] += jnp.sum(g.reshape(SUB // 8, 8, LANES), axis=0)
                first += g
                second += scaled
                dh[part, lanes] = g
            inv = inv_ref[part, :]
            first = jnp.broadcast_to(
                jnp.sum(first, axis=1, keepdims=True) * (1.0 / hid_width), (SUB, LANES)
            )
            second = jnp.broadcast_to(
                jnp.sum(second, axis=1, keepdims=True) * (1.0 / hid_width), (SUB, LANES)
            )
            first = first * inv
            second = second * inv
            for lane in range(n_lane):
                lanes = pl.ds(lane * LANES, LANES)
                value = dh[part, lanes] * inv - first - pre[part, lanes] * second
                target[aligned(first_row + step * SUB, SUB), lanes] = value.astype(BF16)

    d_scale = 2.0 * CONS_COEF / total_rows

    def simnorm(slot, tile, target, row, col):
        rows = aligned(tile * TILE, TILE)
        zt[...] = dot(w2_t[aligned(pair * chip_cols, chip_cols), :], hid[...], 1, 1)
        for side in range(2):
            latt[pl.ds(side * share, share), :] = next_lat[slot, side, rows, :].T.astype(F32)

        @pl.loop(0, chip_cols // PART)
        def _(step):
            part = aligned(step * PART, PART)
            bias = b2_ref[aligned(pair * chip_cols + step * PART, PART), :]
            for lane in range(TILE // LANES):
                lanes = pl.ds(lane * LANES, LANES)
                z = (zt[part, lanes] + bias).reshape(PART // GROUP, GROUP, LANES)
                e = jnp.exp(z - jnp.max(z, axis=1, keepdims=True))
                s = e * (1.0 / jnp.sum(e, axis=1, keepdims=True))
                error = s - latt[part, lanes].reshape(z.shape)
                sum_acc[pl.ds(0, 8), :] += jnp.sum(error * error, axis=0)
                d_lat = d_scale * error
                d_z = s * (d_lat - jnp.sum(s * d_lat, axis=1, keepdims=True))
                zt[part, lanes] = s.reshape(PART, LANES)
                b2_acc[part, :] += d_z.reshape(PART, LANES)
                target[
                    aligned(row + step * PART, PART), aligned(col + lane * LANES, LANES)
                ] = d_z.reshape(PART, LANES).astype(BF16)

        for side in range(2):
            lat_stage[slot, side, rows, :] = zt[pl.ds(side * share, share), :].astype(BF16).T

    def lat_copies(slot, tile):
        device = across if slot == 0 else mine
        rows = aligned(tile * TILE, TILE)
        out_rows = lat_out.at[aligned(device * own_rows + tile * TILE, TILE), :]
        index = slot * n_tiles + tile
        local = pltpu.make_async_copy(
            lat_stage.at[slot, half, rows, :], out_rows, l_local.at[index]
        )
        remote = pltpu.make_async_remote_copy(
            src_ref=lat_stage.at[slot, 1 - half, rows, :],
            dst_ref=out_rows,
            send_sem=l_send.at[index],
            recv_sem=l_recv.at[index],
            device_id={"mp": near},
            device_id_type=MESH,
        )
        return local, remote

    def dpl_copy(tile):
        cols = aligned(tile * TILE, TILE)
        return pltpu.make_async_remote_copy(
            src_ref=dpl_send.at[:, cols],
            dst_ref=dpl.at[aligned(pair * chip_cols, chip_cols), cols],
            send_sem=d_send.at[tile],
            recv_sem=d_recv.at[tile],
            device_id={"mp": across},
            device_id_type=MESH,
        )

    def grad_copies(tile):
        rows = aligned(tile * TILE, TILE)
        out_rows = grad_out.at[aligned(mine * own_rows + tile * TILE, TILE), :]
        remotes = []
        for flip in (2, 3, 1):
            peer = peer_of(flip)
            remotes.append(
                pltpu.make_async_remote_copy(
                    src_ref=lg_stage.at[peer, rows, :],
                    dst_ref=out_rows,
                    send_sem=g_send.at[flip - 1, tile],
                    recv_sem=g_recv.at[flip - 1, tile],
                    device_id={"mp": peer},
                    device_id_type=MESH,
                )
            )
        local = pltpu.make_async_copy(lg_stage.at[mine, rows, :], out_rows, g_local.at[tile])
        return local, remotes

    prepare(0)
    loads[2].wait()
    next_copy(0).wait_recv()

    @pl.loop(0, n_tiles)
    def _(tile):
        forward(0, aligned(tile * TILE, TILE), False)

        @pl.when(tile == 0)
        def _():
            gathered(w_needs[0][2:3])

        simnorm(0, tile, dpl_send, 0, tile * TILE)
        dpl_copy(tile).start()
        local, remote = lat_copies(0, tile)
        local.start()
        remote.start()

    def add_into(target, others, n_rows):
        step_rows = next(size for size in (128, 96, 80, 64, 48, 32, 16) if n_rows % size == 0)

        @pl.loop(0, n_rows // step_rows)
        def _(step):
            rows = aligned(step * step_rows, step_rows)
            total = target[rows, :].astype(F32)
            for other in others:
                total = total + other[rows, :].astype(F32)
            target[rows, :] = total.astype(BF16)

    def reduction(key, part, got, fin, order, with_sums):
        n_rows = part.shape[2]
        stages, gathers = [], []
        offset, length, spot, both = 0, n_rows, n_rows, True

        def sides(rows, where, other_side):
            if both:
                return part.at[half, :, rows, :], got.at[:, where, :]
            return part.at[half, other_side, rows, :], got.at[0, where, :]

        def adds(rows, wheres, count):
            if both:
                return [
                    (part.at[half, k, rows, :], [got.at[k, where, :] for where in wheres], count)
                    for k in range(2)
                ]
            return [(part.at[half, pair, rows, :], [got.at[0, w, :] for w in wheres], count)]

        for what in order:
            if what == "near":
                where = pl.ds(0, n_rows)
                copies = [(part.at[1 - half], got.at[:, where, :], {"mp": near})]
                stages.append((copies, adds(pl.ds(0, n_rows), [where], n_rows), None, half))
                continue
            if what == "across":
                both = False
                rows, where = aligned_to(offset, length), pl.ds(spot, length)
                source, target = sides(rows, where, 1 - pair)
                copies = [(source, target, {"mp": across})]
                stages.append((copies, adds(rows, [where], length), None, pair))
                spot += length
                continue
            if what == "cross":
                both = False
                length //= 2
                keep_at = offset + place_in(groups[0], 0) * length
                other_at = offset + place_in(groups[0], 1) * length
                copies, wheres = [], []
                for side, at, device in (
                    (1 - pair, other_at, aslant),
                    (1 - pair, keep_at, {"mp": across}),
                    (pair, other_at, {"dp": column_peer(1)}),
                ):
                    where = pl.ds(spot, length)
                    spot += length
                    source, target = sides(aligned_to(at, length), where, side)
                    copies.append((source, target, device))
                    wheres.append(where)
                keep = aligned_to(keep_at, length)
                here = 2 * pair + place_in(groups[0], 0)
                stages.append((copies, adds(keep, wheres, length), None, here))
                gathers.append((groups[0], keep_at, length))
                offset = keep_at
                continue
            if length % (16 << len(what)) == 0:
                parts = [what]
            else:
                parts = [(bit,) for bit in what]
            for group in parts:
                whole = length % (16 << len(group)) != 0
                if not whole:
                    length >>= len(group)
                mine_at = 0 if whole else place_in(group, 0) * length
                copies, wheres = [], []
                for flip in flips(group):
                    at = 0 if whole else place_in(group, flip) * length
                    where = pl.ds(spot, length)
                    spot += length
                    source, target = sides(aligned_to(offset + at, length), where, pair)
                    copies.append((source, target, {"dp": column_peer(mask_of(group, flip))}))
                    wheres.append(where)
                keep = aligned_to(offset + mine_at, length)
                kind = "whole" if whole else None
                stages.append((copies, adds(keep, wheres, length), kind, place_in(group, 0)))
                if not whole:
                    gathers.append((group, offset + mine_at, length))
                offset = offset + mine_at
        last = len(stages)
        final = aligned_to(offset, length)
        for group, start, count in gathers[::-1]:
            rows = aligned_to(start, count)
            copies = [
                (fin.at[rows, :], fin.at[rows, :], {"dp": column_peer(mask_of(group, flip))})
                for flip in flips(group)
            ]
            stages.append((copies, [], None, None))
        firsts = [sum(len(stage[0]) for stage in stages[:i]) for i in range(len(stages))]
        slots = [sum(len(stage[0]) + 1 for stage in stages[:i]) for i in range(last)]

        def copies_of(index):
            for number, (source, target, device) in enumerate(stages[index][0]):
                at = firsts[index] + number
                yield pltpu.make_async_remote_copy(
                    src_ref=source,
                    dst_ref=target,
                    send_sem=r_send.at[key, at],
                    recv_sem=r_recv.at[key, at],
                    device_id=device,
                    device_id_type=MESH,
                )

        def sums_copies(index):
            if with_sums and index < last:
                for number, (_, _, device) in enumerate(stages[index][0]):
                    at = firsts[index] + number
                    yield pltpu.make_async_remote_copy(
                        src_ref=sums.at[index],
                        dst_ref=got_sums.at[slots[index] + stages[index][3]],
                        send_sem=s_send.at[at],
                        recv_sem=s_recv.at[at],
                        device_id=device,
                        device_id_type=MESH,
                    )

        def start(index):
            for copy in copies_of(index):
                copy.start()
            for copy in sums_copies(index):
                copy.start()

        def finish(index):
            for copy in copies_of(index):
                if stages[index][2] == "whole":
                    copy.wait_send()
                copy.wait_recv()
            for copy in sums_copies(index):
                copy.wait_recv()
            if with_sums and index < last:
                got_sums[slots[index] + stages[index][3]] = sums[index]
                total = got_sums[slots[index]]
                for other in range(len(stages[index][0])):
                    total = total + got_sums[slots[index] + 1 + other]
                sums[index + 1] = total
            for target, others, count in stages[index][1]:
                add_into(target, others, count)
            if index + 1 == last:
                fin[final, :] = part[half, pair, final, :]
            if index + 1 < len(stages):
                start(index + 1)

        def drain():
            for index, stage in enumerate(stages):
                if stage[2] != "whole":
                    for copy in copies_of(index):
                        copy.wait_send()
                for copy in sums_copies(index):
                    copy.wait_send()

        return start, finish, drain, len(stages), last

    def fill(part, net, first, count, source, base):
        for device in range(n_mp):
            cols = pl.ds(net * hid_width + device * shard, shard)
            part[device % 2, device // 2, pl.ds(first, count), :] = source[
                pl.ds(base, count), cols
            ].astype(BF16)

    def add_columns(net):
        cols = pl.ds(net * hid_width, hid_width)
        for line in range(2):
            total = jnp.sum(col_acc[pl.ds(8 * line, 8), cols], axis=0, keepdims=True)
            g1[pl.ds(lat_width + n_task + 8 + line, 1), cols] = total / vecs[pl.ds(1, 1), cols]

    def order_of(kind):
        if kind == 0 or len(groups) < 2:
            return ["near", "cross"] + groups[1:]
        if kind == 1:
            return ["near", groups[1], "cross"] + groups[2:]
        if kind == 2:
            return ["near"] + groups[:1] + ["across"] + groups[1:]
        return ["near", "across"] + groups

    split = part_b.shape[2]
    dyn_places = (
        (part_a, got_a, in_rows, lat_width),
        (part_b, got_b, 0, split),
        (part_c, got_c, split, in_rows - split),
    )
    chunks = [
        reduction(k, part, got, fin_dyn.at[pl.ds(first, count), :], order_of(DYN_KINDS[k]), False)
        for k, (part, got, first, count) in enumerate(dyn_places)
    ]
    gathered(w_needs[0][3:])
    with_gain(w2_t, w2_g, 0)
    loads[3].wait()
    next_copy(1).wait_recv()

    @pl.loop(0, n_tiles)
    def _(tile):
        cols = aligned(tile * TILE, TILE)
        forward(0, aligned(own_rows + tile * TILE, TILE), True)
        simnorm(1, tile, dpl, pair * chip_cols, tile * TILE)
        local, remote = lat_copies(1, tile)
        local.start()
        remote.start()
        dpl_copy(tile).wait_recv()
        d_lat = dpl[:, cols]
        g2t[...] += dot(d_lat, hid[...])

        @pl.when(tile == n_tiles - 1)
        def _():
            fill(part_a, 0, 0, lat_width, g2t, 0)
            chunks[0][0](0)

        dh[...] = dot(d_lat, w2_g[...], 0, 0)
        backward(0, d_dyn, tile * TILE)
        g1[:, pl.ds(0, hid_width)] += dot(x_t[:, cols], d_dyn[cols, :])

    fill(part_b, 0, 0, split, g1, 0)
    chunks[1][0](0)
    add_columns(0)
    fill(part_c, 0, 0, in_rows - split, g1, split)
    chunks[2][0](0)
    per_tile = 4
    inside = sorted(
        (place, chunk, index)
        for chunk, places in enumerate(EVENTS)
        for index, place in enumerate(places)
        if index < chunks[chunk][3] and place < per_tile * n_tiles
    )

    prepare(1)
    gathered(w_needs[1][2:])
    with_gain(rw2_t, rw2_g, 1)

    for place, chunk, index in inside:
        if place < 0:
            chunks[chunk][1](index)

    def point(tile, number):
        for place, chunk, index in inside:
            if place >= 0 and place % per_tile == number:

                @pl.when(tile == place // per_tile)
                def _():
                    chunks[chunk][1](index)

    def kept(tile):
        return aligned(jnp.maximum(tile - (n_tiles - LATE - 1), 0) * TILE, TILE)

    def latent_grads(tile):
        cols = aligned(tile * TILE, TILE)
        lat_rows = pl.ds(0, lat_width)
        lg = dot(d_dyn[cols, :], w1_raw[lat_rows, pl.ds(0, hid_width)], 1, 1)
        lg = lg + dot(d_pre[kept(tile), :], w1_raw[lat_rows, pl.ds(hid_width, hid_width)], 1, 1)
        lg = (lg * total_rows).astype(BF16)
        for device in range(n_mp):
            lg_stage[device, cols, :] = lg[:, device * share : (device + 1) * share]

    def send_grads(tile):
        local, remotes = grad_copies(tile)
        local.start()
        for remote in remotes:
            remote.start()

    @pl.loop(0, n_tiles)
    def _(tile):
        cols = aligned(tile * TILE, TILE)
        forward(1, aligned(own_rows + tile * TILE, TILE), True)
        point(tile, 0)
        bins = bins_ref[:, aligned(mine * own_rows + tile * TILE, TILE)]
        frac = frac_ref[:, aligned(mine * own_rows + tile * TILE, TILE)]
        z = dot(rw2_t[...], hid[...], 1, 1)
        bias = rb2_ref[...]
        z = z + jnp.concatenate([bias] * (TILE // LANES), axis=1)
        z = z - jnp.max(z, axis=0, keepdims=True)
        e = jnp.exp(z)
        total = jnp.sum(e, axis=0, keepdims=True)
        row = lax.broadcasted_iota(jnp.int32, z.shape, 0)
        target = jnp.where(row == bins, 1.0 - frac, 0.0) + jnp.where(row == bins + 1, frac, 0.0)
        loss = jnp.sum(target * (jnp.log(total) - z), axis=0, keepdims=True)
        row_acc[...] += loss
        d_logits = (REW_COEF / total_rows) * (e * (1.0 / total) - target)
        dlog[...] = d_logits.astype(BF16)
        sum_acc[pl.ds(8, 8), :] += dot(jnp.ones((8, TILE), BF16), dlog[...], 1, 1)
        rg2t[...] += dot(dlog[...], hid[...])
        dh[...] = dot(dlog[...], rw2_g[...], 0, 0)
        point(tile, 1)
        backward(1, d_pre, jnp.maximum(tile - (n_tiles - LATE - 1), 0) * TILE)
        point(tile, 2)
        g1[:, pl.ds(hid_width, hid_width)] += dot(x_t[:, cols], d_pre[kept(tile), :])

        if LATE < n_tiles:

            @pl.when(tile < n_tiles - LATE)
            def _():
                latent_grads(tile)

        point(tile, 3)

        if LATE < n_tiles:

            @pl.when(tile < n_tiles - LATE)
            def _():
                send_grads(tile)


    add_columns(1)
    third = part_rew.shape[3]
    spare = in_rows - 2 * third - 32
    for k in range(3):
        chunks.append(
            reduction(
                3 + k,
                part_rew.at[k],
                got_rew.at[k],
                fin_rew.at[pl.ds(k * third, third), :],
                order_of(REW_KINDS[k]),
                k == 2,
            )
        )
    for k in range(3):
        rest = min(third, in_rows - k * third)
        for device in range(n_mp):
            cols = pl.ds(hid_width + device * shard, shard)
            where = (k, device % 2, device // 2)
            part_rew[where + (pl.ds(0, rest),)] = g1[pl.ds(k * third, rest), cols].astype(BF16)
            if rest < third:
                block = pl.ds(device * shard, shard)
                part_rew[where + (pl.ds(rest, LANES),)] = rg2t[:, block].astype(BF16)
        if k < 2:
            chunks[3 + k][0](0)
    tasks = g1[pl.ds(lat_width, n_task), :]
    table = split_dot(tasks, w1_raw[pl.ds(lat_width, n_rest), :], 1, 1).astype(BF16)
    for device in range(n_mp):
        where = (2, device % 2, device // 2)
        part_rew[where + (pl.ds(spare, 32), pl.ds(0, n_rest))] = table[0:32]
        part_rew[where + (pl.ds(spare, 32), pl.ds(LANES, n_rest))] = table[32:64]
        part_rew[where + (pl.ds(third - 16, 16), pl.ds(0, n_rest))] = table[64:80]
    sums[0] = jnp.zeros(sums.shape[1:], F32)
    sums[0, pl.ds(0, 1), aligned(pair * chip_cols, chip_cols)] = jnp.sum(
        b2_acc[...].T, axis=0, keepdims=True
    )
    sums[0, pl.ds(1, 1), pl.ds(0, LANES)] = sum_acc[pl.ds(8, 1), :]
    cons = jnp.sum(sum_acc[pl.ds(0, 8), :])
    rew = jnp.sum(row_acc[...])
    sums[0, pl.ds(2, 1), :] = jnp.full((1, lat_width), cons)
    sums[0, pl.ds(3, 1), :] = jnp.full((1, lat_width), rew)
    chunks[5][0](0)
    done = [(chunk, index) for _, chunk, index in inside]
    left = [(index, c) for c in range(3) for index in range(chunks[c][3]) if (c, index) not in done]
    base = min([index for index, _ in left], default=0)
    left = [(index - base, c, index) for index, c in left]
    left += [(index, c, index) for c in range(3, 6) for index in range(chunks[c][3])]
    late = [n_tiles - LATE + k for k in range(LATE)]
    for tile in late[:1]:
        latent_grads(tile)
    step = 0
    for when, chunk, index in sorted(left):
        if when > step:
            step = when
            for tile in late[step - 1 : step]:
                send_grads(tile)
            for tile in late[step : step + 1]:
                latent_grads(tile)
        chunks[chunk][1](index)
    fin_sums[...] = sums[chunks[5][4]]
    for chunk in chunks:
        chunk[2]()

    for index in range(n_weights):
        for kind in range(3):
            weight_copy(index, kind).wait_send()
    for slot in range(2):
        next_copy(slot).wait_send()

        @pl.loop(0, n_tiles)
        def _(tile):
            local, remote = lat_copies(slot, tile)
            local.wait()
            remote.wait()

    @pl.loop(0, n_tiles)
    def _(tile):
        dpl_copy(tile).wait_send()
        local, remotes = grad_copies(tile)
        local.wait()
        for remote in remotes:
            remote.wait()


def finish_kernel(
    lat_in,
    grad_in,
    dyn_in,
    rew_in,
    sums_in,
    embed,
    lat_out,
    grad_out,
    losses,
    grad_embed,
    dyn_w1,
    dyn_b1,
    dyn_gain,
    dyn_shift,
    rew_w1,
    rew_b1,
    rew_gain,
    rew_shift,
    dyn_w2,
    dyn_b2,
    rew_w2,
    rew_b2,
    dyn,
    rew,
    sums,
    stage,
    sems,
    *,
    total_rows,
    lat_width,
):
    n_big = stage.shape[1]
    copies = [
        pltpu.make_async_copy(source, target, sems.at[i])
        for i, (source, target) in enumerate(((dyn_in, dyn), (rew_in, rew), (sums_in, sums)))
    ]
    rows = stage.shape[2]
    outs = []
    for k in range(n_big):
        part = pl.ds(k * rows, rows)
        for side, (source, target) in enumerate(((lat_in, lat_out), (grad_in, grad_out))):
            first, last = sems.at[3 + 4 * k + 2 * side], sems.at[4 + 4 * k + 2 * side]
            copies.append(
                pltpu.make_async_copy(source.at[part, :], stage.at[side, k], first)
            )
            outs.append(pltpu.make_async_copy(stage.at[side, k], target.at[part, :], last))
    for copy in copies:
        copy.start()
    for copy, out in zip(copies[3:], outs):
        copy.wait()
        out.start()
    for copy in copies[:3]:
        copy.wait()
    n_task, n_embed = embed.shape
    n_rest = dyn_w1.shape[0] - lat_width
    n_act = n_rest - n_embed
    in_rows = lat_width + LANES
    first = lat_width + n_task
    moved = lax.broadcasted_iota(jnp.int32, (n_embed, n_rest), 1) == (
        lax.broadcasted_iota(jnp.int32, (n_embed, n_rest), 0) + n_act
    )
    moved = jnp.where(moved, 1.0, 0.0).astype(BF16)
    line = lax.broadcasted_iota(jnp.int32, (LANES - n_task, n_rest), 0)
    lane = lax.broadcasted_iota(jnp.int32, (LANES - n_task, n_rest), 1)
    acts = jnp.where((line == lane) & (line < n_act), 1.0, 0.0).astype(BF16)
    mix = jnp.concatenate([dot(embed[...], moved).astype(BF16), acts], axis=0)
    for net, w1, b1, gain, shift in (
        (dyn, dyn_w1, dyn_b1, dyn_gain, dyn_shift),
        (rew, rew_w1, rew_b1, rew_gain, rew_shift),
    ):
        w1[pl.ds(0, lat_width), :] = net[pl.ds(0, lat_width), :].astype(F32)
        w1[pl.ds(lat_width, n_rest), :] = dot(mix, net[pl.ds(lat_width, LANES), :], 0, 0)
        small = net[pl.ds(first, 16), :].astype(F32)
        b1[...] = small[n_act : n_act + 1]
        gain[...] = small[8:9]
        shift[...] = small[9:10]
    dyn_w2[...] = dyn[pl.ds(in_rows, lat_width), :].astype(F32).T
    n_bins = rew_w2.shape[0]
    rew_w2[...] = rew[pl.ds(in_rows, LANES), :].astype(F32)[:n_bins]
    dyn_b2[...] = sums[pl.ds(0, 1), :]
    rew_b2[...] = sums[pl.ds(1, 1), pl.ds(0, n_bins)]
    pieces = (
        (0, 32, in_rows - 32, 0),
        (32, 32, in_rows - 32, LANES),
        (64, n_task - 64, in_rows + LANES - 16, 0),
    )
    for to, count, row, col in pieces:
        grad_embed[pl.ds(to, count), :] = dot(
            rew[pl.ds(row, count), pl.ds(col, n_rest)], moved, 1, 1
        )
    pick = lax.broadcasted_iota(jnp.int32, losses.shape, 1) == 0
    both = jnp.where(pick, sums[pl.ds(2, 1), pl.ds(0, 2)], sums[pl.ds(3, 1), pl.ds(0, 2)])
    losses[...] = both * (1.0 / total_rows)
    for out in outs:
        out.wait()


def run_finish(total_rows, lat_width, n_in, n_bins, lat, grad, dyn, rew, sums, embed):
    shape = jax.ShapeDtypeStruct
    shard = dyn.shape[1]
    line = shape((1, shard), F32)
    first = [shape((n_in, shard), F32), line, line, line]
    any_spec = pl.BlockSpec(memory_space=pl.ANY)
    vmem_spec = pl.BlockSpec(memory_space=pltpu.VMEM)
    return pl.pallas_call(
        functools.partial(finish_kernel, total_rows=total_rows, lat_width=lat_width),
        out_shape=(
            shape(lat.shape, BF16),
            shape(grad.shape, BF16),
            shape((1, 2), F32),
            shape(embed.shape, F32),
            *first,
            *first,
            shape((shard, lat_width), F32),
            shape((1, lat_width), F32),
            shape((n_bins, shard), F32),
            shape((1, n_bins), F32),
        ),
        in_specs=[any_spec] * 5 + [vmem_spec],
        out_specs=[any_spec] * 2 + [vmem_spec] * 14,
        scratch_shapes=[
            pltpu.VMEM(dyn.shape, BF16),
            pltpu.VMEM(rew.shape, BF16),
            pltpu.VMEM(sums.shape, F32),
            pltpu.VMEM((2, PIECES, lat.shape[0] // PIECES, lat.shape[1]), BF16),
            pltpu.SemaphoreType.DMA((3 + 4 * PIECES,)),
        ],
        compiler_params=pltpu.CompilerParams(vmem_limit_bytes=60 << 20),
    )(lat, grad, dyn, rew, sums, embed)


def run_main(n_mp, n_dp, total_rows, args):
    latent, next_latent, w1, dyn_w2, rew_w2 = args[0], args[1], args[2], args[4], args[5]
    tok_rows, lat_width = latent.shape
    share = next_latent.shape[1]
    n_in, shard = w1.shape
    hid_width = n_mp * shard
    own = tok_rows // n_mp
    in_rows = lat_width + LANES
    n_tiles = own // TILE
    n_task = args[17].shape[0]
    any_spec = pl.BlockSpec(memory_space=pl.ANY)
    vmem_spec = pl.BlockSpec(memory_space=pltpu.VMEM)
    shape = jax.ShapeDtypeStruct
    dma = pltpu.SemaphoreType.DMA
    n_bits = n_dp.bit_length() - 1
    n_copies = 4 + 2 * sum(len(flips(group)) for group in column_groups(n_bits))
    third = (in_rows + LANES) // 3
    split = 3 * in_rows // 5
    return pl.pallas_call(
        functools.partial(main_kernel, (n_mp, n_dp, total_rows, hid_width)),
        out_shape=(
            shape((tok_rows, share), BF16),
            shape((tok_rows, share), BF16),
            shape((in_rows + lat_width, shard), BF16),
            shape((3 * third, shard), BF16),
            shape((8, lat_width), F32),
        ),
        in_specs=[any_spec] * 4 + [vmem_spec] * 16,
        out_specs=[any_spec] * 2 + [vmem_spec] * 3,
        scratch_shapes=[
            pltpu.VMEM((2 * own, in_rows), BF16),
            pltpu.VMEM((in_rows, own), BF16),
            pltpu.VMEM((n_in, 2 * hid_width), BF16),
            pltpu.VMEM((in_rows, 2 * hid_width), BF16),
            pltpu.VMEM((lat_width, hid_width), BF16),
            pltpu.VMEM((LANES, hid_width), BF16),
            pltpu.VMEM((lat_width, hid_width), BF16),
            pltpu.VMEM((LANES, hid_width), BF16),
            pltpu.VMEM((8, 2 * hid_width), F32),
            pltpu.VMEM((lat_width, shard), BF16),
            pltpu.VMEM((LANES, shard), BF16),
            pltpu.VMEM((2, 8, shard), F32),
            pltpu.VMEM((n_task, n_in - lat_width), BF16),
            pltpu.VMEM((16, TILE), F32),
            pltpu.VMEM((lat_width, LANES), F32),
            pltpu.VMEM((LANES, LANES), F32),
            pltpu.VMEM((2, 2, own, share), BF16),
            pltpu.VMEM((lat_width, own), BF16),
            pltpu.VMEM((2 * share, own), BF16),
            pltpu.VMEM((2, 2, own, share), BF16),
            pltpu.VMEM((n_mp, own, share), BF16),
            pltpu.VMEM((own, hid_width), BF16),
            pltpu.VMEM((2, 2, lat_width, shard), BF16),
            pltpu.VMEM((2, 2, split, shard), BF16),
            pltpu.VMEM((2, 2, in_rows - split, shard), BF16),
            pltpu.VMEM((3, 2, 2, third, shard), BF16),
            pltpu.VMEM((2, room(lat_width, n_bits), shard), BF16),
            pltpu.VMEM((2, room(split, n_bits), shard), BF16),
            pltpu.VMEM((2, room(in_rows - split, n_bits), shard), BF16),
            pltpu.VMEM((3, 2, room(third, n_bits), shard), BF16),
            pltpu.VMEM((3 + n_bits, 8, lat_width), F32),
            pltpu.VMEM((4 + 2 * n_bits, 8, lat_width), F32),
            pltpu.VMEM((in_rows, 2 * hid_width), F32),
            pltpu.VMEM((lat_width, hid_width), F32),
            pltpu.VMEM((LANES, hid_width), F32),
            pltpu.VMEM((TILE, hid_width), F32),
            pltpu.VMEM((TILE, hid_width), F32),
            pltpu.VMEM((TILE, hid_width), BF16),
            pltpu.VMEM((TILE, hid_width), BF16),
            pltpu.VMEM(((LATE + 1) * TILE, hid_width), BF16),
            pltpu.VMEM((2 * share, TILE), F32),
            pltpu.VMEM((2 * share, TILE), F32),
            pltpu.VMEM((LANES, TILE), BF16),
            pltpu.VMEM((TILE, LANES), F32),
            pltpu.VMEM((16, 2 * hid_width), F32),
            pltpu.VMEM((16, LANES), F32),
            pltpu.VMEM((1, TILE), F32),
            pltpu.VMEM((2 * share, LANES), F32),
            dma((11,)),
            dma((3, 7)),
            dma((3, 7)),
            dma((2,)),
            dma((2,)),
            dma((n_tiles,)),
            dma((n_tiles,)),
            dma((2 * n_tiles,)),
            dma((2 * n_tiles,)),
            dma((2 * n_tiles,)),
            dma((n_tiles,)),
            dma((3, n_tiles)),
            dma((3, n_tiles)),
            dma((6, n_copies)),
            dma((6, n_copies)),
            dma((n_copies,)),
            dma((n_copies,)),
        ],
        compiler_params=pltpu.CompilerParams(
            collective_id=0, has_side_effects=True, vmem_limit_bytes=62 << 20
        ),
    )(*args)


def on_device(
    latent,
    actions,
    task_ids,
    action_masks,
    next_latent,
    reward_bins,
    reward_frac,
    task_embed,
    dyn_w1,
    dyn_b1,
    dyn_gain,
    dyn_shift,
    rew_w1,
    rew_b1,
    rew_gain,
    rew_shift,
    dyn_w2,
    dyn_b2,
    rew_w2,
    rew_b2,
):
    n_mp, n_dp = lax.axis_size("mp"), lax.axis_size("dp")
    tok_rows, lat_width = latent.shape
    total_rows = tok_rows * n_dp

    def row(vector):
        return vector.reshape(1, -1)

    args = (
        latent,
        next_latent,
        dyn_w1,
        rew_w1,
        dyn_w2,
        rew_w2.T,
        *(row(v) for v in (dyn_b1, dyn_gain, dyn_shift, rew_b1, rew_gain, rew_shift)),
        row(task_ids),
        actions,
        action_masks.T,
        row(reward_bins),
        row(reward_frac),
        task_embed,
        row(dyn_b2),
        row(rew_b2),
    )
    latents, latent_grad, dyn, rew, sums = run_main(n_mp, n_dp, total_rows, args)
    n_bins = rew_b2.shape[0]
    n_in = dyn_w1.shape[0]
    outs = run_finish(
        total_rows, lat_width, n_in, n_bins, latents, latent_grad, dyn, rew, sums, task_embed
    )
    outs = [out.reshape(-1) if out.shape[0] == 1 else out for out in outs]
    outs[14] = outs[14].T
    return tuple(outs)


def solution(mesh):
    return jax.shard_map(
        on_device,
        mesh=mesh,
        in_specs=(
            P("dp", None),
            P(None, "dp"),
            P("dp"),
            P(),
            P("dp", "mp"),
            P("dp"),
            P("dp"),
            P(),
            P(None, "mp"),
            P("mp"),
            P("mp"),
            P("mp"),
            P(None, "mp"),
            P("mp"),
            P("mp"),
            P("mp"),
            P("mp", None),
            P(),
            P("mp", None),
            P(),
        ),
        out_specs=(
            P("dp", "mp"),
            P("dp", "mp"),
            P(),
            P(),
            P(None, "mp"),
            P("mp"),
            P("mp"),
            P("mp"),
            P(None, "mp"),
            P("mp"),
            P("mp"),
            P("mp"),
            P("mp", None),
            P(),
            P("mp", None),
            P(),
        ),
        check_vma=False,
    )
```

```python
import functools

import jax
import jax.numpy as jnp
from jax import lax
from jax.experimental import pallas as pl
from jax.experimental.pallas import tpu as pltpu
from jax.sharding import PartitionSpec as P

GROUP = 8
CONS_COEF = 20.0
REW_COEF = 0.1
EPS = 1e-05
LANES = 128
TILE = 512
SUB = 128
PART = 64
LATE = 2
PIECES = 2
DYN_KINDS = (0, 1, 0)
REW_KINDS = (0, 1, 0)
EVENTS = ((-1, 4, 9, 13, 99), (0, 6, 10, 14, 99), (0, 7, 11, 99, 99))
MESH = pl.DeviceIdType.MESH
F32 = jnp.float32
BF16 = jnp.bfloat16


def dot(left, right, left_dim=1, right_dim=0):
    return lax.dot_general(
        left, right, (((left_dim,), (right_dim,)), ((), ())), preferred_element_type=F32
    )


def aligned(start, size):
    return pl.ds(pl.multiple_of(start, size), size)


def aligned_to(start, size):
    return pl.ds(pl.multiple_of(start, 16), size)


def column_groups(n_bits):
    groups = [group for group in ((0,), (1, 2)) if group[-1] < n_bits]
    return groups + [(bit,) for bit in range(sum(map(len, groups)), n_bits)]


def flips(group):
    return range(1, 1 << len(group))


def mask_of(group, flip):
    return sum(1 << bit for at, bit in enumerate(group) if flip >> at & 1)


def group_masks(group):
    return [mask_of(group, flip) for flip in flips(group)] + [1 << bit for bit in group]


def room(n_rows, n_bits):
    extra, length = 2 * n_rows, n_rows
    for group in column_groups(n_bits):
        if length % (16 << len(group)) == 0:
            length >>= len(group)
            extra += length * ((1 << len(group)) - 1)
        else:
            for _ in group:
                length = length // 2 if length % 32 == 0 else length
                extra += length
    return extra


def split_dot(left, right, left_dim, right_dim):
    high = left.astype(BF16)
    low = (left - high.astype(F32)).astype(BF16)
    return dot(high, right, left_dim, right_dim) + dot(low, right, left_dim, right_dim)


def main_kernel(
    sizes,
    latent_in,
    next_in,
    dyn_w1,
    rew_w1,
    dyn_w2,
    rew_w2,
    dyn_b1,
    dyn_gain,
    dyn_shift,
    rew_b1,
    rew_gain,
    rew_shift,
    ids_ref,
    act_ref,
    masks_ref,
    bins_ref,
    frac_ref,
    embed_ref,
    dyn_b2,
    rew_b2,
    lat_out,
    grad_out,
    fin_dyn,
    fin_rew,
    fin_sums,
    x_all,
    x_t,
    w1_raw,
    w1_c,
    w2_t,
    rw2_t,
    w2_g,
    rw2_g,
    vecs,
    w2_own,
    rw2_own,
    vecs_own,
    embed_wide,
    extra_rows,
    b2_ref,
    rb2_ref,
    next_lat,
    dpl,
    dpl_send,
    lat_stage,
    lg_stage,
    d_dyn,
    part_a,
    part_b,
    part_c,
    part_rew,
    got_a,
    got_b,
    got_c,
    got_rew,
    sums,
    got_sums,
    g1,
    g2t,
    rg2t,
    pre,
    dh,
    dm,
    hid,
    d_pre,
    zt,
    next_t,
    dlog,
    inv_ref,
    col_acc,
    sum_acc,
    row_acc,
    b2_acc,
    load_sem,
    w_send,
    w_recv,
    n_send,
    n_recv,
    d_send,
    d_recv,
    l_local,
    l_send,
    l_recv,
    g_local,
    g_send,
    g_recv,
    r_send,
    r_recv,
    s_send,
    s_recv,
):
    n_mp, n_dp, total_rows, hid_width = sizes
    n_bits = n_dp.bit_length() - 1
    mine = lax.axis_index("mp")
    column = lax.axis_index("dp")
    pair = mine // 2
    half = mine % 2
    own_rows = x_all.shape[0] // 2
    lat_width = latent_in.shape[1]
    shard = dyn_w1.shape[1]
    n_act = act_ref.shape[0]
    in_rows = g1.shape[0]
    share = next_in.shape[1]
    n_task = embed_ref.shape[0]
    chip_cols = 2 * share
    n_tiles = own_rows // TILE
    n_lane = hid_width // LANES

    def peer_of(flip):
        near = mine + 1 - 2 * half
        if flip == 1:
            return near
        across = 2 * (1 - pair)
        return across + half if flip == 2 else across + 1 - half

    def bit_of(bit):
        return (column // (1 << bit)) % 2

    def column_peer(mask):
        peer = column
        for bit in range(n_bits):
            if mask >> bit & 1:
                peer = peer + (1 - 2 * bit_of(bit)) * (1 << bit)
        return peer

    groups = column_groups(n_bits)

    def place_in(group, flip):
        place = 0
        for at, bit in enumerate(group):
            here = 1 - bit_of(bit) if flip >> at & 1 else bit_of(bit)
            place = place + here * (1 << (len(group) - 1 - at))
        return place

    def rows_of(device):
        return aligned(device * own_rows, own_rows)

    barrier = pltpu.get_barrier_semaphore()
    for flip in (1, 2, 3):
        pl.semaphore_signal(
            barrier, inc=1, device_id={"mp": peer_of(flip)}, device_id_type=MESH
        )
    aslant = {"mp": peer_of(2), "dp": column_peer(1)}
    pl.semaphore_signal(barrier, inc=1, device_id=aslant, device_id_type=MESH)
    masks = sorted({mask for group in groups for mask in group_masks(group)})
    for mask in masks:
        pl.semaphore_signal(
            barrier, inc=1, device_id={"dp": column_peer(mask)}, device_id_type=MESH
        )

    vecs_own[...] = jnp.zeros_like(vecs_own)
    for net, rows in enumerate(((dyn_b1, dyn_gain, dyn_shift), (rew_b1, rew_gain, rew_shift))):
        for line, ref in enumerate(rows):
            vecs_own[net, pl.ds(line, 1), :] = ref[...]
    w2_own[...] = dyn_w2[...].T
    n_bins = rew_w2.shape[0]
    rw2_own[...] = jnp.zeros_like(rw2_own)
    rw2_own[pl.ds(0, n_bins), :] = rew_w2[...]

    near, across = peer_of(1), peer_of(2)

    def w_pairs(block, rows_first):
        pairs = []
        for net in range(2):
            cols = aligned(net * hid_width + block * shard, shard)
            pairs.append(((dyn_w1, rew_w1)[net], w1_raw.at[:, cols]))
            pairs.append((vecs_own.at[net], vecs.at[:, cols]))
        cols = aligned(block * shard, shard)
        for side in (rows_first, 1 - rows_first):
            rows = aligned(side * chip_cols, chip_cols)
            pairs.append((w2_own.at[rows, :], w2_t.at[rows, cols]))
        pairs.append((rw2_own, rw2_t.at[:, cols]))
        return pairs

    w_needs = ((1, 0, 4, 5), (3, 2, 6))
    n_weights = 7

    def weight_copy(index, kind):
        source, target = w_pairs(mine, 1 - pair if kind == 1 else pair)[index]
        if kind == 2:
            source = target = w_pairs(across, pair)[index][1]
        return pltpu.make_async_remote_copy(
            src_ref=source,
            dst_ref=target,
            send_sem=w_send.at[kind, index],
            recv_sem=w_recv.at[kind, index],
            device_id={"mp": across if kind == 1 else near},
            device_id_type=MESH,
        )

    def next_copy(slot):
        rows = near if slot == 1 else peer_of(3)
        return pltpu.make_async_remote_copy(
            src_ref=next_in.at[rows_of(rows), :],
            dst_ref=next_lat.at[slot, half],
            send_sem=n_send.at[slot],
            recv_sem=n_recv.at[slot],
            device_id={"mp": near},
            device_id_type=MESH,
        )

    loads = []
    for slot, device in ((0, across), (1, mine)):
        loads.append(
            (
                latent_in.at[rows_of(device), :],
                x_all.at[pl.ds(slot * own_rows, own_rows), pl.ds(0, lat_width)],
            )
        )
    for slot, device in ((0, across), (1, mine)):
        loads.append((next_in.at[rows_of(device), :], next_lat.at[slot, half]))
    loads += w_pairs(mine, pair)
    loads = [
        pltpu.make_async_copy(source, target, load_sem.at[i])
        for i, (source, target) in enumerate(loads)
    ]
    for copy in loads:
        copy.start()
    pl.semaphore_wait(barrier, 4 + len(masks))
    next_copy(0).start()
    next_copy(1).start()
    for index in w_needs[0] + w_needs[1]:
        weight_copy(index, 1).start()
        weight_copy(index, 0).start()

    for ref in (g1, g2t, rg2t, col_acc, sum_acc, row_acc, b2_acc):
        ref[...] = jnp.zeros_like(ref)

    line = lax.broadcasted_iota(jnp.int32, extra_rows.shape, 0)
    extra_rows[...] = jnp.where((line == n_act) | (line == n_act + 1), 1.0, 0.0)
    n_embed = embed_ref.shape[1]
    n_rest = n_act + n_embed
    moved = lax.broadcasted_iota(jnp.int32, (n_embed, n_rest), 1) == (
        lax.broadcasted_iota(jnp.int32, (n_embed, n_rest), 0) + n_act
    )
    embed_wide[...] = dot(embed_ref[...], jnp.where(moved, 1.0, 0.0).astype(BF16)).astype(BF16)
    b2_ref[...] = jnp.broadcast_to(dyn_b2[...], (LANES, lat_width)).T
    rb2_ref[...] = jnp.full(rb2_ref.shape, -1e30, F32)
    rb2_ref[:, pl.ds(0, n_bins)] = jnp.broadcast_to(rew_b2[...], (LANES, n_bins))
    rb2_ref[...] = rb2_ref[...].T

    for slot, device in ((0, across), (1, mine)):
        base = device * own_rows

        @pl.loop(0, n_tiles)
        def _(tile):
            lanes = aligned(base + tile * TILE, TILE)
            ids = ids_ref[:, lanes]
            tasks = lax.broadcasted_iota(jnp.int32, (n_task, TILE), 0)
            onehot = jnp.where(tasks == ids, 1.0, 0.0).astype(BF16)
            masks = dot(masks_ref[...].astype(F32).astype(BF16), onehot)
            extra_rows[pl.ds(0, n_act), :] = act_ref[:, lanes].astype(F32) * masks
            masked = extra_rows[...].astype(BF16)
            rest = LANES - n_task - masked.shape[0]
            extra = jnp.concatenate([onehot, masked, jnp.zeros((rest, TILE), BF16)], axis=0)
            rows = aligned(slot * own_rows + tile * TILE, TILE)
            x_all[rows, pl.ds(lat_width, LANES)] = extra.T
            if slot == 1:
                x_t[pl.ds(lat_width, LANES), aligned(tile * TILE, TILE)] = extra

    for copy in loads[:2]:
        copy.wait()

    @pl.loop(0, n_tiles)
    def _(tile):
        rows = aligned(own_rows + tile * TILE, TILE)
        x_t[pl.ds(0, lat_width), aligned(tile * TILE, TILE)] = x_all[
            rows, pl.ds(0, lat_width)
        ].T

    def centre(values):
        return values - jnp.sum(values, axis=1, keepdims=True) * (1.0 / hid_width)

    def gathered(indices):
        for index in indices:
            weight_copy(index, 1).wait_recv()
            weight_copy(index, 2).start()
        for index in indices:
            loads[4 + index].wait()
            weight_copy(index, 0).wait_recv()
            weight_copy(index, 2).wait_recv()

    def with_gain(weights, scaled, net):
        gain = vecs[pl.ds(1, 1), pl.ds(net * hid_width, hid_width)]

        @pl.loop(0, weights.shape[0] // PART)
        def _(step):
            rows = aligned(step * PART, PART)
            scaled[rows, :] = (weights[rows, :].astype(F32) * gain).astype(BF16)

    def prepare(net):
        gathered(w_needs[net][:2])
        cols = pl.ds(net * hid_width, hid_width)

        @pl.loop(0, lat_width // PART)
        def _(step):
            rows = aligned(step * PART, PART)
            w1_c[rows, cols] = centre(w1_raw[rows, cols].astype(F32)).astype(BF16)

        table = dot(embed_wide[...], w1_raw[pl.ds(lat_width, n_rest), cols])
        w1_c[pl.ds(lat_width, n_task), cols] = centre(table).astype(BF16)
        act = centre(w1_raw[pl.ds(lat_width, 16), cols].astype(F32))
        bias = centre(vecs[pl.ds(0, 1), cols])
        high = bias.astype(BF16).astype(F32)
        row = lax.broadcasted_iota(jnp.int32, act.shape, 0)
        act = jnp.where(row < n_act, act, 0.0)
        act = jnp.where(row == n_act, high, jnp.where(row == n_act + 1, bias - high, act))
        w1_c[pl.ds(lat_width + n_task, 16), cols] = act.astype(BF16)
        rest = LANES - n_task - 16
        w1_c[pl.ds(lat_width + n_task + 16, rest), cols] = jnp.zeros((rest, hid_width), BF16)

    def forward(net, rows, keep):
        cols = pl.ds(net * hid_width, hid_width)
        values = dot(x_all[rows, :], w1_c[:, cols])
        pre[...] = values
        square = jnp.sum(values * values, axis=1, keepdims=True)
        inv_ref[...] = jnp.broadcast_to(
            lax.rsqrt(square * (1.0 / hid_width) + EPS), (TILE, LANES)
        )

        @pl.loop(0, TILE // SUB)
        def _(step):
            part = aligned(step * SUB, SUB)
            inv = inv_ref[part, :]
            for lane in range(n_lane):
                lanes = pl.ds(lane * LANES, LANES)
                wide = pl.ds(net * hid_width + lane * LANES, LANES)
                xhat = pre[part, lanes] * inv
                y = xhat * vecs[pl.ds(1, 1), wide] + vecs[pl.ds(2, 1), wide]
                if keep:
                    pre[part, lanes] = xhat
                y = y.astype(BF16)
                e = jnp.exp(jnp.minimum(y, 20.0))
                e2 = e + 2.0
                r = 1.0 / (e * e2 + 2.0)
                u = e * r
                t = u * e2
                hid[part, lanes] = y * t
                if keep:
                    dm[part, lanes] = t + (4.0 * y) * (u * (r + u))

    def backward(net, target, first_row):
        @pl.loop(0, TILE // SUB)
        def _(step):
            part = aligned(step * SUB, SUB)
            first = jnp.zeros((SUB, LANES), F32)
            second = jnp.zeros((SUB, LANES), F32)
            for lane in range(n_lane):
                lanes = pl.ds(lane * LANES, LANES)
                wide = pl.ds(net * hid_width + lane * LANES, LANES)
                g = dh[part, lanes] * dm[part, lanes].astype(F32)
                scaled = g * pre[part, lanes]
                col_acc[pl.ds(0, 8), wide] += jnp.sum(
                    scaled.reshape(SUB // 8, 8, LANES), axis=0
                )
                col_acc[pl.ds(8, 8), wide] += jnp.sum(g.reshape(SUB // 8, 8, LANES), axis=0)
                first += g
                second += scaled
                dh[part, lanes] = g
            inv = inv_ref[part, :]
            first = jnp.broadcast_to(
                jnp.sum(first, axis=1, keepdims=True) * (1.0 / hid_width), (SUB, LANES)
            )
            second = jnp.broadcast_to(
                jnp.sum(second, axis=1, keepdims=True) * (1.0 / hid_width), (SUB, LANES)
            )
            first = first * inv
            second = second * inv
            for lane in range(n_lane):
                lanes = pl.ds(lane * LANES, LANES)
                value = dh[part, lanes] * inv - first - pre[part, lanes] * second
                target[aligned(first_row + step * SUB, SUB), lanes] = value.astype(BF16)

    d_scale = 2.0 * CONS_COEF / total_rows

    def simnorm(slot, tile, target, row, col):
        rows = aligned(tile * TILE, TILE)
        zt[...] = dot(w2_t[aligned(pair * chip_cols, chip_cols), :], hid[...], 1, 1)
        @pl.loop(0, chip_cols // PART)
        def _(step):
            part = aligned(step * PART, PART)
            bias = b2_ref[aligned(pair * chip_cols + step * PART, PART), :]
            for lane in range(TILE // LANES):
                lanes = pl.ds(lane * LANES, LANES)
                z = (zt[part, lanes] + bias).reshape(PART // GROUP, GROUP, LANES)
                e = jnp.exp(z - jnp.max(z, axis=1, keepdims=True))
                s = e * (1.0 / jnp.sum(e, axis=1, keepdims=True))
                wanted = next_t[slot, part, aligned(tile * TILE + lane * LANES, LANES)]
                error = s - wanted.astype(F32).reshape(z.shape)
                sum_acc[pl.ds(0, 8), :] += jnp.sum(error * error, axis=0)
                d_lat = d_scale * error
                d_z = s * (d_lat - jnp.sum(s * d_lat, axis=1, keepdims=True))
                zt[part, lanes] = s.reshape(PART, LANES)
                b2_acc[part, :] += d_z.reshape(PART, LANES)
                target[
                    aligned(row + step * PART, PART), aligned(col + lane * LANES, LANES)
                ] = d_z.reshape(PART, LANES).astype(BF16)

        for side in range(2):
            lat_stage[slot, side, rows, :] = zt[pl.ds(side * share, share), :].astype(BF16).T

    def lat_copies(slot, tile):
        device = across if slot == 0 else mine
        rows = aligned(tile * TILE, TILE)
        out_rows = lat_out.at[aligned(device * own_rows + tile * TILE, TILE), :]
        index = slot * n_tiles + tile
        local = pltpu.make_async_copy(
            lat_stage.at[slot, half, rows, :], out_rows, l_local.at[index]
        )
        remote = pltpu.make_async_remote_copy(
            src_ref=lat_stage.at[slot, 1 - half, rows, :],
            dst_ref=out_rows,
            send_sem=l_send.at[index],
            recv_sem=l_recv.at[index],
            device_id={"mp": near},
            device_id_type=MESH,
        )
        return local, remote

    def dpl_copy(tile):
        cols = aligned(tile * TILE, TILE)
        return pltpu.make_async_remote_copy(
            src_ref=dpl_send.at[:, cols],
            dst_ref=dpl.at[aligned(pair * chip_cols, chip_cols), cols],
            send_sem=d_send.at[tile],
            recv_sem=d_recv.at[tile],
            device_id={"mp": across},
            device_id_type=MESH,
        )

    def grad_copies(tile):
        rows = aligned(tile * TILE, TILE)
        out_rows = grad_out.at[aligned(mine * own_rows + tile * TILE, TILE), :]
        remotes = []
        for flip in (2, 3, 1):
            peer = peer_of(flip)
            remotes.append(
                pltpu.make_async_remote_copy(
                    src_ref=lg_stage.at[peer, rows, :],
                    dst_ref=out_rows,
                    send_sem=g_send.at[flip - 1, tile],
                    recv_sem=g_recv.at[flip - 1, tile],
                    device_id={"mp": peer},
                    device_id_type=MESH,
                )
            )
        local = pltpu.make_async_copy(lg_stage.at[mine, rows, :], out_rows, g_local.at[tile])
        return local, remotes

    for slot in range(2):
        loads[2 + slot].wait()
        next_copy(slot).wait_recv()

        @pl.loop(0, n_tiles)
        def _(tile):
            rows = aligned(tile * TILE, TILE)
            for side in range(2):
                next_t[slot, pl.ds(side * share, share), rows] = next_lat[slot, side, rows, :].T

    prepare(0)

    @pl.loop(0, n_tiles)
    def _(tile):
        forward(0, aligned(tile * TILE, TILE), False)

        @pl.when(tile == 0)
        def _():
            gathered(w_needs[0][2:3])

        simnorm(0, tile, dpl_send, 0, tile * TILE)
        dpl_copy(tile).start()
        local, remote = lat_copies(0, tile)
        local.start()
        remote.start()

    def add_into(target, others, n_rows):
        step_rows = next(size for size in (128, 96, 80, 64, 48, 32, 16) if n_rows % size == 0)

        @pl.loop(0, n_rows // step_rows)
        def _(step):
            rows = aligned(step * step_rows, step_rows)
            total = target[rows, :].astype(F32)
            for other in others:
                total = total + other[rows, :].astype(F32)
            target[rows, :] = total.astype(BF16)

    def reduction(key, part, got, fin, order, with_sums):
        n_rows = part.shape[2]
        stages, gathers = [], []
        offset, length, spot, both = 0, n_rows, n_rows, True

        def sides(rows, where, other_side):
            if both:
                return part.at[half, :, rows, :], got.at[:, where, :]
            return part.at[half, other_side, rows, :], got.at[0, where, :]

        def adds(rows, wheres, count):
            if both:
                return [
                    (part.at[half, k, rows, :], [got.at[k, where, :] for where in wheres], count)
                    for k in range(2)
                ]
            return [(part.at[half, pair, rows, :], [got.at[0, w, :] for w in wheres], count)]

        for what in order:
            if what == "near":
                where = pl.ds(0, n_rows)
                copies = [(part.at[1 - half], got.at[:, where, :], {"mp": near})]
                stages.append((copies, adds(pl.ds(0, n_rows), [where], n_rows), None, half))
                continue
            if what == "across":
                both = False
                rows, where = aligned_to(offset, length), pl.ds(spot, length)
                source, target = sides(rows, where, 1 - pair)
                copies = [(source, target, {"mp": across})]
                stages.append((copies, adds(rows, [where], length), None, pair))
                spot += length
                continue
            if what == "cross":
                both = False
                length //= 2
                keep_at = offset + place_in(groups[0], 0) * length
                other_at = offset + place_in(groups[0], 1) * length
                copies, wheres = [], []
                for side, at, device in (
                    (1 - pair, other_at, aslant),
                    (1 - pair, keep_at, {"mp": across}),
                    (pair, other_at, {"dp": column_peer(1)}),
                ):
                    where = pl.ds(spot, length)
                    spot += length
                    source, target = sides(aligned_to(at, length), where, side)
                    copies.append((source, target, device))
                    wheres.append(where)
                keep = aligned_to(keep_at, length)
                here = 2 * pair + place_in(groups[0], 0)
                stages.append((copies, adds(keep, wheres, length), None, here))
                gathers.append((groups[0], keep_at, length))
                offset = keep_at
                continue
            if length % (16 << len(what)) == 0:
                parts = [what]
            else:
                parts = [(bit,) for bit in what]
            for group in parts:
                whole = length % (16 << len(group)) != 0
                if not whole:
                    length >>= len(group)
                mine_at = 0 if whole else place_in(group, 0) * length
                copies, wheres = [], []
                for flip in flips(group):
                    at = 0 if whole else place_in(group, flip) * length
                    where = pl.ds(spot, length)
                    spot += length
                    source, target = sides(aligned_to(offset + at, length), where, pair)
                    copies.append((source, target, {"dp": column_peer(mask_of(group, flip))}))
                    wheres.append(where)
                keep = aligned_to(offset + mine_at, length)
                kind = "whole" if whole else None
                stages.append((copies, adds(keep, wheres, length), kind, place_in(group, 0)))
                if not whole:
                    gathers.append((group, offset + mine_at, length))
                offset = offset + mine_at
        last = len(stages)
        final = aligned_to(offset, length)
        for group, start, count in gathers[::-1]:
            rows = aligned_to(start, count)
            copies = [
                (fin.at[rows, :], fin.at[rows, :], {"dp": column_peer(mask_of(group, flip))})
                for flip in flips(group)
            ]
            stages.append((copies, [], None, None))
        firsts = [sum(len(stage[0]) for stage in stages[:i]) for i in range(len(stages))]
        slots = [sum(len(stage[0]) + 1 for stage in stages[:i]) for i in range(last)]

        def copies_of(index):
            for number, (source, target, device) in enumerate(stages[index][0]):
                at = firsts[index] + number
                yield pltpu.make_async_remote_copy(
                    src_ref=source,
                    dst_ref=target,
                    send_sem=r_send.at[key, at],
                    recv_sem=r_recv.at[key, at],
                    device_id=device,
                    device_id_type=MESH,
                )

        def sums_copies(index):
            if with_sums and index < last:
                for number, (_, _, device) in enumerate(stages[index][0]):
                    at = firsts[index] + number
                    yield pltpu.make_async_remote_copy(
                        src_ref=sums.at[index],
                        dst_ref=got_sums.at[slots[index] + stages[index][3]],
                        send_sem=s_send.at[at],
                        recv_sem=s_recv.at[at],
                        device_id=device,
                        device_id_type=MESH,
                    )

        def start(index):
            for copy in copies_of(index):
                copy.start()
            for copy in sums_copies(index):
                copy.start()

        def finish(index):
            for copy in copies_of(index):
                if stages[index][2] == "whole":
                    copy.wait_send()
                copy.wait_recv()
            for copy in sums_copies(index):
                copy.wait_recv()
            if with_sums and index < last:
                got_sums[slots[index] + stages[index][3]] = sums[index]
                total = got_sums[slots[index]]
                for other in range(len(stages[index][0])):
                    total = total + got_sums[slots[index] + 1 + other]
                sums[index + 1] = total
            for target, others, count in stages[index][1]:
                add_into(target, others, count)
            if index + 1 == last:
                fin[final, :] = part[half, pair, final, :]
            if index + 1 < len(stages):
                start(index + 1)

        def drain():
            for index, stage in enumerate(stages):
                if stage[2] != "whole":
                    for copy in copies_of(index):
                        copy.wait_send()
                for copy in sums_copies(index):
                    copy.wait_send()

        return start, finish, drain, len(stages), last

    def fill(part, net, first, count, source, base):
        for device in range(n_mp):
            cols = pl.ds(net * hid_width + device * shard, shard)
            part[device % 2, device // 2, pl.ds(first, count), :] = source[
                pl.ds(base, count), cols
            ].astype(BF16)

    def add_columns(net):
        cols = pl.ds(net * hid_width, hid_width)
        for line in range(2):
            total = jnp.sum(col_acc[pl.ds(8 * line, 8), cols], axis=0, keepdims=True)
            g1[pl.ds(lat_width + n_task + 8 + line, 1), cols] = total / vecs[pl.ds(1, 1), cols]

    def order_of(kind):
        if kind == 0 or len(groups) < 2:
            return ["near", "cross"] + groups[1:]
        if kind == 1:
            return ["near", groups[1], "cross"] + groups[2:]
        if kind == 2:
            return ["near"] + groups[:1] + ["across"] + groups[1:]
        return ["near", "across"] + groups

    split = part_b.shape[2]
    dyn_places = (
        (part_a, got_a, in_rows, lat_width),
        (part_b, got_b, 0, split),
        (part_c, got_c, split, in_rows - split),
    )
    chunks = [
        reduction(k, part, got, fin_dyn.at[pl.ds(first, count), :], order_of(DYN_KINDS[k]), False)
        for k, (part, got, first, count) in enumerate(dyn_places)
    ]
    gathered(w_needs[0][3:])
    with_gain(w2_t, w2_g, 0)

    @pl.loop(0, n_tiles)
    def _(tile):
        cols = aligned(tile * TILE, TILE)
        forward(0, aligned(own_rows + tile * TILE, TILE), True)
        simnorm(1, tile, dpl, pair * chip_cols, tile * TILE)
        local, remote = lat_copies(1, tile)
        local.start()
        remote.start()
        dpl_copy(tile).wait_recv()
        d_lat = dpl[:, cols]
        g2t[...] += dot(d_lat, hid[...])

        @pl.when(tile == n_tiles - 1)
        def _():
            fill(part_a, 0, 0, lat_width, g2t, 0)
            chunks[0][0](0)

        dh[...] = dot(d_lat, w2_g[...], 0, 0)
        backward(0, d_dyn, tile * TILE)
        g1[:, pl.ds(0, hid_width)] += dot(x_t[:, cols], d_dyn[cols, :])

    fill(part_b, 0, 0, split, g1, 0)
    chunks[1][0](0)
    add_columns(0)
    fill(part_c, 0, 0, in_rows - split, g1, split)
    chunks[2][0](0)
    per_tile = 4
    inside = sorted(
        (place, chunk, index)
        for chunk, places in enumerate(EVENTS)
        for index, place in enumerate(places)
        if index < chunks[chunk][3] and place < per_tile * n_tiles
    )

    prepare(1)
    gathered(w_needs[1][2:])
    with_gain(rw2_t, rw2_g, 1)

    for place, chunk, index in inside:
        if place < 0:
            chunks[chunk][1](index)

    def point(tile, number):
        for place, chunk, index in inside:
            if place >= 0 and place % per_tile == number:

                @pl.when(tile == place // per_tile)
                def _():
                    chunks[chunk][1](index)

    def kept(tile):
        return aligned(jnp.maximum(tile - (n_tiles - LATE - 1), 0) * TILE, TILE)

    def latent_grads(tile):
        cols = aligned(tile * TILE, TILE)
        lat_rows = pl.ds(0, lat_width)
        lg = dot(d_dyn[cols, :], w1_raw[lat_rows, pl.ds(0, hid_width)], 1, 1)
        lg = lg + dot(d_pre[kept(tile), :], w1_raw[lat_rows, pl.ds(hid_width, hid_width)], 1, 1)
        lg = (lg * total_rows).astype(BF16)
        for device in range(n_mp):
            lg_stage[device, cols, :] = lg[:, device * share : (device + 1) * share]

    def send_grads(tile):
        local, remotes = grad_copies(tile)
        local.start()
        for remote in remotes:
            remote.start()

    @pl.loop(0, n_tiles)
    def _(tile):
        cols = aligned(tile * TILE, TILE)
        forward(1, aligned(own_rows + tile * TILE, TILE), True)
        point(tile, 0)
        bins = bins_ref[:, aligned(mine * own_rows + tile * TILE, TILE)]
        frac = frac_ref[:, aligned(mine * own_rows + tile * TILE, TILE)]
        z = dot(rw2_t[...], hid[...], 1, 1)
        bias = rb2_ref[...]
        z = z + jnp.concatenate([bias] * (TILE // LANES), axis=1)
        z = z - jnp.max(z, axis=0, keepdims=True)
        e = jnp.exp(z)
        total = jnp.sum(e, axis=0, keepdims=True)
        row = lax.broadcasted_iota(jnp.int32, z.shape, 0)
        target = jnp.where(row == bins, 1.0 - frac, 0.0) + jnp.where(row == bins + 1, frac, 0.0)
        loss = jnp.sum(target * (jnp.log(total) - z), axis=0, keepdims=True)
        row_acc[...] += loss
        d_logits = (REW_COEF / total_rows) * (e * (1.0 / total) - target)
        dlog[...] = d_logits.astype(BF16)
        sum_acc[pl.ds(8, 8), :] += dot(jnp.ones((8, TILE), BF16), dlog[...], 1, 1)
        rg2t[...] += dot(dlog[...], hid[...])
        dh[...] = dot(dlog[...], rw2_g[...], 0, 0)
        point(tile, 1)
        backward(1, d_pre, jnp.maximum(tile - (n_tiles - LATE - 1), 0) * TILE)
        point(tile, 2)
        g1[:, pl.ds(hid_width, hid_width)] += dot(x_t[:, cols], d_pre[kept(tile), :])

        if LATE < n_tiles:

            @pl.when(tile < n_tiles - LATE)
            def _():
                latent_grads(tile)

        point(tile, 3)

        if LATE < n_tiles:

            @pl.when(tile < n_tiles - LATE)
            def _():
                send_grads(tile)


    add_columns(1)
    third = part_rew.shape[3]
    spare = in_rows - 2 * third - 32
    for k in range(3):
        chunks.append(
            reduction(
                3 + k,
                part_rew.at[k],
                got_rew.at[k],
                fin_rew.at[pl.ds(k * third, third), :],
                order_of(REW_KINDS[k]),
                k == 2,
            )
        )
    for k in range(3):
        rest = min(third, in_rows - k * third)
        for device in range(n_mp):
            cols = pl.ds(hid_width + device * shard, shard)
            where = (k, device % 2, device // 2)
            part_rew[where + (pl.ds(0, rest),)] = g1[pl.ds(k * third, rest), cols].astype(BF16)
            if rest < third:
                block = pl.ds(device * shard, shard)
                part_rew[where + (pl.ds(rest, LANES),)] = rg2t[:, block].astype(BF16)
        if k < 2:
            chunks[3 + k][0](0)
    tasks = g1[pl.ds(lat_width, n_task), :]
    table = split_dot(tasks, w1_raw[pl.ds(lat_width, n_rest), :], 1, 1).astype(BF16)
    for device in range(n_mp):
        where = (2, device % 2, device // 2)
        part_rew[where + (pl.ds(spare, 32), pl.ds(0, n_rest))] = table[0:32]
        part_rew[where + (pl.ds(spare, 32), pl.ds(LANES, n_rest))] = table[32:64]
        part_rew[where + (pl.ds(third - 16, 16), pl.ds(0, n_rest))] = table[64:80]
    sums[0] = jnp.zeros(sums.shape[1:], F32)
    sums[0, pl.ds(0, 1), aligned(pair * chip_cols, chip_cols)] = jnp.sum(
        b2_acc[...].T, axis=0, keepdims=True
    )
    sums[0, pl.ds(1, 1), pl.ds(0, LANES)] = sum_acc[pl.ds(8, 1), :]
    cons = jnp.sum(sum_acc[pl.ds(0, 8), :])
    rew = jnp.sum(row_acc[...])
    sums[0, pl.ds(2, 1), :] = jnp.full((1, lat_width), cons)
    sums[0, pl.ds(3, 1), :] = jnp.full((1, lat_width), rew)
    chunks[5][0](0)
    done = [(chunk, index) for _, chunk, index in inside]
    left = [(index, c) for c in range(3) for index in range(chunks[c][3]) if (c, index) not in done]
    base = min([index for index, _ in left], default=0)
    left = [(index - base, c, index) for index, c in left]
    left += [(index, c, index) for c in range(3, 6) for index in range(chunks[c][3])]
    late = [n_tiles - LATE + k for k in range(LATE)]
    for tile in late[:1]:
        latent_grads(tile)
    step = 0
    for when, chunk, index in sorted(left):
        if when > step:
            step = when
            for tile in late[step - 1 : step]:
                send_grads(tile)
            for tile in late[step : step + 1]:
                latent_grads(tile)
        chunks[chunk][1](index)
    fin_sums[...] = sums[chunks[5][4]]
    for chunk in chunks:
        chunk[2]()

    for index in range(n_weights):
        for kind in range(3):
            weight_copy(index, kind).wait_send()
    for slot in range(2):
        next_copy(slot).wait_send()

        @pl.loop(0, n_tiles)
        def _(tile):
            local, remote = lat_copies(slot, tile)
            local.wait()
            remote.wait()

    @pl.loop(0, n_tiles)
    def _(tile):
        dpl_copy(tile).wait_send()
        local, remotes = grad_copies(tile)
        local.wait()
        for remote in remotes:
            remote.wait()


def finish_kernel(
    lat_in,
    grad_in,
    dyn_in,
    rew_in,
    sums_in,
    embed,
    lat_out,
    grad_out,
    losses,
    grad_embed,
    dyn_w1,
    dyn_b1,
    dyn_gain,
    dyn_shift,
    rew_w1,
    rew_b1,
    rew_gain,
    rew_shift,
    dyn_w2,
    dyn_b2,
    rew_w2,
    rew_b2,
    dyn,
    rew,
    sums,
    stage,
    sems,
    *,
    total_rows,
    lat_width,
):
    n_big = stage.shape[1]
    copies = [
        pltpu.make_async_copy(source, target, sems.at[i])
        for i, (source, target) in enumerate(((dyn_in, dyn), (rew_in, rew), (sums_in, sums)))
    ]
    rows = stage.shape[2]
    outs = []
    for k in range(n_big):
        part = pl.ds(k * rows, rows)
        for side, (source, target) in enumerate(((lat_in, lat_out), (grad_in, grad_out))):
            first, last = sems.at[3 + 4 * k + 2 * side], sems.at[4 + 4 * k + 2 * side]
            copies.append(
                pltpu.make_async_copy(source.at[part, :], stage.at[side, k], first)
            )
            outs.append(pltpu.make_async_copy(stage.at[side, k], target.at[part, :], last))
    for copy in copies:
        copy.start()
    for copy, out in zip(copies[3:], outs):
        copy.wait()
        out.start()
    for copy in copies[:3]:
        copy.wait()
    n_task, n_embed = embed.shape
    n_rest = dyn_w1.shape[0] - lat_width
    n_act = n_rest - n_embed
    in_rows = lat_width + LANES
    first = lat_width + n_task
    moved = lax.broadcasted_iota(jnp.int32, (n_embed, n_rest), 1) == (
        lax.broadcasted_iota(jnp.int32, (n_embed, n_rest), 0) + n_act
    )
    moved = jnp.where(moved, 1.0, 0.0).astype(BF16)
    line = lax.broadcasted_iota(jnp.int32, (LANES - n_task, n_rest), 0)
    lane = lax.broadcasted_iota(jnp.int32, (LANES - n_task, n_rest), 1)
    acts = jnp.where((line == lane) & (line < n_act), 1.0, 0.0).astype(BF16)
    mix = jnp.concatenate([dot(embed[...], moved).astype(BF16), acts], axis=0)
    for net, w1, b1, gain, shift in (
        (dyn, dyn_w1, dyn_b1, dyn_gain, dyn_shift),
        (rew, rew_w1, rew_b1, rew_gain, rew_shift),
    ):
        w1[pl.ds(0, lat_width), :] = net[pl.ds(0, lat_width), :].astype(F32)
        w1[pl.ds(lat_width, n_rest), :] = dot(mix, net[pl.ds(lat_width, LANES), :], 0, 0)
        small = net[pl.ds(first, 16), :].astype(F32)
        b1[...] = small[n_act : n_act + 1]
        gain[...] = small[8:9]
        shift[...] = small[9:10]
    dyn_w2[...] = dyn[pl.ds(in_rows, lat_width), :].astype(F32).T
    n_bins = rew_w2.shape[0]
    rew_w2[...] = rew[pl.ds(in_rows, LANES), :].astype(F32)[:n_bins]
    dyn_b2[...] = sums[pl.ds(0, 1), :]
    rew_b2[...] = sums[pl.ds(1, 1), pl.ds(0, n_bins)]
    pieces = (
        (0, 32, in_rows - 32, 0),
        (32, 32, in_rows - 32, LANES),
        (64, n_task - 64, in_rows + LANES - 16, 0),
    )
    for to, count, row, col in pieces:
        grad_embed[pl.ds(to, count), :] = dot(
            rew[pl.ds(row, count), pl.ds(col, n_rest)], moved, 1, 1
        )
    pick = lax.broadcasted_iota(jnp.int32, losses.shape, 1) == 0
    both = jnp.where(pick, sums[pl.ds(2, 1), pl.ds(0, 2)], sums[pl.ds(3, 1), pl.ds(0, 2)])
    losses[...] = both * (1.0 / total_rows)
    for out in outs:
        out.wait()


def run_finish(total_rows, lat_width, n_in, n_bins, lat, grad, dyn, rew, sums, embed):
    shape = jax.ShapeDtypeStruct
    shard = dyn.shape[1]
    line = shape((1, shard), F32)
    first = [shape((n_in, shard), F32), line, line, line]
    any_spec = pl.BlockSpec(memory_space=pl.ANY)
    vmem_spec = pl.BlockSpec(memory_space=pltpu.VMEM)
    return pl.pallas_call(
        functools.partial(finish_kernel, total_rows=total_rows, lat_width=lat_width),
        out_shape=(
            shape(lat.shape, BF16),
            shape(grad.shape, BF16),
            shape((1, 2), F32),
            shape(embed.shape, F32),
            *first,
            *first,
            shape((shard, lat_width), F32),
            shape((1, lat_width), F32),
            shape((n_bins, shard), F32),
            shape((1, n_bins), F32),
        ),
        in_specs=[any_spec] * 5 + [vmem_spec],
        out_specs=[any_spec] * 2 + [vmem_spec] * 14,
        scratch_shapes=[
            pltpu.VMEM(dyn.shape, BF16),
            pltpu.VMEM(rew.shape, BF16),
            pltpu.VMEM(sums.shape, F32),
            pltpu.VMEM((2, PIECES, lat.shape[0] // PIECES, lat.shape[1]), BF16),
            pltpu.SemaphoreType.DMA((3 + 4 * PIECES,)),
        ],
        compiler_params=pltpu.CompilerParams(vmem_limit_bytes=60 << 20),
    )(lat, grad, dyn, rew, sums, embed)


def run_main(n_mp, n_dp, total_rows, args):
    latent, next_latent, w1, dyn_w2, rew_w2 = args[0], args[1], args[2], args[4], args[5]
    tok_rows, lat_width = latent.shape
    share = next_latent.shape[1]
    n_in, shard = w1.shape
    hid_width = n_mp * shard
    own = tok_rows // n_mp
    in_rows = lat_width + LANES
    n_tiles = own // TILE
    n_task = args[17].shape[0]
    any_spec = pl.BlockSpec(memory_space=pl.ANY)
    vmem_spec = pl.BlockSpec(memory_space=pltpu.VMEM)
    shape = jax.ShapeDtypeStruct
    dma = pltpu.SemaphoreType.DMA
    n_bits = n_dp.bit_length() - 1
    n_copies = 4 + 2 * sum(len(flips(group)) for group in column_groups(n_bits))
    third = (in_rows + LANES) // 3
    split = 3 * in_rows // 5
    return pl.pallas_call(
        functools.partial(main_kernel, (n_mp, n_dp, total_rows, hid_width)),
        out_shape=(
            shape((tok_rows, share), BF16),
            shape((tok_rows, share), BF16),
            shape((in_rows + lat_width, shard), BF16),
            shape((3 * third, shard), BF16),
            shape((8, lat_width), F32),
        ),
        in_specs=[any_spec] * 4 + [vmem_spec] * 16,
        out_specs=[any_spec] * 2 + [vmem_spec] * 3,
        scratch_shapes=[
            pltpu.VMEM((2 * own, in_rows), BF16),
            pltpu.VMEM((in_rows, own), BF16),
            pltpu.VMEM((n_in, 2 * hid_width), BF16),
            pltpu.VMEM((in_rows, 2 * hid_width), BF16),
            pltpu.VMEM((lat_width, hid_width), BF16),
            pltpu.VMEM((LANES, hid_width), BF16),
            pltpu.VMEM((lat_width, hid_width), BF16),
            pltpu.VMEM((LANES, hid_width), BF16),
            pltpu.VMEM((8, 2 * hid_width), F32),
            pltpu.VMEM((lat_width, shard), BF16),
            pltpu.VMEM((LANES, shard), BF16),
            pltpu.VMEM((2, 8, shard), F32),
            pltpu.VMEM((n_task, n_in - lat_width), BF16),
            pltpu.VMEM((16, TILE), F32),
            pltpu.VMEM((lat_width, LANES), F32),
            pltpu.VMEM((LANES, LANES), F32),
            pltpu.VMEM((2, 2, own, share), BF16),
            pltpu.VMEM((lat_width, own), BF16),
            pltpu.VMEM((2 * share, own), BF16),
            pltpu.VMEM((2, 2, own, share), BF16),
            pltpu.VMEM((n_mp, own, share), BF16),
            pltpu.VMEM((own, hid_width), BF16),
            pltpu.VMEM((2, 2, lat_width, shard), BF16),
            pltpu.VMEM((2, 2, split, shard), BF16),
            pltpu.VMEM((2, 2, in_rows - split, shard), BF16),
            pltpu.VMEM((3, 2, 2, third, shard), BF16),
            pltpu.VMEM((2, room(lat_width, n_bits), shard), BF16),
            pltpu.VMEM((2, room(split, n_bits), shard), BF16),
            pltpu.VMEM((2, room(in_rows - split, n_bits), shard), BF16),
            pltpu.VMEM((3, 2, room(third, n_bits), shard), BF16),
            pltpu.VMEM((3 + n_bits, 8, lat_width), F32),
            pltpu.VMEM((4 + 2 * n_bits, 8, lat_width), F32),
            pltpu.VMEM((in_rows, 2 * hid_width), F32),
            pltpu.VMEM((lat_width, hid_width), F32),
            pltpu.VMEM((LANES, hid_width), F32),
            pltpu.VMEM((TILE, hid_width), F32),
            pltpu.VMEM((TILE, hid_width), F32),
            pltpu.VMEM((TILE, hid_width), BF16),
            pltpu.VMEM((TILE, hid_width), BF16),
            pltpu.VMEM(((LATE + 1) * TILE, hid_width), BF16),
            pltpu.VMEM((2 * share, TILE), F32),
            pltpu.VMEM((2, 2 * share, own), BF16),
            pltpu.VMEM((LANES, TILE), BF16),
            pltpu.VMEM((TILE, LANES), F32),
            pltpu.VMEM((16, 2 * hid_width), F32),
            pltpu.VMEM((16, LANES), F32),
            pltpu.VMEM((1, TILE), F32),
            pltpu.VMEM((2 * share, LANES), F32),
            dma((11,)),
            dma((3, 7)),
            dma((3, 7)),
            dma((2,)),
            dma((2,)),
            dma((n_tiles,)),
            dma((n_tiles,)),
            dma((2 * n_tiles,)),
            dma((2 * n_tiles,)),
            dma((2 * n_tiles,)),
            dma((n_tiles,)),
            dma((3, n_tiles)),
            dma((3, n_tiles)),
            dma((6, n_copies)),
            dma((6, n_copies)),
            dma((n_copies,)),
            dma((n_copies,)),
        ],
        compiler_params=pltpu.CompilerParams(
            collective_id=0, has_side_effects=True, vmem_limit_bytes=62 << 20
        ),
    )(*args)


def on_device(
    latent,
    actions,
    task_ids,
    action_masks,
    next_latent,
    reward_bins,
    reward_frac,
    task_embed,
    dyn_w1,
    dyn_b1,
    dyn_gain,
    dyn_shift,
    rew_w1,
    rew_b1,
    rew_gain,
    rew_shift,
    dyn_w2,
    dyn_b2,
    rew_w2,
    rew_b2,
):
    n_mp, n_dp = lax.axis_size("mp"), lax.axis_size("dp")
    tok_rows, lat_width = latent.shape
    total_rows = tok_rows * n_dp

    def row(vector):
        return vector.reshape(1, -1)

    args = (
        latent,
        next_latent,
        dyn_w1,
        rew_w1,
        dyn_w2,
        rew_w2.T,
        *(row(v) for v in (dyn_b1, dyn_gain, dyn_shift, rew_b1, rew_gain, rew_shift)),
        row(task_ids),
        actions,
        action_masks.T,
        row(reward_bins),
        row(reward_frac),
        task_embed,
        row(dyn_b2),
        row(rew_b2),
    )
    latents, latent_grad, dyn, rew, sums = run_main(n_mp, n_dp, total_rows, args)
    n_bins = rew_b2.shape[0]
    n_in = dyn_w1.shape[0]
    outs = run_finish(
        total_rows, lat_width, n_in, n_bins, latents, latent_grad, dyn, rew, sums, task_embed
    )
    outs = [out.reshape(-1) if out.shape[0] == 1 else out for out in outs]
    outs[14] = outs[14].T
    return tuple(outs)


def solution(mesh):
    return jax.shard_map(
        on_device,
        mesh=mesh,
        in_specs=(
            P("dp", None),
            P(None, "dp"),
            P("dp"),
            P(),
            P("dp", "mp"),
            P("dp"),
            P("dp"),
            P(),
            P(None, "mp"),
            P("mp"),
            P("mp"),
            P("mp"),
            P(None, "mp"),
            P("mp"),
            P("mp"),
            P("mp"),
            P("mp", None),
            P(),
            P("mp", None),
            P(),
        ),
        out_specs=(
            P("dp", "mp"),
            P("dp", "mp"),
            P(),
            P(),
            P(None, "mp"),
            P("mp"),
            P("mp"),
            P("mp"),
            P(None, "mp"),
            P("mp"),
            P("mp"),
            P("mp"),
            P("mp", None),
            P(),
            P("mp", None),
            P(),
        ),
        check_vma=False,
    )
```
